256 devices in a mesh: fsdp: 32 (over x_hi, z, core), ctx: 8 (over x_lo, y).
Axes of the slice: x: 4 (x_hi: 2, x_lo: 2; x = x_hi * 2 + x_lo), y: 4, z: 8, core: 2. Of those that a mesh axis runs over, the one named last changes fastest.
Arguments:
- hidden: bfloat16 [2048, 8192], P('ctx', 'fsdp'), may hold values from -6 to 6
- gain: bfloat16 [8192], replicated, may hold values from 0.25 to 1.75
- embed: bfloat16 [512, 8192], P(None, 'fsdp'), may hold values from -6 to 6
- qkv_weight: bfloat16 [8192, 12288], P('fsdp'), may hold values from -0.07164475 to 0.07164475
- out_weight: bfloat16 [4096, 8192], P('fsdp'), may hold values from -1 to 1
- ref_ids: int32 [2048], P('ctx'), may hold values from 0 to 511
- var_pos: int32 [128], P('ctx'), may hold values from 0 to 2047, as said below
- var_base: int32 [128], P('ctx'), may hold values from 0 to 511
Outputs:
- mixed: bfloat16 [2, 2048, 8192], P(None, 'ctx', 'fsdp')
The draws below stay inside these ranges and needn't reach their ends.
Inputs may be any that keep to these rules, and one draw needn't show every extreme that they name: Each block of 256 consecutive positions holds exactly 16 distinct variant positions, and they are listed among that block's 16 entries of var_pos.
All inputs are finite; a program needn't handle non-finite values.
Results may differ from the reference program's by a relative error of at most 0.025.
Values may be sent and summed in bfloat16 or wider, within the bound.
No kernel may reach another device: no remote copies, remote signals or barrier semaphores. Data moves between devices by JAX's collectives and lax.ppermute only.
A program may use at most 128 MiB of HBM per device.

```python
import jax
import jax.numpy as jnp
from jax import lax

D = 8192
VOCAB = 512
HD = 128
TOK_DEV = 256
VAR_DEV = 16
HEADS = 32
L = 2048
NVAR = 128


def draw_hidden(key, part):
    noise = jax.random.truncated_normal(jax.random.fold_in(key, 311), -6.0, 6.0, (L, D), jnp.float32)
    return noise.astype(jnp.bfloat16)


def draw_qkv_weight(key, part):
    base = jax.random.truncated_normal(jax.random.fold_in(key, 523), -6.0, 6.0, (D, 3 * HEADS * HD), jnp.float32) * D ** (-0.5)
    return base.astype(jnp.bfloat16)


def draw_var_pos(key, part):
    blocks_count = L // TOK_DEV
    keys_list = jax.random.split(key, blocks_count)

    def one_block(block_key):
        return jax.random.permutation(block_key, TOK_DEV)[:VAR_DEV]
    picked = jax.vmap(one_block)(keys_list)
    offsets = (jnp.arange(blocks_count) * TOK_DEV)[:, None]
    return (picked + offsets).reshape(-1).astype(jnp.int32)


def with_ends(array, own_key, least, largest):
    spot = [jax.random.randint(jax.random.fold_in(own_key, axis), (), 0, length) for axis, length in enumerate(array.shape)]
    widest = array.shape.index(max(array.shape))
    beside = spot[:widest] + [(spot[widest] + 1) % array.shape[widest]] + spot[widest + 1:]
    return array.at[tuple(spot)].set(least).at[tuple(beside)].set(largest)


def block_levels(stream_key, extent, pieces, least, top_value):
    level, own = 1.0, jax.random.fold_in(stream_key, 6)
    for dim, blocks in pieces:
        heights = jnp.exp(jax.random.uniform(jax.random.fold_in(own, dim), (blocks,), jnp.float32, least / len(pieces), top_value / len(pieces)))
        level = level * jnp.repeat(heights, extent[dim] // blocks).reshape([-1 if axis == dim else 1 for axis in range(len(extent))])
    return level


def scatter_about(rng, extent, width, most, cuts=(), dtype=jnp.bfloat16):
    array = jax.random.normal(rng, extent, jnp.float32) * width
    if len(cuts) > 0:
        array = block_levels(rng, extent, cuts, -0.22, 0.18) * array
    return jnp.clip(array, min=-most, max=most).astype(dtype)


def setup_inputs(seed: int = 0) -> dict:
    seeds = jax.random.split(jax.random.key(seed), 9)
    return {
        "hidden": draw_hidden(jax.random.fold_in(seeds[8], 71), 0),
        "gain": jnp.clip(1.0 + 0.15 * jax.random.normal(seeds[1], (D,), jnp.float32), 0.25, 1.75).astype(jnp.bfloat16),
        "embed": scatter_about(seeds[2], (VOCAB, D), 1.0, 6.0, ((1, 32),)),
        "qkv_weight": draw_qkv_weight(jax.random.fold_in(seeds[8], 71), 0),
        "out_weight": scatter_about(seeds[4], (HEADS * HD, D), (HD // 4) ** -0.5, 1.0, ((0, 32),)),
        "ref_ids": with_ends(jax.random.randint(seeds[5], (L,), 0, VOCAB), jax.random.fold_in(seeds[5], 1), 0, VOCAB - 1).astype(jnp.int32),
        "var_pos": draw_var_pos(jax.random.fold_in(seeds[8], 71), 0),
        "var_base": with_ends(jax.random.randint(seeds[7], (NVAR,), 0, VOCAB), jax.random.fold_in(seeds[7], 1), 0, VOCAB - 1).astype(jnp.int32),
    }


epsilon = 1e-05
rope_base = 10000.0

def rotate(values, positions):
    half = values.shape[-1] // 2
    exponent = jnp.arange(half).astype(jnp.float32) * (-2.0 / values.shape[-1])
    inv_freq = jnp.power(jnp.float32(rope_base), exponent)
    angle = positions.astype(jnp.float32)[:, None] * inv_freq[None, :]
    cosine = jnp.cos(angle)
    sine = jnp.sin(angle)
    first = values[..., :half]
    second = values[..., half:]
    return jnp.concatenate([first * cosine - second * sine, second * cosine + first * sine], axis=-1)

def reference(hidden, gain, embed, qkv_weight, out_weight, ref_ids, var_pos, var_base):
    change = embed[var_base].astype(jnp.float32) - embed[ref_ids[var_pos]].astype(jnp.float32)
    var_rows = (hidden[var_pos].astype(jnp.float32) + change).astype(jnp.bfloat16)
    variant = hidden.at[var_pos].set(var_rows)
    seqs = jnp.stack([hidden, variant])
    widened = seqs.astype(jnp.float32)
    inv_rms = lax.rsqrt(lax.optimization_barrier(jnp.sum(widened * widened, axis=-1)) / D + epsilon)
    scaled = (widened * gain.astype(jnp.float32)).astype(jnp.bfloat16)
    proj = jnp.dot(scaled.reshape(2 * L, D), qkv_weight, preferred_element_type=jnp.float32)
    proj = proj.reshape(2, L, HEADS, 3, HD) * inv_rms[:, :, None, None, None]
    proj = jnp.transpose(proj, (2, 3, 0, 1, 4))
    positions = jnp.arange(L)
    queries = rotate(proj[:, 0], positions).astype(jnp.bfloat16)
    keys = rotate(proj[:, 1], positions).astype(jnp.bfloat16)
    values = proj[:, 2].astype(jnp.bfloat16)
    causal = positions[:, None] >= positions[None, :]
    score_scale = 1.0 / HD ** 0.5
    out_rows = out_weight.reshape(HEADS, HD, D)

    def one_head(total, items):
        q_head, k_head, v_head, w_head = items
        score = jnp.einsum('sqd,skd->sqk', q_head.astype(jnp.float32), k_head.astype(jnp.float32)) * score_scale
        score = jnp.where(causal[None], score, -jnp.inf)
        top = lax.optimization_barrier(jnp.max(score, axis=-1, keepdims=True))
        probs = jnp.exp(score - top)
        rounded = lax.optimization_barrier(probs.astype(jnp.bfloat16)).astype(jnp.float32)
        numer = jnp.einsum('sqk,skd->sqd', rounded, v_head.astype(jnp.float32))
        attn = (numer / lax.optimization_barrier(jnp.sum(probs, axis=-1, keepdims=True))).astype(jnp.bfloat16)
        part = jnp.dot(attn.reshape(2 * L, HD), w_head, preferred_element_type=jnp.float32).astype(jnp.bfloat16)
        return (total + part.astype(jnp.float32), None)
    branch, unused = lax.scan(one_head, jnp.zeros((2 * L, D), jnp.float32), (queries, keys, values, out_rows))
    return (widened + branch.reshape(2, L, D)).astype(jnp.bfloat16)
```

```python
import functools

import jax
import jax.numpy as jnp
from jax import lax
from jax.experimental import pallas as pl
from jax.experimental.pallas import tpu as pltpu
from jax.sharding import Mesh, PartitionSpec as P

epsilon = 1e-05
rope_base = 10000.0

X_HI, Z, CORE, X_LO, Y = 2, 8, 2, 2, 4
FSDP = ("x_hi", "z", "core")
CTX = ("x_lo", "y")
HD = 128
TOK = 256
VAR = 16
ROWS = TOK + VAR
PAY = ROWS + VAR
bf16 = jnp.bfloat16
f32 = jnp.float32
VMEM_LIMIT = 48 * 1024 * 1024


def shift(value, axis, size, distance):
    return lax.ppermute(value, axis, [(i, (i + distance) % size) for i in range(size)])


def shift_ctx(value, dx, dy):
    route = [
        (a * Y + b, ((a + dx) % X_LO) * Y + (b + dy) % Y) for a in range(X_LO) for b in range(Y)
    ]
    return lax.ppermute(value, CTX, route)


def vmem():
    return pl.BlockSpec(memory_space=pltpu.VMEM)


def smem():
    return pl.BlockSpec(memory_space=pltpu.SMEM)


def anywhere():
    return pl.BlockSpec(memory_space=pl.ANY)


def pick_kernel(place, w, kv_send, q_send, kv_own, q_own, sems):
    z, core, x_hi = place[0], place[1], place[2]
    copies = []
    for k in range(Z):
        for xr in range(X_HI):
            head_pair = lax.rem(x_hi + xr, X_HI) * Z + lax.rem(z + k, Z)
            slot = k * X_HI + xr
            for side, (kv, q) in enumerate(((kv_send, q_send), (kv_own, q_own))):
                mine = core if side else 1 - core
                start = (head_pair * 2 + mine) * (3 * HD)
                copies.append(
                    pltpu.make_async_copy(
                        w.at[:, pl.ds(pl.multiple_of(start + HD, HD), 2 * HD)],
                        kv.at[:, pl.ds(slot * 2 * HD, 2 * HD)],
                        sems.at[side, 0, slot],
                    )
                )
                copies.append(
                    pltpu.make_async_copy(
                        w.at[:, pl.ds(pl.multiple_of(start, HD), HD)],
                        q.at[:, pl.ds(slot * HD, HD)],
                        sems.at[side, 1, slot],
                    )
                )
    for copy in copies:
        copy.start()
    for copy in copies:
        copy.wait()


def pick_columns(place, w):
    rows = w.shape[0]
    kv = jax.ShapeDtypeStruct((rows, Z * X_HI * 2 * HD), bf16)
    q = jax.ShapeDtypeStruct((rows, Z * X_HI * HD), bf16)
    return pl.pallas_call(
        pick_kernel,
        out_shape=(kv, q, kv, q),
        in_specs=[smem(), anywhere()],
        out_specs=(anywhere(),) * 4,
        scratch_shapes=[pltpu.SemaphoreType.DMA((2, 2, Z * X_HI))],
    )(place, w)


def partial_kernel(width, x_own, x_sis, w_own, w_sis, *outs):
    for k in range(Z):
        cols = slice(k * width, (k + 1) * width)
        acc = jnp.dot(x_own[...], w_own[:, cols], preferred_element_type=f32)
        acc = acc + jnp.dot(x_sis[...], w_sis[:, cols], preferred_element_type=f32)
        outs[k][...] = acc.astype(bf16)


def partials(x_own, x_sis, w_own, w_sis):
    width = w_own.shape[1] // Z
    out = jax.ShapeDtypeStruct((ROWS, width), bf16)
    return pl.pallas_call(
        functools.partial(partial_kernel, width),
        out_shape=(out,) * Z,
        in_specs=[vmem()] * 4,
        out_specs=(vmem(),) * Z,
        compiler_params=pltpu.CompilerParams(vmem_limit_bytes=VMEM_LIMIT),
    )(x_own, x_sis, w_own, w_sis)


def add(a, b):
    return (a.astype(f32) + b.astype(f32)).astype(bf16)


def ring_sum(parts):
    half = parts[0].shape[1] // 2
    up = parts[4][:, :half]
    down = parts[4][:, half:]
    up = shift(up, "z", Z, 1)
    down = shift(down, "z", Z, -1)
    up = jnp.concatenate([add(up, parts[3][:, :half]), parts[3][:, half:]], axis=1)
    down = jnp.concatenate([parts[5][:, :half], add(down, parts[5][:, half:])], axis=1)
    for k in (2, 1):
        up = shift(up, "z", Z, 1)
        down = shift(down, "z", Z, -1)
        up = add(up, parts[k])
        down = add(down, parts[Z - k])
    up = shift(up, "z", Z, 1)
    down = shift(down, "z", Z, -1)
    return parts[0].astype(f32) + up.astype(f32) + down.astype(f32)


def finish_sum(parts):
    total = ring_sum(parts)
    half = total.shape[1] // 2
    other = shift(total[:, half:].astype(bf16), "x_hi", X_HI, 1)
    return total[:, :half], other


def rotated(x, cosine, sine):
    return x * cosine + pltpu.roll(x, HD // 2, 1) * sine


def kv_kernel(mine, other, inv, cosine, sine, onehot, out):
    kv = (mine[...] + other[...].astype(f32))
    scale = inv[...]
    key = rotated(kv[:, :HD] * scale, cosine[...], sine[...])
    out[:ROWS, :HD] = key.astype(bf16)
    out[:ROWS, HD:] = (kv[:, HD:] * scale).astype(bf16)
    out[ROWS:, :] = onehot[...]


def q_kernel(mine, other, inv, cosine, sine, out):
    q = (mine[...] + other[...].astype(f32)) * inv[...]
    out[...] = rotated(q, cosine[...], sine[...]).astype(bf16)


def attend_kernel(seen, q_ref, *refs):
    blocks = refs[:8]
    out, top, denom, total = refs[8:]
    scale = 1.0 / HD**0.5
    contract_rows = (((0,), (0,)), ((), ()))
    contract_cols = (((1,), (1,)), ((), ()))

    def varied(block, base, rows):
        spots = block[ROWS:, :]
        changed = lax.dot_general(
            spots, jnp.ones((VAR, HD), bf16), contract_rows, preferred_element_type=f32
        )
        placed = lax.dot_general(spots, rows, contract_rows, preferred_element_type=f32)
        return jnp.where(changed > 0.5, placed, base.astype(f32)).astype(bf16)

    q_base = q_ref[:TOK, :]
    queries = (q_base, varied(blocks[0], q_base, q_ref[TOK:, :]))

    def pieces(block, seq):
        key, value = block[:TOK, :HD], block[:TOK, HD:]
        if seq == 1:
            key = varied(block, key, block[TOK:ROWS, :HD])
            value = varied(block, value, block[TOK:ROWS, HD:])
        return key, value

    for seq in range(2):
        key, value = pieces(blocks[0], seq)
        score = lax.dot_general(queries[seq], key, contract_cols, preferred_element_type=f32) * scale
        row = lax.broadcasted_iota(jnp.int32, (TOK, TOK), 0)
        col = lax.broadcasted_iota(jnp.int32, (TOK, TOK), 1)
        score = jnp.where(row >= col, score, -jnp.inf)
        peak = jnp.max(score, axis=1, keepdims=True)
        probs = jnp.exp(score - peak)
        top[seq] = peak
        denom[seq] = jnp.sum(probs, axis=1, keepdims=True)
        total[seq] = jnp.dot(probs.astype(bf16), value, preferred_element_type=f32)

    for j in range(1, 8):

        @pl.when(seen[j] > 0)
        def _():
            for seq in range(2):
                key, value = pieces(blocks[j], seq)
                score = (
                    lax.dot_general(queries[seq], key, contract_cols, preferred_element_type=f32)
                    * scale
                )
                peak = jnp.maximum(top[seq], jnp.max(score, axis=1, keepdims=True))
                probs = jnp.exp(score - peak)
                factor = jnp.exp(top[seq] - peak)
                top[seq] = peak
                denom[seq] = denom[seq] * factor + jnp.sum(probs, axis=1, keepdims=True)
                total[seq] = total[seq] * factor + jnp.dot(
                    probs.astype(bf16), value, preferred_element_type=f32
                )

    for seq in range(2):
        out[seq * TOK : (seq + 1) * TOK, :] = (total[seq] / denom[seq]).astype(bf16)


def attend(seen, q, blocks):
    return pl.pallas_call(
        attend_kernel,
        out_shape=jax.ShapeDtypeStruct((2 * TOK, HD), bf16),
        in_specs=[smem()] + [vmem()] * 9,
        out_specs=vmem(),
        scratch_shapes=[
            pltpu.VMEM((2, TOK, 1), f32),
            pltpu.VMEM((2, TOK, 1), f32),
            pltpu.VMEM((2, TOK, HD), f32),
        ],
        compiler_params=pltpu.CompilerParams(vmem_limit_bytes=VMEM_LIMIT),
    )(seen, q, *blocks)


def project_kernel(place, w, *refs):
    shards, (keep, near, far) = refs[:Z], refs[Z:]
    z, core, x_hi = place[0], place[1], place[2]
    for xr in range(X_HI):
        for cr in range(CORE):
            column = (lax.rem(x_hi + xr, X_HI) * CORE + lax.rem(core + cr, CORE)) * TOK
            column = pl.multiple_of(column, TOK)
            acc = None
            for d in range(Z):
                source = lax.rem(z + Z - d, Z)
                term = jnp.dot(
                    shards[d][...], w[source, :, pl.ds(column, TOK)], preferred_element_type=f32
                )
                acc = term if acc is None else acc + term
            if cr == 1:
                near[:, xr * TOK : (xr + 1) * TOK] = acc.astype(bf16)
            elif xr == 0:
                keep[...] = acc
            else:
                far[...] = acc


def project(place, w, shards):
    rows = shards[0].shape[0]
    return pl.pallas_call(
        project_kernel,
        out_shape=(
            jax.ShapeDtypeStruct((rows, TOK), f32),
            jax.ShapeDtypeStruct((rows, 2 * TOK), bf16),
            jax.ShapeDtypeStruct((rows, TOK), f32),
        ),
        in_specs=[smem()] + [vmem()] * (1 + Z),
        out_specs=(vmem(),) * 3,
        compiler_params=pltpu.CompilerParams(vmem_limit_bytes=VMEM_LIMIT),
    )(place, w, *shards)


def shards(hidden, gain, embed, qkv_weight, out_weight, ref_ids, var_pos, var_base):
    tok_rows, width_part = hidden.shape
    vocab_size = embed.shape[0]
    full_width = out_weight.shape[1]
    x_hi, z, core = lax.axis_index("x_hi"), lax.axis_index("z"), lax.axis_index("core")
    x_lo, y = lax.axis_index("x_lo"), lax.axis_index("y")
    my_block = x_lo * Y + y
    my_slice = (x_hi * Z + z) * CORE + core
    place = jnp.stack([z, core, x_hi]).astype(jnp.int32)

    with jax.named_scope("weights"):
        kv_send, q_send, kv_own, q_own = pick_columns(place, qkv_weight)
        kv_sis = shift(kv_send, "core", CORE, 1)
        q_sis = shift(q_send, "core", CORE, 1)

    with jax.named_scope("variant"):
        local_pos = var_pos - my_block * tok_rows
        var_spots = local_pos[:, None] == jnp.arange(tok_rows)[None, :]
        onehot = var_spots.astype(bf16)
        changed = jnp.any(var_spots, axis=0)
        ref_at = jnp.sum(jnp.where(var_spots, ref_ids[None, :], 0), axis=1)
        vocab_line = jnp.arange(vocab_size)[None, :]
        onehot_diff = (vocab_line == var_base[:, None]).astype(bf16) - (
            vocab_line == ref_at[:, None]
        ).astype(bf16)
        change = jnp.dot(onehot_diff, embed, preferred_element_type=f32)
        picked_rows = jnp.dot(onehot, hidden, preferred_element_type=f32)
        var_rows = (picked_rows + change).astype(bf16)
        rows = jnp.concatenate([hidden, var_rows], axis=0)
        widened = rows.astype(f32)
        gain_part = lax.dynamic_slice(gain, (my_slice * width_part,), (width_part,)).astype(f32)
        scaled = (widened * gain_part[None, :]).astype(bf16)
        scaled_sis = shift(scaled, "core", CORE, 1)
        squares = lax.psum(jnp.sum(widened * widened, axis=1), FSDP)

    with jax.named_scope("tables"):
        positions = jnp.concatenate([my_block * tok_rows + jnp.arange(tok_rows), var_pos])
        exponent = jnp.arange(HD // 2).astype(f32) * (-2.0 / HD)
        inv_freq = jnp.power(f32(rope_base), exponent)
        angle = positions.astype(f32)[:, None] * inv_freq[None, :]
        cosine, sine = jnp.cos(angle), jnp.sin(angle)
        cosine = jnp.concatenate([cosine, cosine], axis=1)
        sine = jnp.concatenate([-sine, sine], axis=1)
        inv_rms = lax.rsqrt(squares / full_width + epsilon)
        inv = jnp.broadcast_to(inv_rms[:, None], (ROWS, HD))

    with jax.named_scope("projection"):
        kv_parts = partials(scaled, scaled_sis, kv_own, kv_sis)
        q_parts = partials(scaled, scaled_sis, q_own, q_sis)
        kv_mine, kv_other = finish_sum(kv_parts)
        payload = pl.pallas_call(
            kv_kernel,
            out_shape=jax.ShapeDtypeStruct((PAY, 2 * HD), bf16),
            in_specs=[vmem()] * 6,
            out_specs=vmem(),
        )(kv_mine, kv_other, inv, cosine, sine, onehot)
        q_mine, q_other = finish_sum(q_parts)
        q = pl.pallas_call(
            q_kernel,
            out_shape=jax.ShapeDtypeStruct((ROWS, HD), bf16),
            in_specs=[vmem()] * 5,
            out_specs=vmem(),
        )(q_mine, q_other, inv, cosine, sine)

    with jax.named_scope("out_weights"):
        eighth = tok_rows // (X_LO * Y) // 2
        mine = lax.dynamic_slice(out_weight, (my_block * eighth, 0), (eighth, full_width))
        mine = mine.reshape(eighth, X_HI, Z, 2 * width_part).transpose(2, 0, 1, 3)
        mine = mine.reshape(Z, eighth, X_HI * 2 * width_part)
        mine = lax.all_to_all(mine, "z", 0, 0, tiled=True)
        out_w = lax.all_gather(mine, CTX, axis=1, tiled=True)

    with jax.named_scope("attention"):
        blocks, seen = [payload], [jnp.int32(1)]
        for dy in (2, 1, 3, 0):
            for dx in (1, 0):
                if dx or dy:
                    blocks.append(shift_ctx(payload, dx, dy))
                    source = lax.rem(x_lo + dx, X_LO) * Y + lax.rem(y + Y - dy, Y)
                    seen.append((source < my_block).astype(jnp.int32))
        attn = attend(jnp.stack(seen), q, blocks)

    with jax.named_scope("output"):
        pieces = [None] * Z
        pieces[0] = attn
        for d in (4, 3, 5, 2, 6, 1, 7):
            pieces[d] = shift(attn, "z", Z, d)
        keep, near, far = project(place, out_w, pieces)
        near = shift(near, "core", CORE, 1).astype(f32)
        far = (far + near[:, width_part:]).astype(bf16)
        far = shift(far, "x_hi", X_HI, 1).astype(f32)
        branch = (keep + near[:, :width_part] + far).reshape(2, tok_rows, width_part)
        placed = jnp.dot(onehot.T, var_rows, preferred_element_type=f32)
        variant = jnp.where(changed[:, None], placed, hidden.astype(f32))
        seqs = jnp.stack([hidden.astype(f32), variant])
        return (seqs + branch).astype(bf16)


def solution(mesh):
    fine = Mesh(mesh.devices.reshape(X_HI, Z, CORE, X_LO, Y), (*FSDP, *CTX))
    in_specs = (
        P(CTX, FSDP),
        P(),
        P(None, FSDP),
        P(FSDP, None),
        P(FSDP, None),
        P(CTX),
        P(CTX),
        P(CTX),
    )
    out_specs = P(None, CTX, FSDP)
    return jax.shard_map(shards, mesh=fine, in_specs=in_specs, out_specs=out_specs, check_vma=False)
```

```python
import functools

import jax
import jax.numpy as jnp
from jax import lax
from jax.experimental import pallas as pl
from jax.experimental.pallas import tpu as pltpu
from jax.sharding import Mesh, PartitionSpec as P

epsilon = 1e-05
rope_base = 10000.0

X_HI, Z, CORE, X_LO, Y = 2, 8, 2, 2, 4
FSDP = ("x_hi", "z", "core")
CTX = ("x_lo", "y")
HD = 128
TOK = 256
VAR = 16
ROWS = TOK + VAR
PAY = ROWS + VAR
bf16 = jnp.bfloat16
f32 = jnp.float32
CTX_SHIFTS = ((0, 0), (1, 2), (0, 2), (1, 1), (0, 1), (1, 3), (0, 3), (1, 0))
VMEM_LIMIT = 48 * 1024 * 1024


def shift(value, axis, size, distance):
    return lax.ppermute(value, axis, [(i, (i + distance) % size) for i in range(size)])


def shift_ctx(value, dx, dy):
    route = [
        (a * Y + b, ((a + dx) % X_LO) * Y + (b + dy) % Y) for a in range(X_LO) for b in range(Y)
    ]
    return lax.ppermute(value, CTX, route)


def vmem():
    return pl.BlockSpec(memory_space=pltpu.VMEM)


def smem():
    return pl.BlockSpec(memory_space=pltpu.SMEM)


def anywhere():
    return pl.BlockSpec(memory_space=pl.ANY)


def pick_kernel(sister, w, kv, q, sems):
    z, core, x_hi = lax.axis_index("z"), lax.axis_index("core"), lax.axis_index("x_hi")
    whose = 1 - core if sister else core
    copies = []
    for k in range(Z):
        for xr in range(X_HI):
            head_pair = lax.rem(x_hi + xr, X_HI) * Z + lax.rem(z + k, Z)
            slot = k * X_HI + xr
            start = (head_pair * 2 + whose) * (3 * HD)
            copies.append(
                pltpu.make_async_copy(
                    w.at[:, pl.ds(pl.multiple_of(start + HD, HD), 2 * HD)],
                    kv.at[:, pl.ds(slot * 2 * HD, 2 * HD)],
                    sems.at[0, slot],
                )
            )
            copies.append(
                pltpu.make_async_copy(
                    w.at[:, pl.ds(pl.multiple_of(start, HD), HD)],
                    q.at[:, pl.ds(slot * HD, HD)],
                    sems.at[1, slot],
                )
            )
    for copy in copies:
        copy.start()
    for copy in copies:
        copy.wait()


def pick_columns(sister, w):
    rows = w.shape[0]
    kv = jax.ShapeDtypeStruct((rows, Z * X_HI * 2 * HD), bf16)
    q = jax.ShapeDtypeStruct((rows, Z * X_HI * HD), bf16)
    return pl.pallas_call(
        functools.partial(pick_kernel, sister),
        out_shape=(kv, q),
        in_specs=[anywhere()],
        out_specs=(vmem(), vmem()),
        scratch_shapes=[pltpu.SemaphoreType.DMA((2, Z * X_HI))],
    )(w)


def partial_kernel(width, x_own, x_sis, w_own, w_sis, out, up, down):
    def product(k):
        cols = pl.ds(pl.multiple_of(k * width, width), width)
        acc = jnp.dot(x_own[...], w_own[:, cols], preferred_element_type=f32)
        acc = acc + jnp.dot(x_sis[...], w_sis[:, cols], preferred_element_type=f32)
        return acc.astype(bf16)

    def step(k, carry):
        out[k] = product(k)
        return carry

    lax.fori_loop(0, Z, step, 0)
    up[...] = out[Z // 2][:, : width // 2]
    down[...] = out[Z // 2][:, width // 2 :]


def partials(x_own, x_sis, w_own, w_sis):
    width = w_own.shape[1] // Z
    half = jax.ShapeDtypeStruct((ROWS, width // 2), bf16)
    return pl.pallas_call(
        functools.partial(partial_kernel, width),
        out_shape=(jax.ShapeDtypeStruct((Z, ROWS, width), bf16), half, half),
        in_specs=[vmem()] * 4,
        out_specs=(vmem(),) * 3,
        compiler_params=pltpu.CompilerParams(vmem_limit_bytes=VMEM_LIMIT),
    )(x_own, x_sis, w_own, w_sis)


def add(a, b):
    return (a.astype(f32) + b.astype(f32)).astype(bf16)


def ring_sum(parts, up, down):
    half = up.shape[1]
    up = shift(up, "z", Z, 1)
    down = shift(down, "z", Z, -1)
    up = jnp.concatenate([add(up, parts[3, :, :half]), parts[3, :, half:]], axis=1)
    down = jnp.concatenate([parts[5, :, :half], add(down, parts[5, :, half:])], axis=1)
    for k in (2, 1):
        up = shift(up, "z", Z, 1)
        down = shift(down, "z", Z, -1)
        up = add(up, parts[k])
        down = add(down, parts[Z - k])
    up = shift(up, "z", Z, 1)
    down = shift(down, "z", Z, -1)
    return parts[0].astype(f32) + up.astype(f32) + down.astype(f32)


def finish_sum(parts):
    total = ring_sum(*parts)
    half = total.shape[1] // 2
    other = shift(total[:, half:].astype(bf16), "x_hi", X_HI, 1)
    return total[:, :half], other


def rotated(x, cosine, sine):
    return x * cosine + pltpu.roll(x, HD // 2, 1) * sine


def kv_kernel(mine, other, inv, cosine, sine, onehot, out):
    kv = (mine[...] + other[...].astype(f32))
    scale = inv[...]
    key = rotated(kv[:, :HD] * scale, cosine[...], sine[...])
    out[:ROWS, :HD] = key.astype(bf16)
    out[:ROWS, HD:] = (kv[:, HD:] * scale).astype(bf16)
    out[ROWS:, :] = onehot[...]


def q_kernel(mine, other, inv, cosine, sine, out):
    q = (mine[...] + other[...].astype(f32)) * inv[...]
    out[...] = rotated(q, cosine[...], sine[...]).astype(bf16)


def attend_kernel(q_ref, *refs):
    x_lo, y = lax.axis_index("x_lo"), lax.axis_index("y")
    blocks = refs[:8]
    out, top, denom, total = refs[8:]
    scale = 1.0 / HD**0.5
    contract_rows = (((0,), (0,)), ((), ()))
    contract_cols = (((1,), (1,)), ((), ()))

    def varied(block, base, rows):
        spots = block[ROWS:, :]
        changed = lax.dot_general(
            spots, jnp.ones((VAR, HD), bf16), contract_rows, preferred_element_type=f32
        )
        placed = lax.dot_general(spots, rows, contract_rows, preferred_element_type=f32)
        return jnp.where(changed > 0.5, placed, base.astype(f32)).astype(bf16)

    q_base = q_ref[:TOK, :]
    queries = (q_base, varied(blocks[0], q_base, q_ref[TOK:, :]))

    def pieces(block, seq):
        key, value = block[:TOK, :HD], block[:TOK, HD:]
        if seq == 1:
            key = varied(block, key, block[TOK:ROWS, :HD])
            value = varied(block, value, block[TOK:ROWS, HD:])
        return key, value

    for seq in range(2):
        key, value = pieces(blocks[0], seq)
        score = lax.dot_general(queries[seq], key, contract_cols, preferred_element_type=f32) * scale
        row = lax.broadcasted_iota(jnp.int32, (TOK, TOK), 0)
        col = lax.broadcasted_iota(jnp.int32, (TOK, TOK), 1)
        score = jnp.where(row >= col, score, -jnp.inf)
        peak = jnp.max(score, axis=1, keepdims=True)
        probs = jnp.exp(score - peak)
        top[seq] = peak
        denom[seq] = jnp.sum(probs, axis=1, keepdims=True)
        total[seq] = jnp.dot(probs.astype(bf16), value, preferred_element_type=f32)

    for j in range(1, 8):

        dx, dy = CTX_SHIFTS[j]
        source = lax.rem(x_lo + dx, X_LO) * Y + lax.rem(y + Y - dy, Y)

        @pl.when(source < x_lo * Y + y)
        def _():
            for seq in range(2):
                key, value = pieces(blocks[j], seq)
                score = (
                    lax.dot_general(queries[seq], key, contract_cols, preferred_element_type=f32)
                    * scale
                )
                peak = jnp.maximum(top[seq], jnp.max(score, axis=1, keepdims=True))
                probs = jnp.exp(score - peak)
                factor = jnp.exp(top[seq] - peak)
                top[seq] = peak
                denom[seq] = denom[seq] * factor + jnp.sum(probs, axis=1, keepdims=True)
                total[seq] = total[seq] * factor + jnp.dot(
                    probs.astype(bf16), value, preferred_element_type=f32
                )

    for seq in range(2):
        out[seq * TOK : (seq + 1) * TOK, :] = (total[seq] / denom[seq]).astype(bf16)


def attend(q, blocks):
    return pl.pallas_call(
        attend_kernel,
        out_shape=jax.ShapeDtypeStruct((2 * TOK, HD), bf16),
        in_specs=[vmem()] * 9,
        out_specs=vmem(),
        scratch_shapes=[
            pltpu.VMEM((2, TOK, 1), f32),
            pltpu.VMEM((2, TOK, 1), f32),
            pltpu.VMEM((2, TOK, HD), f32),
        ],
        compiler_params=pltpu.CompilerParams(vmem_limit_bytes=VMEM_LIMIT),
    )(q, *blocks)


def project_kernel(w, *refs):
    shards, (keep, near, far), (joined, turned) = refs[:Z], refs[Z : Z + 3], refs[Z + 3 :]
    z, core, x_hi = lax.axis_index("z"), lax.axis_index("core"), lax.axis_index("x_hi")
    for d in range(Z):
        joined[:, d * HD : (d + 1) * HD] = shards[d][...]
        source = lax.rem(z + Z - d, Z)
        turned[d * HD : (d + 1) * HD, :] = w[source]

    def product(xr, cr, rows):
        column = (lax.rem(x_hi + xr, X_HI) * CORE + lax.rem(core + cr, CORE)) * TOK
        column = pl.ds(pl.multiple_of(column, TOK), TOK)
        return jnp.dot(joined[rows, :], turned[:, column], preferred_element_type=f32)

    size = 128

    def step(i, carry):
        rows = pl.ds(pl.multiple_of(i * size, size), size)
        for xr in range(X_HI):
            near[rows, xr * TOK : (xr + 1) * TOK] = product(xr, 1, rows).astype(bf16)
        keep[rows, :] = product(0, 0, rows)
        far[rows, :] = product(1, 0, rows)
        return carry

    lax.fori_loop(0, 2 * TOK // size, step, 0)


def project(w, shards):
    rows = shards[0].shape[0]
    return pl.pallas_call(
        project_kernel,
        out_shape=(
            jax.ShapeDtypeStruct((rows, TOK), f32),
            jax.ShapeDtypeStruct((rows, 2 * TOK), bf16),
            jax.ShapeDtypeStruct((rows, TOK), f32),
        ),
        in_specs=[vmem()] * (1 + Z),
        out_specs=(vmem(),) * 3,
        scratch_shapes=[
            pltpu.VMEM((rows, Z * HD), bf16),
            pltpu.VMEM((Z * HD, w.shape[2]), bf16),
        ],
        compiler_params=pltpu.CompilerParams(vmem_limit_bytes=VMEM_LIMIT),
    )(w, *shards)


def shards(hidden, gain, embed, qkv_weight, out_weight, ref_ids, var_pos, var_base):
    tok_rows, width_part = hidden.shape
    vocab_size = embed.shape[0]
    full_width = out_weight.shape[1]
    x_hi, z, core = lax.axis_index("x_hi"), lax.axis_index("z"), lax.axis_index("core")
    x_lo, y = lax.axis_index("x_lo"), lax.axis_index("y")
    my_block = x_lo * Y + y
    my_slice = (x_hi * Z + z) * CORE + core

    with jax.named_scope("weights"):
        kv_send, q_send = pick_columns(True, qkv_weight)
        kv_sis = shift(kv_send, "core", CORE, 1)
        q_sis = shift(q_send, "core", CORE, 1)
        kv_own, q_own = pick_columns(False, qkv_weight)

    with jax.named_scope("variant"):
        local_pos = var_pos - my_block * tok_rows
        var_spots = local_pos[:, None] == jnp.arange(tok_rows)[None, :]
        onehot = var_spots.astype(bf16)
        changed = jnp.any(var_spots, axis=0)
        ref_at = jnp.sum(jnp.where(var_spots, ref_ids[None, :], 0), axis=1)
        vocab_line = jnp.arange(vocab_size)[None, :]
        onehot_diff = (vocab_line == var_base[:, None]).astype(bf16) - (
            vocab_line == ref_at[:, None]
        ).astype(bf16)
        change = jnp.dot(onehot_diff, embed, preferred_element_type=f32)
        picked_rows = jnp.dot(onehot, hidden, preferred_element_type=f32)
        var_rows = (picked_rows + change).astype(bf16)
        rows = jnp.concatenate([hidden, var_rows], axis=0)
        widened = rows.astype(f32)
        gain_part = lax.dynamic_slice(gain, (my_slice * width_part,), (width_part,)).astype(f32)
        scaled = (widened * gain_part[None, :]).astype(bf16)
        scaled_sis = shift(scaled, "core", CORE, 1)
        squares = jnp.sum(widened * widened, axis=1)
        squares = squares + shift(squares, "core", CORE, 1)
        squares = squares + shift(squares, "x_hi", X_HI, 1)
        for distance in (1, 2, 4):
            squares = squares + shift(squares, "z", Z, distance)

    with jax.named_scope("tables"):
        positions = jnp.concatenate([my_block * tok_rows + jnp.arange(tok_rows), var_pos])
        exponent = jnp.arange(HD // 2).astype(f32) * (-2.0 / HD)
        inv_freq = jnp.power(f32(rope_base), exponent)
        angle = positions.astype(f32)[:, None] * inv_freq[None, :]
        cosine, sine = jnp.cos(angle), jnp.sin(angle)
        cosine = jnp.concatenate([cosine, cosine], axis=1)
        sine = jnp.concatenate([-sine, sine], axis=1)
        inv_rms = lax.rsqrt(squares / full_width + epsilon)
        inv = jnp.broadcast_to(inv_rms[:, None], (ROWS, HD))

    with jax.named_scope("projection"):
        kv_parts = partials(scaled, scaled_sis, kv_own, kv_sis)
        q_parts = partials(scaled, scaled_sis, q_own, q_sis)
        kv_mine, kv_other = finish_sum(kv_parts)
        payload = pl.pallas_call(
            kv_kernel,
            out_shape=jax.ShapeDtypeStruct((PAY, 2 * HD), bf16),
            in_specs=[vmem()] * 6,
            out_specs=vmem(),
        )(kv_mine, kv_other, inv, cosine, sine, onehot)
        q_mine, q_other = finish_sum(q_parts)
        q = pl.pallas_call(
            q_kernel,
            out_shape=jax.ShapeDtypeStruct((ROWS, HD), bf16),
            in_specs=[vmem()] * 5,
            out_specs=vmem(),
        )(q_mine, q_other, inv, cosine, sine)

    with jax.named_scope("out_weights"):
        eighth = tok_rows // (X_LO * Y) // 2
        mine = lax.dynamic_slice(out_weight, (my_block * eighth, 0), (eighth, full_width))
        mine = mine.reshape(eighth, X_HI, Z, 2 * width_part).transpose(2, 0, 1, 3)
        mine = mine.reshape(Z, eighth, X_HI * 2 * width_part)
        mine = lax.all_to_all(mine, "z", 0, 0, tiled=True)
        out_w = lax.all_gather(mine, CTX, axis=1, tiled=True)

    with jax.named_scope("attention"):
        blocks = [payload] + [shift_ctx(payload, dx, dy) for dx, dy in CTX_SHIFTS[1:]]
        attn = attend(q, blocks)

    with jax.named_scope("output"):
        pieces = [None] * Z
        pieces[0] = attn
        for d in (4, 3, 5, 2, 6, 1, 7):
            pieces[d] = shift(attn, "z", Z, d)
        keep, near, far = project(out_w, pieces)
        near = shift(near, "core", CORE, 1).astype(f32)
        far = (far + near[:, width_part:]).astype(bf16)
        far = shift(far, "x_hi", X_HI, 1).astype(f32)
        branch = (keep + near[:, :width_part] + far).reshape(2, tok_rows, width_part)
        placed = jnp.dot(onehot.T, var_rows, preferred_element_type=f32)
        variant = jnp.where(changed[:, None], placed, hidden.astype(f32))
        seqs = jnp.stack([hidden.astype(f32), variant])
        return (seqs + branch).astype(bf16)


def solution(mesh):
    fine = Mesh(mesh.devices.reshape(X_HI, Z, CORE, X_LO, Y), (*FSDP, *CTX))
    in_specs = (
        P(CTX, FSDP),
        P(),
        P(None, FSDP),
        P(FSDP, None),
        P(FSDP, None),
        P(CTX),
        P(CTX),
        P(CTX),
    )
    out_specs = P(None, CTX, FSDP)
    return jax.shard_map(shards, mesh=fine, in_specs=in_specs, out_specs=out_specs, check_vma=False)
```

```python
import functools

import jax
import jax.numpy as jnp
from jax import lax
from jax.experimental import pallas as pl
from jax.experimental.pallas import tpu as pltpu
from jax.sharding import Mesh, PartitionSpec as P

epsilon = 1e-05
rope_base = 10000.0

X_HI, Z, CORE, X_LO, Y = 2, 8, 2, 2, 4
FSDP = ("x_hi", "z", "core")
CTX = ("x_lo", "y")
BLOCKS = X_LO * Y
HD = 128
QKV = 3 * HD
TOK = 256
VAR = 16
ROWS = TOK + VAR
SUM_ROWS = ROWS + 16
PAY = ROWS + VAR
bf16 = jnp.bfloat16
f32 = jnp.float32
MIB = 1024 * 1024


def shift(value, axis, size, distance):
    return lax.ppermute(value, axis, [(i, (i + distance) % size) for i in range(size)])


def vmem():
    return pl.BlockSpec(memory_space=pltpu.VMEM)


def anywhere():
    return pl.BlockSpec(memory_space=pl.ANY)


def limit(mib):
    return pltpu.CompilerParams(vmem_limit_bytes=mib * MIB)


def column_copies(w, out, sems, sister):
    z, core, x_hi = lax.axis_index("z"), lax.axis_index("core"), lax.axis_index("x_hi")
    whose = 1 - core if sister else core
    copies = []
    for k in range(Z):
        for xr in range(X_HI):
            head_pair = lax.rem(x_hi + xr, X_HI) * Z + lax.rem(z + k, Z)
            slot = k * X_HI + xr
            start = pl.multiple_of((head_pair * 2 + whose) * QKV, HD)
            copies.append(
                pltpu.make_async_copy(
                    w.at[:, pl.ds(start, QKV)],
                    out.at[:, pl.ds(slot * QKV, QKV)],
                    sems.at[slot],
                )
            )
    return copies


def pick_kernel(w, out, sems):
    copies = column_copies(w, out, sems, True)
    for copy in copies:
        copy.start()
    for copy in copies:
        copy.wait()


def pick_columns(w):
    return pl.pallas_call(
        pick_kernel,
        out_shape=jax.ShapeDtypeStruct((w.shape[0], Z * X_HI * QKV), bf16),
        in_specs=[anywhere()],
        out_specs=vmem(),
        scratch_shapes=[pltpu.SemaphoreType.DMA((Z * X_HI,))],
        compiler_params=limit(8),
    )(w)


def two_rows(row, width):
    high = row.astype(bf16)
    low = (row - high.astype(f32)).astype(bf16)
    line = lax.broadcasted_iota(jnp.int32, (16, width), 0)
    both = jnp.where(line == 0, high.astype(f32), jnp.where(line == 1, low.astype(f32), 0.0))
    return both.astype(bf16)


def one_row(rows):
    return jnp.sum(rows.astype(f32), axis=0, keepdims=True)


def partial_kernel(own, sis, gains, w, w_sis, out, up, down, w_own, sems):
    copies = column_copies(w, w_own, sems, False)
    for copy in copies:
        copy.start()
    width = X_HI * QKV
    own_rows, sis_rows = own[...].astype(f32), sis[...].astype(f32)
    x_own = (own_rows * gains[0:1, :]).astype(bf16)
    x_sis = (sis_rows * gains[1:2, :]).astype(bf16)
    squares = jnp.sum(own_rows * own_rows + sis_rows * sis_rows, axis=1, keepdims=True)
    line = lax.broadcasted_iota(jnp.int32, (ROWS, QKV), 0)
    lane = lax.broadcasted_iota(jnp.int32, (ROWS, QKV), 1)
    row = jnp.sum(jnp.where(line == lane, squares, 0.0), axis=0, keepdims=True)
    tail = two_rows(row, QKV)
    for copy in copies:
        copy.wait()

    def step(k, carry):
        cols = pl.ds(pl.multiple_of(k * width, width), width)
        acc = jnp.dot(x_own, w_own[:, cols], preferred_element_type=f32)
        acc = acc + jnp.dot(x_sis, w_sis[:, cols], preferred_element_type=f32)
        out[k, :ROWS, :] = acc.astype(bf16)
        out[k, ROWS:, :QKV] = tail
        out[k, ROWS:, QKV:] = tail
        return carry

    lax.fori_loop(0, Z, step, 0)
    up[...] = out[Z // 2, :, :QKV]
    down[...] = out[Z // 2, :, QKV:]


def partials(own, sis, gains, w, w_sis):
    half = jax.ShapeDtypeStruct((SUM_ROWS, QKV), bf16)
    return pl.pallas_call(
        partial_kernel,
        out_shape=(jax.ShapeDtypeStruct((Z, SUM_ROWS, X_HI * QKV), bf16), half, half),
        in_specs=[vmem(), vmem(), vmem(), anywhere(), vmem()],
        out_specs=(vmem(),) * 3,
        scratch_shapes=[
            pltpu.VMEM((w.shape[0], Z * X_HI * QKV), bf16),
            pltpu.SemaphoreType.DMA((Z * X_HI,)),
        ],
        compiler_params=limit(24),
    )(own, sis, gains, w, w_sis)


def store_sum(out, cols, terms):
    body = sum(term[:ROWS].astype(f32) for term in terms)
    row = sum(one_row(term[ROWS:]) for term in terms)
    out[:ROWS, cols] = body.astype(bf16)
    out[ROWS:, cols] = two_rows(row, row.shape[1])


def first_kernel(up, down, near_up, near_down, out_up, out_down):
    left, right = slice(0, QKV), slice(QKV, 2 * QKV)
    store_sum(out_up, left, [up[...], near_up[0, :, left]])
    out_up[:, right] = near_up[0, :, right]
    out_down[:, left] = near_down[0, :, left]
    store_sum(out_down, right, [down[...], near_down[0, :, right]])


def next_kernel(up, down, near_up, near_down, out_up, out_down):
    every = slice(0, 2 * QKV)
    store_sum(out_up, every, [up[...], near_up[0]])
    store_sum(out_down, every, [down[...], near_down[0]])


def part(k):
    return pl.BlockSpec((1, SUM_ROWS, X_HI * QKV), lambda i: (k, 0, 0))


def whole(shape):
    return pl.BlockSpec(shape, lambda i: (0, 0))


def ring_add(kernel, up, down, parts, k):
    shape = (SUM_ROWS, X_HI * QKV)
    out = jax.ShapeDtypeStruct(shape, bf16)
    return pl.pallas_call(
        kernel,
        grid=(1,),
        out_shape=(out, out),
        in_specs=[whole(up.shape), whole(down.shape), part(k), part(Z - k)],
        out_specs=(whole(shape), whole(shape)),
        compiler_params=limit(12),
    )(up, down, parts, parts)


def last_kernel(up, down, near, mine, other):
    own, far = slice(0, QKV), slice(QKV, 2 * QKV)
    terms = [up, down, near.at[0]]
    mine[:ROWS] = sum(term[:ROWS, own].astype(f32) for term in terms)
    row = sum(one_row(term[ROWS:, own]) for term in terms)
    mine[ROWS:] = jnp.broadcast_to(row, (8, QKV))
    store_sum(other, slice(0, QKV), [term[:, far] for term in terms])


def ring_last(up, down, parts):
    return pl.pallas_call(
        last_kernel,
        grid=(1,),
        out_shape=(
            jax.ShapeDtypeStruct((ROWS + 8, QKV), f32),
            jax.ShapeDtypeStruct((SUM_ROWS, QKV), bf16),
        ),
        in_specs=[whole(up.shape), whole(down.shape), part(0)],
        out_specs=(whole((ROWS + 8, QKV)), whole((SUM_ROWS, QKV))),
        compiler_params=limit(12),
    )(up, down, parts)


def rotated(x, cosine, sine):
    return x * cosine + pltpu.roll(x, HD // 2, 1) * sine


def finish_kernel(full_width, mine, other, cosine, sine, onehot, payload, queries):
    row = mine[ROWS : ROWS + 1, :] + one_row(other[ROWS:, :])
    line = lax.broadcasted_iota(jnp.int32, (ROWS, QKV), 0)
    lane = lax.broadcasted_iota(jnp.int32, (ROWS, QKV), 1)
    squares = jnp.sum(jnp.where(line == lane, row, 0.0), axis=1, keepdims=True)
    inv_rms = lax.rsqrt(squares / full_width + epsilon)
    proj = (mine[:ROWS, :] + other[:ROWS, :].astype(f32)) * inv_rms
    query = rotated(proj[:, :HD], cosine[...], sine[...]).astype(bf16)
    key = rotated(proj[:, HD : 2 * HD], cosine[...], sine[...]).astype(bf16)
    value = proj[:, 2 * HD :].astype(bf16)
    spots = onehot[...]

    def step(b, carry):
        payload[b, :ROWS, :HD] = key
        payload[b, :ROWS, HD:] = value
        payload[b, ROWS:, :] = spots
        return carry

    lax.fori_loop(0, BLOCKS, step, 0)
    contract = (((0,), (0,)), ((), ()))
    ones = jnp.ones((VAR, HD), bf16)
    changed = lax.dot_general(spots, ones, contract, preferred_element_type=f32)
    placed = lax.dot_general(spots, query[TOK:], contract, preferred_element_type=f32)
    base = query[:TOK]
    queries[:TOK] = base
    queries[TOK:] = jnp.where(changed > 0.5, placed, base.astype(f32)).astype(bf16)


def finish(full_width, mine, other, cosine, sine, onehot):
    return pl.pallas_call(
        functools.partial(finish_kernel, full_width),
        out_shape=(
            jax.ShapeDtypeStruct((BLOCKS, PAY, 2 * HD), bf16),
            jax.ShapeDtypeStruct((2 * TOK, HD), bf16),
        ),
        in_specs=[vmem()] * 5,
        out_specs=(vmem(), vmem()),
        compiler_params=limit(12),
    )(mine, other, cosine, sine, onehot)


def attend_kernel(queries, blocks, out, scores, peak, denom, total, var_kv, spots):
    my_block = lax.axis_index("x_lo") * Y + lax.axis_index("y")
    scale = 1.0 / HD**0.5
    by_cols = (((1,), (1,)), ((), ()))
    lowest = -jnp.inf
    query = queries[...]

    def score_block(j, own):
        score = lax.dot_general(
            query, blocks[j, :TOK, :HD], by_cols, preferred_element_type=f32
        ) * scale
        gone = jnp.sum(blocks[j, ROWS:, :].astype(f32), axis=0, keepdims=True) > 0.5
        line = lax.broadcasted_iota(jnp.int32, (2 * TOK, TOK), 0)
        hidden = (line >= TOK) & gone
        if own:
            lane = lax.broadcasted_iota(jnp.int32, (2 * TOK, TOK), 1)
            hidden = hidden | (lax.rem(line, TOK) < lane)
        return jnp.where(hidden, lowest, score)

    score = score_block(my_block, True)
    scores[my_block] = score
    peak[...] = jnp.maximum(score[:, :HD], score[:, HD:])

    def first(j, carry):
        score = score_block(j, False)
        scores[j] = score
        peak[...] = jnp.maximum(peak[...], jnp.maximum(score[:, :HD], score[:, HD:]))
        return carry

    lax.fori_loop(0, my_block, first, 0)

    for j in range(BLOCKS):
        var_kv[j * VAR : (j + 1) * VAR, :] = blocks[j, TOK:ROWS, :]
        spots[j * VAR : (j + 1) * VAR, :] = blocks[j, ROWS:, :]
    row = lax.broadcasted_iota(jnp.int32, (TOK, TOK), 0)
    col = lax.broadcasted_iota(jnp.int32, (TOK, TOK), 1)
    reached = lax.dot_general(
        jnp.where(row >= col, 1.0, 0.0).astype(bf16), spots[...], by_cols, preferred_element_type=f32
    )
    source = lax.broadcasted_iota(jnp.int32, (TOK, BLOCKS * VAR), 1) // VAR
    seen = (source < my_block) | ((source == my_block) & (reached > 0.5))
    more = lax.dot_general(
        query[TOK:], var_kv[:, :HD], by_cols, preferred_element_type=f32
    ) * scale
    more = jnp.where(seen, more, lowest)
    peak[TOK:, :] = jnp.maximum(peak[TOK:, :], more)
    top = jnp.max(peak[...], axis=1, keepdims=True)
    peak[...] = jnp.broadcast_to(top, (2 * TOK, HD))

    more = jnp.exp(more - top[TOK:])
    denom[:TOK, :] = jnp.zeros((TOK, HD), f32)
    denom[TOK:, :] = more
    total[:TOK, :] = jnp.zeros((TOK, HD), f32)
    total[TOK:, :] = jnp.dot(more.astype(bf16), var_kv[:, HD:], preferred_element_type=f32)

    def second(j, carry):
        best = peak[...]
        left = jnp.exp(scores[j, :, :HD] - best)
        right = jnp.exp(scores[j, :, HD:] - best)
        denom[...] = denom[...] + left + right
        probs = jnp.concatenate([left.astype(bf16), right.astype(bf16)], axis=1)
        total[...] = total[...] + jnp.dot(
            probs, blocks[j, :TOK, HD:], preferred_element_type=f32
        )
        return carry

    lax.fori_loop(0, my_block + 1, second, 0)
    out[...] = (total[...] / jnp.sum(denom[...], axis=1, keepdims=True)).astype(bf16)


def attend(queries, blocks):
    return pl.pallas_call(
        attend_kernel,
        out_shape=jax.ShapeDtypeStruct((2 * TOK, HD), bf16),
        in_specs=[vmem(), vmem()],
        out_specs=vmem(),
        scratch_shapes=[
            pltpu.VMEM((BLOCKS, 2 * TOK, TOK), f32),
            pltpu.VMEM((2 * TOK, HD), f32),
            pltpu.VMEM((2 * TOK, HD), f32),
            pltpu.VMEM((2 * TOK, HD), f32),
            pltpu.VMEM((BLOCKS * VAR, 2 * HD), bf16),
            pltpu.VMEM((BLOCKS * VAR, TOK), bf16),
        ],
        compiler_params=limit(16),
    )(queries, blocks)


def share_kernel(w, out, sems):
    my_block = lax.axis_index("x_lo") * Y + lax.axis_index("y")
    share, columns = out.shape[1], out.shape[2] // X_HI
    copies = []
    for k in range(Z):
        for x in range(X_HI):
            copies.append(
                pltpu.make_async_copy(
                    w.at[pl.ds(pl.multiple_of(my_block * share, share), share), pl.ds((x * Z + k) * columns, columns)],
                    out.at[k, :, pl.ds(x * columns, columns)],
                    sems.at[k, x],
                )
            )
    for copy in copies:
        copy.start()
    for copy in copies:
        copy.wait()


def share_rows(w):
    rows, columns = w.shape
    return pl.pallas_call(
        share_kernel,
        out_shape=jax.ShapeDtypeStruct((Z, rows // BLOCKS, columns // Z), bf16),
        in_specs=[anywhere()],
        out_specs=vmem(),
        scratch_shapes=[pltpu.SemaphoreType.DMA((Z, X_HI))],
        compiler_params=limit(4),
    )(w)


def project_kernel(w, *refs):
    shards, (keep, near, far), (joined, turned) = refs[:Z], refs[Z : Z + 3], refs[Z + 3 :]
    z, core, x_hi = lax.axis_index("z"), lax.axis_index("core"), lax.axis_index("x_hi")
    for d in range(Z):
        joined[:, d * HD : (d + 1) * HD] = shards[d][...]
        source = lax.rem(z + Z - d, Z)
        turned[d * HD : (d + 1) * HD, :] = w[source]

    def product(xr, cr, rows):
        column = (lax.rem(x_hi + xr, X_HI) * CORE + lax.rem(core + cr, CORE)) * TOK
        column = pl.ds(pl.multiple_of(column, TOK), TOK)
        return jnp.dot(joined[rows, :], turned[:, column], preferred_element_type=f32)

    size = 128

    def step(i, carry):
        rows = pl.ds(pl.multiple_of(i * size, size), size)
        for xr in range(X_HI):
            near[rows, xr * TOK : (xr + 1) * TOK] = product(xr, 1, rows).astype(bf16)
        keep[rows, :] = product(0, 0, rows)
        far[rows, :] = product(1, 0, rows)
        return carry

    lax.fori_loop(0, 2 * TOK // size, step, 0)


def project(w, shards):
    rows = shards[0].shape[0]
    return pl.pallas_call(
        project_kernel,
        out_shape=(
            jax.ShapeDtypeStruct((rows, TOK), f32),
            jax.ShapeDtypeStruct((rows, 2 * TOK), bf16),
            jax.ShapeDtypeStruct((rows, TOK), f32),
        ),
        in_specs=[vmem()] * (1 + Z),
        out_specs=(vmem(),) * 3,
        scratch_shapes=[
            pltpu.VMEM((rows, Z * HD), bf16),
            pltpu.VMEM((Z * HD, w.shape[2]), bf16),
        ],
        compiler_params=limit(16),
    )(w, *shards)


def shards(hidden, gain, embed, qkv_weight, out_weight, ref_ids, var_pos, var_base):
    tok_rows, width_part = hidden.shape
    vocab_size = embed.shape[0]
    full_width = out_weight.shape[1]
    x_hi, z, core = lax.axis_index("x_hi"), lax.axis_index("z"), lax.axis_index("core")
    my_block = lax.axis_index("x_lo") * Y + lax.axis_index("y")
    chip_slice = x_hi * Z + z

    with jax.named_scope("weights"):
        w_sis = shift(pick_columns(qkv_weight), "core", CORE, 1)

    with jax.named_scope("variant"):
        local_pos = var_pos - my_block * tok_rows
        var_spots = local_pos[:, None] == jnp.arange(tok_rows)[None, :]
        onehot = var_spots.astype(bf16)
        changed = jnp.any(var_spots, axis=0)
        ref_at = jnp.sum(jnp.where(var_spots, ref_ids[None, :], 0), axis=1)
        vocab_line = jnp.arange(vocab_size)[None, :]
        onehot_diff = (vocab_line == var_base[:, None]).astype(bf16) - (
            vocab_line == ref_at[:, None]
        ).astype(bf16)
        change = jnp.dot(onehot_diff, embed, preferred_element_type=f32)
        picked_rows = jnp.dot(onehot, hidden, preferred_element_type=f32)
        var_rows = (picked_rows + change).astype(bf16)
        rows = jnp.concatenate([hidden, var_rows], axis=0)
        rows_sis = shift(rows, "core", CORE, 1)
        gains = lax.dynamic_slice(gain, (chip_slice * 2 * width_part,), (2 * width_part,))
        gains = gains.astype(f32).reshape(2, width_part)
        gains = jnp.where(core == 0, gains, gains[::-1])

    with jax.named_scope("projection"):
        parts, up, down = partials(rows, rows_sis, gains, qkv_weight, w_sis)
        up, down = shift(up, "z", Z, 1), shift(down, "z", Z, -1)
        up, down = ring_add(first_kernel, up, down, parts, 3)
        for k in (2, 1):
            up, down = shift(up, "z", Z, 1), shift(down, "z", Z, -1)
            if k == 2:
                out_weight, up, down = lax.optimization_barrier((out_weight, up, down))
            up, down = ring_add(next_kernel, up, down, parts, k)
        up, down = shift(up, "z", Z, 1), shift(down, "z", Z, -1)
        mine, other = ring_last(up, down, parts)
        other = shift(other, "x_hi", X_HI, 1)

    with jax.named_scope("tables"):
        positions = jnp.concatenate([my_block * tok_rows + jnp.arange(tok_rows), var_pos])
        exponent = jnp.arange(HD // 2).astype(f32) * (-2.0 / HD)
        inv_freq = jnp.power(f32(rope_base), exponent)
        angle = positions.astype(f32)[:, None] * inv_freq[None, :]
        cosine, sine = jnp.cos(angle), jnp.sin(angle)
        cosine = jnp.concatenate([cosine, cosine], axis=1)
        sine = jnp.concatenate([-sine, sine], axis=1)

    with jax.named_scope("out_weights"):
        shared = lax.all_to_all(share_rows(out_weight), "z", 0, 0, tiled=True)
        out_w = lax.all_gather(shared, CTX, axis=1, tiled=True)

    with jax.named_scope("attention"):
        payload, queries = finish(full_width, mine, other, cosine, sine, onehot)
        blocks = lax.all_to_all(payload, CTX, 0, 0, tiled=True)
        attn = attend(queries, blocks)

    with jax.named_scope("output"):
        pieces = [None] * Z
        pieces[0] = attn
        for d in (4, 3, 5, 2, 6, 1, 7):
            pieces[d] = shift(attn, "z", Z, d)
        keep, near, far = project(out_w, pieces)
        near = shift(near, "core", CORE, 1).astype(f32)
        far = (far + near[:, width_part:]).astype(bf16)
        far = shift(far, "x_hi", X_HI, 1).astype(f32)
        branch = (keep + near[:, :width_part] + far).reshape(2, tok_rows, width_part)
        placed = jnp.dot(onehot.T, var_rows, preferred_element_type=f32)
        variant = jnp.where(changed[:, None], placed, hidden.astype(f32))
        seqs = jnp.stack([hidden.astype(f32), variant])
        return (seqs + branch).astype(bf16)


def solution(mesh):
    fine = Mesh(mesh.devices.reshape(X_HI, Z, CORE, X_LO, Y), (*FSDP, *CTX))
    in_specs = (
        P(CTX, FSDP),
        P(),
        P(None, FSDP),
        P(FSDP, None),
        P(FSDP, None),
        P(CTX),
        P(CTX),
        P(CTX),
    )
    out_specs = P(None, CTX, FSDP)
    return jax.shard_map(shards, mesh=fine, in_specs=in_specs, out_specs=out_specs, check_vma=False)
```

```python
import functools

import jax
import jax.numpy as jnp
from jax import lax
from jax.experimental import pallas as pl
from jax.experimental.pallas import tpu as pltpu
from jax.sharding import Mesh, PartitionSpec as P

epsilon = 1e-05
rope_base = 10000.0

X_HI, Z, CORE, X_LO, Y = 2, 8, 2, 2, 4
FSDP = ("x_hi", "z", "core")
CTX = ("x_lo", "y")
BLOCKS = X_LO * Y
HD = 128
QKV = 3 * HD
TOK = 256
VAR = 16
ROWS = TOK + VAR
SUM_ROWS = ROWS + 16
PAY = ROWS + VAR
bf16 = jnp.bfloat16
f32 = jnp.float32
MIB = 1024 * 1024


def shift(value, axis, size, distance):
    return lax.ppermute(value, axis, [(i, (i + distance) % size) for i in range(size)])


def vmem():
    return pl.BlockSpec(memory_space=pltpu.VMEM)


def anywhere():
    return pl.BlockSpec(memory_space=pl.ANY)


def hbm():
    return pl.BlockSpec(memory_space=pltpu.HBM)


def limit(mib):
    return pltpu.CompilerParams(vmem_limit_bytes=mib * MIB)


FIRST = (3, 4, 5)
SECOND = (6, 7, 0, 1, 2)


def pick_kernel(w, *refs):
    sems = refs[-1]
    z, core, x_hi = lax.axis_index("z"), lax.axis_index("core"), lax.axis_index("x_hi")
    copies = []
    for index, (whose, ks) in enumerate(
        ((1 - core, FIRST), (1 - core, SECOND), (core, FIRST), (core, SECOND))
    ):
        for i, k in enumerate(ks):
            for xr in range(X_HI):
                head_pair = lax.rem(x_hi + xr, X_HI) * Z + lax.rem(z + k, Z)
                slot = i * X_HI + xr
                start = pl.multiple_of((head_pair * 2 + whose) * QKV, HD)
                copies.append(
                    pltpu.make_async_copy(
                        w.at[:, pl.ds(start, QKV)],
                        refs[index].at[:, slot * QKV : (slot + 1) * QKV],
                        sems.at[index, slot],
                    )
                )
    for copy in copies:
        copy.start()
    for copy in copies:
        copy.wait()


def pick_columns(w):
    first = jax.ShapeDtypeStruct((w.shape[0], len(FIRST) * X_HI * QKV), bf16)
    second = jax.ShapeDtypeStruct((w.shape[0], len(SECOND) * X_HI * QKV), bf16)
    return pl.pallas_call(
        pick_kernel,
        out_shape=(first, second, first, second),
        in_specs=[hbm()],
        out_specs=(vmem(),) * 4,
        scratch_shapes=[pltpu.SemaphoreType.DMA((4, len(SECOND) * X_HI))],
        compiler_params=limit(12),
    )(w)


def two_rows(row, width):
    high = row.astype(bf16)
    low = (row - high.astype(f32)).astype(bf16)
    line = lax.broadcasted_iota(jnp.int32, (16, width), 0)
    both = jnp.where(line == 0, high.astype(f32), jnp.where(line == 1, low.astype(f32), 0.0))
    return both.astype(bf16)


def one_row(rows):
    return jnp.sum(rows.astype(f32), axis=0, keepdims=True)


def partial_kernel(ks, own, sis, gains, w_own, w_sis, *outs):
    width = X_HI * QKV
    core = lax.axis_index("core")
    own_rows, sis_rows = own[...].astype(f32), sis[...].astype(f32)
    left, right = gains[:, :TOK].astype(f32), gains[:, TOK:].astype(f32)
    x_own = (own_rows * jnp.where(core == 0, left, right)).astype(bf16)
    x_sis = (sis_rows * jnp.where(core == 0, right, left)).astype(bf16)
    squares = jnp.sum(own_rows * own_rows + sis_rows * sis_rows, axis=1, keepdims=True)
    line = lax.broadcasted_iota(jnp.int32, (ROWS, QKV), 0)
    lane = lax.broadcasted_iota(jnp.int32, (ROWS, QKV), 1)
    row = jnp.sum(jnp.where(line == lane, squares, 0.0), axis=0, keepdims=True)
    tail = two_rows(row, QKV)

    def product(slot, count):
        cols = slice(slot * QKV, (slot + count) * QKV)
        acc = jnp.dot(x_own, w_own[:, cols], preferred_element_type=f32)
        acc = acc + jnp.dot(x_sis, w_sis[:, cols], preferred_element_type=f32)
        return acc.astype(bf16)

    outs = list(outs)
    for i, k in enumerate(ks):
        if k == Z // 2:
            for xr in range(X_HI):
                out = outs.pop(0)
                out[:ROWS, :] = product(i * X_HI + xr, 1)
                out[ROWS:, :] = tail
        else:
            out = outs.pop(0)
            out[:ROWS, :] = product(i * X_HI, X_HI)
            out[ROWS:, :QKV] = tail
            out[ROWS:, QKV:] = tail


def partials(ks, own, sis, gains, w_own, w_sis):
    half = jax.ShapeDtypeStruct((SUM_ROWS, QKV), bf16)
    full = jax.ShapeDtypeStruct((SUM_ROWS, X_HI * QKV), bf16)
    shapes = []
    for k in ks:
        shapes += [half, half] if k == Z // 2 else [full]
    return pl.pallas_call(
        functools.partial(partial_kernel, ks),
        out_shape=tuple(shapes),
        in_specs=[vmem()] * 5,
        out_specs=(vmem(),) * len(shapes),
        compiler_params=limit(20),
        cost_estimate=pl.CostEstimate(
            flops=4 * ROWS * w_own.size, bytes_accessed=8 * w_own.size, transcendentals=0
        ),
    )(own, sis, gains, w_own, w_sis)


def store_sum(out, cols, terms):
    body = sum(term[:ROWS].astype(f32) for term in terms)
    row = sum(one_row(term[ROWS:]) for term in terms)
    out[:ROWS, cols] = body.astype(bf16)
    out[ROWS:, cols] = two_rows(row, row.shape[1])


def first_kernel(up, down, near_up, near_down, out_up, out_down):
    left, right = slice(0, QKV), slice(QKV, 2 * QKV)
    store_sum(out_up, left, [up[...], near_up[:, left]])
    out_up[:, right] = near_up[:, right]
    out_down[:, left] = near_down[:, left]
    store_sum(out_down, right, [down[...], near_down[:, right]])


def next_kernel(up, down, near_up, near_down, out_up, out_down):
    every = slice(0, 2 * QKV)
    store_sum(out_up, every, [up[...], near_up[...]])
    store_sum(out_down, every, [down[...], near_down[...]])


def ring_add(kernel, up, down, near_up, near_down):
    out = jax.ShapeDtypeStruct((SUM_ROWS, X_HI * QKV), bf16)
    return pl.pallas_call(
        kernel,
        out_shape=(out, out),
        in_specs=[vmem()] * 4,
        out_specs=(vmem(), vmem()),
        compiler_params=limit(8),
    )(up, down, near_up, near_down)


def last_kernel(up, down, near, mine, other):
    own, far = slice(0, QKV), slice(QKV, 2 * QKV)
    terms = [up, down, near]
    mine[:ROWS] = sum(term[:ROWS, own].astype(f32) for term in terms)
    row = sum(one_row(term[ROWS:, own]) for term in terms)
    mine[ROWS:] = jnp.broadcast_to(row, (8, QKV))
    store_sum(other, slice(0, QKV), [term[:, far] for term in terms])


def ring_last(up, down, near):
    return pl.pallas_call(
        last_kernel,
        out_shape=(
            jax.ShapeDtypeStruct((ROWS + 8, QKV), f32),
            jax.ShapeDtypeStruct((SUM_ROWS, QKV), bf16),
        ),
        in_specs=[vmem()] * 3,
        out_specs=(vmem(), vmem()),
        compiler_params=limit(8),
    )(up, down, near)


def rotated(x, cosine, sine):
    return x * cosine + pltpu.roll(x, HD // 2, 1) * sine


def finish_kernel(full_width, mine, other, cosine, sine, onehot, payload, queries):
    row = mine[ROWS : ROWS + 1, :] + one_row(other[ROWS:, :])
    line = lax.broadcasted_iota(jnp.int32, (ROWS, QKV), 0)
    lane = lax.broadcasted_iota(jnp.int32, (ROWS, QKV), 1)
    squares = jnp.sum(jnp.where(line == lane, row, 0.0), axis=1, keepdims=True)
    inv_rms = lax.rsqrt(squares / full_width + epsilon)
    proj = (mine[:ROWS, :] + other[:ROWS, :].astype(f32)) * inv_rms
    query = rotated(proj[:, :HD], cosine[...], sine[...]).astype(bf16)
    key = rotated(proj[:, HD : 2 * HD], cosine[...], sine[...]).astype(bf16)
    value = proj[:, 2 * HD :].astype(bf16)
    spots = onehot[...]

    def step(b, carry):
        payload[b, :ROWS, :HD] = key
        payload[b, :ROWS, HD:] = value
        payload[b, ROWS:, :] = spots
        return carry

    lax.fori_loop(0, BLOCKS, step, 0)
    contract = (((0,), (0,)), ((), ()))
    ones = jnp.ones((VAR, HD), bf16)
    changed = lax.dot_general(spots, ones, contract, preferred_element_type=f32)
    placed = lax.dot_general(spots, query[TOK:], contract, preferred_element_type=f32)
    base = query[:TOK]
    queries[:TOK] = base
    queries[TOK:] = jnp.where(changed > 0.5, placed, base.astype(f32)).astype(bf16)


def finish(full_width, mine, other, cosine, sine, onehot):
    return pl.pallas_call(
        functools.partial(finish_kernel, full_width),
        out_shape=(
            jax.ShapeDtypeStruct((BLOCKS, PAY, 2 * HD), bf16),
            jax.ShapeDtypeStruct((2 * TOK, HD), bf16),
        ),
        in_specs=[vmem()] * 5,
        out_specs=(vmem(), vmem()),
        compiler_params=limit(12),
    )(mine, other, cosine, sine, onehot)


def attend_kernel(queries, blocks, out, scores, peak, denom, total, var_kv, spots):
    my_block = lax.axis_index("x_lo") * Y + lax.axis_index("y")
    scale = 1.0 / HD**0.5
    by_cols = (((1,), (1,)), ((), ()))
    lowest = -jnp.inf
    query = queries[...]

    def score_block(j, own):
        score = lax.dot_general(
            query, blocks[j, :TOK, :HD], by_cols, preferred_element_type=f32
        ) * scale
        gone = jnp.sum(blocks[j, ROWS:, :].astype(f32), axis=0, keepdims=True) > 0.5
        line = lax.broadcasted_iota(jnp.int32, (2 * TOK, TOK), 0)
        hidden = (line >= TOK) & gone
        if own:
            lane = lax.broadcasted_iota(jnp.int32, (2 * TOK, TOK), 1)
            hidden = hidden | (lax.rem(line, TOK) < lane)
        return jnp.where(hidden, lowest, score)

    score = score_block(my_block, True)
    scores[my_block] = score
    peak[...] = jnp.maximum(score[:, :HD], score[:, HD:])

    def first(j, carry):
        score = score_block(j, False)
        scores[j] = score
        peak[...] = jnp.maximum(peak[...], jnp.maximum(score[:, :HD], score[:, HD:]))
        return carry

    lax.fori_loop(0, my_block, first, 0)

    for j in range(BLOCKS):
        var_kv[j * VAR : (j + 1) * VAR, :] = blocks[j, TOK:ROWS, :]
        spots[j * VAR : (j + 1) * VAR, :] = blocks[j, ROWS:, :]
    row = lax.broadcasted_iota(jnp.int32, (TOK, TOK), 0)
    col = lax.broadcasted_iota(jnp.int32, (TOK, TOK), 1)
    reached = lax.dot_general(
        jnp.where(row >= col, 1.0, 0.0).astype(bf16), spots[...], by_cols, preferred_element_type=f32
    )
    source = lax.broadcasted_iota(jnp.int32, (TOK, BLOCKS * VAR), 1) // VAR
    seen = (source < my_block) | ((source == my_block) & (reached > 0.5))
    more = lax.dot_general(
        query[TOK:], var_kv[:, :HD], by_cols, preferred_element_type=f32
    ) * scale
    more = jnp.where(seen, more, lowest)
    peak[TOK:, :] = jnp.maximum(peak[TOK:, :], more)
    top = jnp.max(peak[...], axis=1, keepdims=True)
    peak[...] = jnp.broadcast_to(top, (2 * TOK, HD))

    more = jnp.exp(more - top[TOK:])
    denom[:TOK, :] = jnp.zeros((TOK, HD), f32)
    denom[TOK:, :] = more
    total[:TOK, :] = jnp.zeros((TOK, HD), f32)
    total[TOK:, :] = jnp.dot(more.astype(bf16), var_kv[:, HD:], preferred_element_type=f32)

    def second(j, carry):
        best = peak[...]
        left = jnp.exp(scores[j, :, :HD] - best)
        right = jnp.exp(scores[j, :, HD:] - best)
        denom[...] = denom[...] + left + right
        probs = jnp.concatenate([left.astype(bf16), right.astype(bf16)], axis=1)
        total[...] = total[...] + jnp.dot(
            probs, blocks[j, :TOK, HD:], preferred_element_type=f32
        )
        return carry

    lax.fori_loop(0, my_block + 1, second, 0)
    out[...] = (total[...] / jnp.sum(denom[...], axis=1, keepdims=True)).astype(bf16)


def attend(queries, blocks):
    return pl.pallas_call(
        attend_kernel,
        out_shape=jax.ShapeDtypeStruct((2 * TOK, HD), bf16),
        in_specs=[vmem(), vmem()],
        out_specs=vmem(),
        scratch_shapes=[
            pltpu.VMEM((BLOCKS, 2 * TOK, TOK), f32),
            pltpu.VMEM((2 * TOK, HD), f32),
            pltpu.VMEM((2 * TOK, HD), f32),
            pltpu.VMEM((2 * TOK, HD), f32),
            pltpu.VMEM((BLOCKS * VAR, 2 * HD), bf16),
            pltpu.VMEM((BLOCKS * VAR, TOK), bf16),
        ],
        compiler_params=limit(16),
    )(queries, blocks)


def share_kernel(w, out, buffer, sems, out_sem):
    my_block = lax.axis_index("x_lo") * Y + lax.axis_index("y")
    share, columns = buffer.shape[1], buffer.shape[2] // X_HI
    rows = pl.ds(pl.multiple_of(my_block * share, share), share)
    copies = []
    for k in range(Z):
        for x in range(X_HI):
            start = (x * Z + k) * columns
            copies.append(
                pltpu.make_async_copy(
                    w.at[rows, start : start + columns],
                    buffer.at[k, :, x * columns : (x + 1) * columns],
                    sems.at[k, x],
                )
            )
    for copy in copies:
        copy.start()
    for copy in copies:
        copy.wait()
    copy = pltpu.make_async_copy(buffer, out, out_sem)
    copy.start()
    copy.wait()


def share_rows(w):
    rows, columns = w.shape
    shape = (Z, rows // BLOCKS, columns // Z)
    return pl.pallas_call(
        share_kernel,
        out_shape=jax.ShapeDtypeStruct(shape, bf16),
        in_specs=[hbm()],
        out_specs=hbm(),
        scratch_shapes=[
            pltpu.VMEM(shape, bf16),
            pltpu.SemaphoreType.DMA((Z, X_HI)),
            pltpu.SemaphoreType.DMA(()),
        ],
        compiler_params=limit(4),
    )(w)


def project_kernel(w, *refs):
    shards, (keep, near, far), (joined, turned) = refs[:Z], refs[Z : Z + 3], refs[Z + 3 :]
    z, core, x_hi = lax.axis_index("z"), lax.axis_index("core"), lax.axis_index("x_hi")
    for d in range(Z):
        joined[:, d * HD : (d + 1) * HD] = shards[d][...]
        source = lax.rem(z + Z - d, Z)
        turned[d * HD : (d + 1) * HD, :] = w[source]

    def product(xr, cr, rows):
        column = (lax.rem(x_hi + xr, X_HI) * CORE + lax.rem(core + cr, CORE)) * TOK
        column = pl.ds(pl.multiple_of(column, TOK), TOK)
        return jnp.dot(joined[rows, :], turned[:, column], preferred_element_type=f32)

    size = 128

    def step(i, carry):
        rows = pl.ds(pl.multiple_of(i * size, size), size)
        for xr in range(X_HI):
            near[rows, xr * TOK : (xr + 1) * TOK] = product(xr, 1, rows).astype(bf16)
        keep[rows, :] = product(0, 0, rows)
        far[rows, :] = product(1, 0, rows)
        return carry

    lax.fori_loop(0, 2 * TOK // size, step, 0)


def project(w, shards):
    rows = shards[0].shape[0]
    return pl.pallas_call(
        project_kernel,
        out_shape=(
            jax.ShapeDtypeStruct((rows, TOK), f32),
            jax.ShapeDtypeStruct((rows, 2 * TOK), bf16),
            jax.ShapeDtypeStruct((rows, TOK), f32),
        ),
        in_specs=[vmem()] * (1 + Z),
        out_specs=(vmem(),) * 3,
        scratch_shapes=[
            pltpu.VMEM((rows, Z * HD), bf16),
            pltpu.VMEM((Z * HD, w.shape[2]), bf16),
        ],
        compiler_params=limit(16),
    )(w, *shards)


def shards(hidden, gain, embed, qkv_weight, out_weight, ref_ids, var_pos, var_base):
    tok_rows, width_part = hidden.shape
    vocab_size = embed.shape[0]
    full_width = out_weight.shape[1]
    x_hi, z, core = lax.axis_index("x_hi"), lax.axis_index("z"), lax.axis_index("core")
    my_block = lax.axis_index("x_lo") * Y + lax.axis_index("y")
    chip_slice = x_hi * Z + z

    with jax.named_scope("weights"):
        send_first, send_second, own_first, own_second = pick_columns(
            pltpu.with_memory_space_constraint(qkv_weight, pltpu.HBM)
        )
        sis_first = shift(send_first, "core", CORE, 1)

    with jax.named_scope("variant"):
        local_pos = var_pos - my_block * tok_rows
        var_spots = local_pos[:, None] == jnp.arange(tok_rows)[None, :]
        onehot = var_spots.astype(bf16)
        changed = jnp.any(var_spots, axis=0)
        ref_at = jnp.sum(jnp.where(var_spots, ref_ids[None, :], 0), axis=1)
        vocab_line = jnp.arange(vocab_size)[None, :]
        onehot_diff = (vocab_line == var_base[:, None]).astype(bf16) - (
            vocab_line == ref_at[:, None]
        ).astype(bf16)
        change = jnp.dot(onehot_diff, embed, preferred_element_type=f32)
        picked_rows = jnp.dot(onehot, hidden, preferred_element_type=f32)
        var_rows = (picked_rows + change).astype(bf16)
        rows = jnp.concatenate([hidden, var_rows], axis=0)
        rows, send_second = lax.optimization_barrier((rows, send_second))
        rows_sis = shift(rows, "core", CORE, 1)
        sis_second = shift(send_second, "core", CORE, 1)
        start = chip_slice * 2 * width_part
        gains = lax.dynamic_slice(gain.reshape(1, full_width), (0, start), (1, 2 * width_part))

    with jax.named_scope("projection"):
        near_up, up, down, near_down = partials(FIRST, rows, rows_sis, gains, own_first, sis_first)
        up, down = shift(up, "z", Z, 1), shift(down, "z", Z, -1)
        parts = partials(SECOND, rows, rows_sis, gains, own_second, sis_second)
        up, down, parts = lax.optimization_barrier((up, down, parts))
        up, down = ring_add(first_kernel, up, down, near_up, near_down)
        up, down, out_weight = lax.optimization_barrier((up, down, out_weight))
        parts = dict(zip(SECOND, parts))
        up, down = shift(up, "z", Z, 1), shift(down, "z", Z, -1)
        share = share_rows(pltpu.with_memory_space_constraint(out_weight, pltpu.HBM))
        shared = lax.all_to_all(share, "z", 0, 0, tiled=True)
        up, down = ring_add(next_kernel, up, down, parts[2], parts[6])
        up, down = shift(up, "z", Z, 1), shift(down, "z", Z, -1)
        shared, up, down = lax.optimization_barrier((shared, up, down))
        out_w = lax.all_gather(shared, CTX, axis=1, tiled=True)
        up, down = ring_add(next_kernel, up, down, parts[1], parts[7])
        up, down = shift(up, "z", Z, 1), shift(down, "z", Z, -1)
        mine, other = ring_last(up, down, parts[0])
        other = shift(other, "x_hi", X_HI, 1)

    with jax.named_scope("tables"):
        positions = jnp.concatenate([my_block * tok_rows + jnp.arange(tok_rows), var_pos])
        exponent = jnp.arange(HD // 2).astype(f32) * (-2.0 / HD)
        inv_freq = jnp.power(f32(rope_base), exponent)
        angle = positions.astype(f32)[:, None] * inv_freq[None, :]
        cosine, sine = jnp.cos(angle), jnp.sin(angle)
        cosine = jnp.concatenate([cosine, cosine], axis=1)
        sine = jnp.concatenate([-sine, sine], axis=1)

    with jax.named_scope("attention"):
        payload, queries = finish(full_width, mine, other, cosine, sine, onehot)
        blocks = lax.all_to_all(payload, CTX, 0, 0, tiled=True)
        attn = attend(queries, blocks)

    with jax.named_scope("output"):
        pieces = [attn] + [None] * (Z - 1)
        for d in (1, 2, 3):
            pieces[d] = shift(pieces[d - 1], "z", Z, 1)
            pieces[Z - d] = shift(pieces[(Z - d + 1) % Z], "z", Z, -1)
            if d == 1:
                pieces[Z // 2] = shift(attn, "z", Z, Z // 2)
        keep, near, far = project(out_w, pieces)
        near = shift(near, "core", CORE, 1).astype(f32)
        far = (far + near[:, width_part:]).astype(bf16)
        far = shift(far, "x_hi", X_HI, 1).astype(f32)
        branch = (keep + near[:, :width_part] + far).reshape(2, tok_rows, width_part)
        placed = jnp.dot(onehot.T, var_rows, preferred_element_type=f32)
        variant = jnp.where(changed[:, None], placed, hidden.astype(f32))
        seqs = jnp.stack([hidden.astype(f32), variant])
        return (seqs + branch).astype(bf16)


def solution(mesh):
    fine = Mesh(mesh.devices.reshape(X_HI, Z, CORE, X_LO, Y), (*FSDP, *CTX))
    in_specs = (
        P(CTX, FSDP),
        P(),
        P(None, FSDP),
        P(FSDP, None),
        P(FSDP, None),
        P(CTX),
        P(CTX),
        P(CTX),
    )
    out_specs = P(None, CTX, FSDP)
    return jax.shard_map(shards, mesh=fine, in_specs=in_specs, out_specs=out_specs, check_vma=False)
```

```python
import functools

import jax
import jax.numpy as jnp
from jax import lax
from jax.experimental import pallas as pl
from jax.experimental.pallas import tpu as pltpu
from jax.sharding import Mesh, PartitionSpec as P

epsilon = 1e-05
rope_base = 10000.0

X_HI, Z, CORE, X_LO, Y = 2, 8, 2, 2, 4
FSDP = ("x_hi", "z", "core")
CTX = ("x_lo", "y")
BLOCKS = X_LO * Y
HD = 128
QKV = 3 * HD
TOK = 256
VAR = 16
ROWS = TOK + VAR
SUM_ROWS = ROWS + 16
PAY = ROWS + VAR
bf16 = jnp.bfloat16
f32 = jnp.float32
MIB = 1024 * 1024


def shift(value, axis, size, distance):
    return lax.ppermute(value, axis, [(i, (i + distance) % size) for i in range(size)])


def vmem():
    return pl.BlockSpec(memory_space=pltpu.VMEM)


def anywhere():
    return pl.BlockSpec(memory_space=pl.ANY)


def hbm():
    return pl.BlockSpec(memory_space=pltpu.HBM)


def limit(mib):
    return pltpu.CompilerParams(vmem_limit_bytes=mib * MIB)


FIRST = (3, 4, 5)
SECOND = (6, 7, 0, 1, 2)


def variant_kernel(pos, base, ids, hidden, embed, rows, onehot, variant):
    first = (lax.axis_index("x_lo") * Y + lax.axis_index("y")) * TOK
    vocab = embed.shape[0]
    spot = lax.broadcasted_iota(jnp.int32, (VAR, TOK), 0)
    lane = lax.broadcasted_iota(jnp.int32, (VAR, TOK), 1)
    word_spot = lax.broadcasted_iota(jnp.int32, (VAR, vocab), 0)
    word = lax.broadcasted_iota(jnp.int32, (VAR, vocab), 1)
    places = jnp.zeros((VAR, TOK), f32)
    words = jnp.zeros((VAR, vocab), f32)
    for j in range(VAR):
        place = pos[j] - first
        places = jnp.where((spot == j) & (lane == place), 1.0, places)
        new = jnp.where(word == base[j], 1.0, 0.0)
        old = jnp.where(word == ids[place], 1.0, 0.0)
        words = jnp.where(word_spot == j, new - old, words)
    places = places.astype(bf16)
    change = jnp.dot(words.astype(bf16), embed[...], preferred_element_type=f32)
    picked = jnp.dot(places, hidden[...], preferred_element_type=f32)
    changed_rows = (picked + change).astype(bf16)
    rows[:TOK] = hidden[...]
    rows[TOK:] = changed_rows
    onehot[...] = places
    contract = (((0,), (0,)), ((), ()))
    placed = lax.dot_general(places, changed_rows, contract, preferred_element_type=f32)
    ones = jnp.ones((VAR, hidden.shape[1]), bf16)
    changed = lax.dot_general(places, ones, contract, preferred_element_type=f32)
    variant[...] = jnp.where(changed > 0.5, placed, hidden[...].astype(f32)).astype(bf16)


def make_variant(pos, base, ids, hidden, embed):
    width = hidden.shape[1]
    smem = pl.BlockSpec(memory_space=pltpu.SMEM)
    return pl.pallas_call(
        variant_kernel,
        out_shape=(
            jax.ShapeDtypeStruct((ROWS, width), bf16),
            jax.ShapeDtypeStruct((VAR, TOK), bf16),
            jax.ShapeDtypeStruct((TOK, width), bf16),
        ),
        in_specs=[smem, smem, smem, vmem(), vmem()],
        out_specs=(vmem(),) * 3,
        compiler_params=limit(4),
    )(pos, base, ids, hidden, embed)


def column_copies(ks, w, send, own, sems):
    z, core, x_hi = lax.axis_index("z"), lax.axis_index("core"), lax.axis_index("x_hi")
    copies = []
    for index, (whose, out) in enumerate(((1 - core, send), (core, own))):
        for i, k in enumerate(ks):
            for xr in range(X_HI):
                head_pair = lax.rem(x_hi + xr, X_HI) * Z + lax.rem(z + k, Z)
                slot = i * X_HI + xr
                start = pl.multiple_of((head_pair * 2 + whose) * QKV, HD)
                copies.append(
                    pltpu.make_async_copy(
                        w.at[:, pl.ds(start, QKV)],
                        out.at[:, slot * QKV : (slot + 1) * QKV],
                        sems.at[index, slot],
                    )
                )
    return copies


def first_columns_kernel(w, send, own, sems):
    copies = column_copies(FIRST, w, send, own, sems)
    for copy in copies:
        copy.start()
    for copy in copies:
        copy.wait()


def first_columns(w):
    columns = jax.ShapeDtypeStruct((w.shape[0], len(FIRST) * X_HI * QKV), bf16)
    return pl.pallas_call(
        first_columns_kernel,
        out_shape=(columns, columns),
        in_specs=[hbm()],
        out_specs=(vmem(), vmem()),
        scratch_shapes=[pltpu.SemaphoreType.DMA((2, len(FIRST) * X_HI))],
        compiler_params=limit(8),
    )(pltpu.with_memory_space_constraint(w, pltpu.HBM))


def second_columns_kernel(w, out_weight, send, own, share, buffer, sems, share_sems, out_sem):
    my_block = lax.axis_index("x_lo") * Y + lax.axis_index("y")
    size, width = buffer.shape[1], buffer.shape[2] // X_HI
    share_copies = []
    for k in range(Z):
        for x in range(X_HI):
            start = (x * Z + k) * width
            share_copies.append(
                pltpu.make_async_copy(
                    out_weight.at[
                        pl.ds(pl.multiple_of(my_block * size, size), size), start : start + width
                    ],
                    buffer.at[k, :, x * width : (x + 1) * width],
                    share_sems.at[k, x],
                )
            )
    copies = column_copies(SECOND, w, send, own, sems)
    for copy in share_copies + copies:
        copy.start()
    for copy in share_copies:
        copy.wait()
    out_copy = pltpu.make_async_copy(buffer, share, out_sem)
    out_copy.start()
    for copy in copies:
        copy.wait()
    out_copy.wait()


def second_columns(w, out_weight):
    columns = jax.ShapeDtypeStruct((w.shape[0], len(SECOND) * X_HI * QKV), bf16)
    shape = (Z, out_weight.shape[0] // BLOCKS, out_weight.shape[1] // Z)
    return pl.pallas_call(
        second_columns_kernel,
        out_shape=(columns, columns, jax.ShapeDtypeStruct(shape, bf16)),
        in_specs=[hbm(), hbm()],
        out_specs=(vmem(), vmem(), hbm()),
        scratch_shapes=[
            pltpu.VMEM(shape, bf16),
            pltpu.SemaphoreType.DMA((2, len(SECOND) * X_HI)),
            pltpu.SemaphoreType.DMA((Z, X_HI)),
            pltpu.SemaphoreType.DMA(()),
        ],
        compiler_params=limit(12),
    )(
        pltpu.with_memory_space_constraint(w, pltpu.HBM),
        pltpu.with_memory_space_constraint(out_weight, pltpu.HBM),
    )


def two_rows(row, width):
    high = row.astype(bf16)
    low = (row - high.astype(f32)).astype(bf16)
    line = lax.broadcasted_iota(jnp.int32, (16, width), 0)
    both = jnp.where(line == 0, high.astype(f32), jnp.where(line == 1, low.astype(f32), 0.0))
    return both.astype(bf16)


def one_row(rows):
    return jnp.sum(rows.astype(f32), axis=0, keepdims=True)


def partial_kernel(ks, own, sis, gains, w_own, w_sis, *outs):
    width = X_HI * QKV
    core = lax.axis_index("core")
    own_rows, sis_rows = own[...].astype(f32), sis[...].astype(f32)
    left, right = gains[:, :TOK].astype(f32), gains[:, TOK:].astype(f32)
    x_own = (own_rows * jnp.where(core == 0, left, right)).astype(bf16)
    x_sis = (sis_rows * jnp.where(core == 0, right, left)).astype(bf16)
    squares = jnp.sum(own_rows * own_rows + sis_rows * sis_rows, axis=1, keepdims=True)
    line = lax.broadcasted_iota(jnp.int32, (ROWS, QKV), 0)
    lane = lax.broadcasted_iota(jnp.int32, (ROWS, QKV), 1)
    row = jnp.sum(jnp.where(line == lane, squares, 0.0), axis=0, keepdims=True)
    tail = two_rows(row, QKV)

    def product(slot, count):
        cols = slice(slot * QKV, (slot + count) * QKV)
        acc = jnp.dot(x_own, w_own[:, cols], preferred_element_type=f32)
        acc = acc + jnp.dot(x_sis, w_sis[:, cols], preferred_element_type=f32)
        return acc.astype(bf16)

    outs = list(outs)
    for i, k in enumerate(ks):
        if k == Z // 2:
            for xr in range(X_HI):
                out = outs.pop(0)
                out[:ROWS, :] = product(i * X_HI + xr, 1)
                out[ROWS:, :] = tail
        else:
            out = outs.pop(0)
            out[:ROWS, :] = product(i * X_HI, X_HI)
            out[ROWS:, :QKV] = tail
            out[ROWS:, QKV:] = tail


def partials(ks, own, sis, gains, w_own, w_sis):
    half = jax.ShapeDtypeStruct((SUM_ROWS, QKV), bf16)
    full = jax.ShapeDtypeStruct((SUM_ROWS, X_HI * QKV), bf16)
    shapes = []
    for k in ks:
        shapes += [half, half] if k == Z // 2 else [full]
    return pl.pallas_call(
        functools.partial(partial_kernel, ks),
        out_shape=tuple(shapes),
        in_specs=[vmem()] * 5,
        out_specs=(vmem(),) * len(shapes),
        compiler_params=limit(20),
        cost_estimate=pl.CostEstimate(
            flops=4 * ROWS * w_own.size, bytes_accessed=8 * w_own.size, transcendentals=0
        ),
    )(own, sis, gains, w_own, w_sis)


def store_sum(out, cols, terms):
    body = sum(term[:ROWS].astype(f32) for term in terms)
    row = sum(one_row(term[ROWS:]) for term in terms)
    out[:ROWS, cols] = body.astype(bf16)
    out[ROWS:, cols] = two_rows(row, row.shape[1])


def first_kernel(up, down, near_up, near_down, out_up, out_down):
    left, right = slice(0, QKV), slice(QKV, 2 * QKV)
    store_sum(out_up, left, [up[...], near_up[:, left]])
    out_up[:, right] = near_up[:, right]
    out_down[:, left] = near_down[:, left]
    store_sum(out_down, right, [down[...], near_down[:, right]])


def next_kernel(up, down, near_up, near_down, out_up, out_down):
    every = slice(0, 2 * QKV)
    store_sum(out_up, every, [up[...], near_up[...]])
    store_sum(out_down, every, [down[...], near_down[...]])


def ring_add(kernel, up, down, near_up, near_down):
    out = jax.ShapeDtypeStruct((SUM_ROWS, X_HI * QKV), bf16)
    return pl.pallas_call(
        kernel,
        out_shape=(out, out),
        in_specs=[vmem()] * 4,
        out_specs=(vmem(), vmem()),
        compiler_params=limit(8),
    )(up, down, near_up, near_down)


def last_kernel(up, down, near, mine, other):
    own, far = slice(0, QKV), slice(QKV, 2 * QKV)
    terms = [up, down, near]
    mine[:ROWS] = sum(term[:ROWS, own].astype(f32) for term in terms)
    row = sum(one_row(term[ROWS:, own]) for term in terms)
    mine[ROWS:] = jnp.broadcast_to(row, (8, QKV))
    store_sum(other, slice(0, QKV), [term[:, far] for term in terms])


def ring_last(up, down, near):
    return pl.pallas_call(
        last_kernel,
        out_shape=(
            jax.ShapeDtypeStruct((ROWS + 8, QKV), f32),
            jax.ShapeDtypeStruct((SUM_ROWS, QKV), bf16),
        ),
        in_specs=[vmem()] * 3,
        out_specs=(vmem(), vmem()),
        compiler_params=limit(8),
    )(up, down, near)


def rotated(x, cosine, sine):
    return x * cosine + pltpu.roll(x, HD // 2, 1) * sine


def finish_kernel(full_width, mine, other, cosine, sine, onehot, payload, queries):
    row = mine[ROWS : ROWS + 1, :] + one_row(other[ROWS:, :])
    line = lax.broadcasted_iota(jnp.int32, (ROWS, QKV), 0)
    lane = lax.broadcasted_iota(jnp.int32, (ROWS, QKV), 1)
    squares = jnp.sum(jnp.where(line == lane, row, 0.0), axis=1, keepdims=True)
    inv_rms = lax.rsqrt(squares / full_width + epsilon)
    proj = (mine[:ROWS, :] + other[:ROWS, :].astype(f32)) * inv_rms
    query = rotated(proj[:, :HD], cosine[...], sine[...]).astype(bf16)
    key = rotated(proj[:, HD : 2 * HD], cosine[...], sine[...]).astype(bf16)
    value = proj[:, 2 * HD :].astype(bf16)
    spots = onehot[...]

    def step(b, carry):
        payload[b, :ROWS, :HD] = key
        payload[b, :ROWS, HD:] = value
        payload[b, ROWS:, :] = spots
        return carry

    lax.fori_loop(0, BLOCKS, step, 0)
    contract = (((0,), (0,)), ((), ()))
    ones = jnp.ones((VAR, HD), bf16)
    changed = lax.dot_general(spots, ones, contract, preferred_element_type=f32)
    placed = lax.dot_general(spots, query[TOK:], contract, preferred_element_type=f32)
    base = query[:TOK]
    queries[:TOK] = base
    queries[TOK:] = jnp.where(changed > 0.5, placed, base.astype(f32)).astype(bf16)


def finish(full_width, mine, other, cosine, sine, onehot):
    return pl.pallas_call(
        functools.partial(finish_kernel, full_width),
        out_shape=(
            jax.ShapeDtypeStruct((BLOCKS, PAY, 2 * HD), bf16),
            jax.ShapeDtypeStruct((2 * TOK, HD), bf16),
        ),
        in_specs=[vmem()] * 5,
        out_specs=(vmem(), vmem()),
        compiler_params=limit(12),
    )(mine, other, cosine, sine, onehot)


def attend_kernel(queries, blocks, out, scores, peak, denom, total, var_kv, spots):
    my_block = lax.axis_index("x_lo") * Y + lax.axis_index("y")
    scale = 1.0 / HD**0.5
    by_cols = (((1,), (1,)), ((), ()))
    lowest = -jnp.inf
    query = queries[...]

    def score_block(j, own):
        score = lax.dot_general(
            query, blocks[j, :TOK, :HD], by_cols, preferred_element_type=f32
        ) * scale
        gone = jnp.sum(blocks[j, ROWS:, :].astype(f32), axis=0, keepdims=True) > 0.5
        line = lax.broadcasted_iota(jnp.int32, (2 * TOK, TOK), 0)
        hidden = (line >= TOK) & gone
        if own:
            lane = lax.broadcasted_iota(jnp.int32, (2 * TOK, TOK), 1)
            hidden = hidden | (lax.rem(line, TOK) < lane)
        return jnp.where(hidden, lowest, score)

    score = score_block(my_block, True)
    scores[my_block] = score
    peak[...] = jnp.maximum(score[:, :HD], score[:, HD:])

    def first(j, carry):
        score = score_block(j, False)
        scores[j] = score
        peak[...] = jnp.maximum(peak[...], jnp.maximum(score[:, :HD], score[:, HD:]))
        return carry

    lax.fori_loop(0, my_block, first, 0)

    for j in range(BLOCKS):
        var_kv[j * VAR : (j + 1) * VAR, :] = blocks[j, TOK:ROWS, :]
        spots[j * VAR : (j + 1) * VAR, :] = blocks[j, ROWS:, :]
    row = lax.broadcasted_iota(jnp.int32, (TOK, TOK), 0)
    col = lax.broadcasted_iota(jnp.int32, (TOK, TOK), 1)
    reached = lax.dot_general(
        jnp.where(row >= col, 1.0, 0.0).astype(bf16), spots[...], by_cols, preferred_element_type=f32
    )
    source = lax.broadcasted_iota(jnp.int32, (TOK, BLOCKS * VAR), 1) // VAR
    seen = (source < my_block) | ((source == my_block) & (reached > 0.5))
    more = lax.dot_general(
        query[TOK:], var_kv[:, :HD], by_cols, preferred_element_type=f32
    ) * scale
    more = jnp.where(seen, more, lowest)
    peak[TOK:, :] = jnp.maximum(peak[TOK:, :], more)
    top = jnp.max(peak[...], axis=1, keepdims=True)
    peak[...] = jnp.broadcast_to(top, (2 * TOK, HD))

    more = jnp.exp(more - top[TOK:])
    denom[:TOK, :] = jnp.zeros((TOK, HD), f32)
    denom[TOK:, :] = more
    total[:TOK, :] = jnp.zeros((TOK, HD), f32)
    total[TOK:, :] = jnp.dot(more.astype(bf16), var_kv[:, HD:], preferred_element_type=f32)

    def second(j, carry):
        best = peak[...]
        left = jnp.exp(scores[j, :, :HD] - best)
        right = jnp.exp(scores[j, :, HD:] - best)
        denom[...] = denom[...] + left + right
        probs = jnp.concatenate([left.astype(bf16), right.astype(bf16)], axis=1)
        total[...] = total[...] + jnp.dot(
            probs, blocks[j, :TOK, HD:], preferred_element_type=f32
        )
        return carry

    lax.fori_loop(0, my_block + 1, second, 0)
    out[...] = (total[...] / jnp.sum(denom[...], axis=1, keepdims=True)).astype(bf16)


def attend(queries, blocks):
    return pl.pallas_call(
        attend_kernel,
        out_shape=jax.ShapeDtypeStruct((2 * TOK, HD), bf16),
        in_specs=[vmem(), vmem()],
        out_specs=vmem(),
        scratch_shapes=[
            pltpu.VMEM((BLOCKS, 2 * TOK, TOK), f32),
            pltpu.VMEM((2 * TOK, HD), f32),
            pltpu.VMEM((2 * TOK, HD), f32),
            pltpu.VMEM((2 * TOK, HD), f32),
            pltpu.VMEM((BLOCKS * VAR, 2 * HD), bf16),
            pltpu.VMEM((BLOCKS * VAR, TOK), bf16),
        ],
        compiler_params=limit(16),
    )(queries, blocks)


def project_kernel(w, *refs):
    shards, (keep, near, far), (joined, turned) = refs[:Z], refs[Z : Z + 3], refs[Z + 3 :]
    z, core, x_hi = lax.axis_index("z"), lax.axis_index("core"), lax.axis_index("x_hi")
    for d in range(Z):
        joined[:, d * HD : (d + 1) * HD] = shards[d][...]
        source = lax.rem(z + Z - d, Z)
        turned[d * HD : (d + 1) * HD, :] = w[source]

    def product(xr, cr, rows):
        column = (lax.rem(x_hi + xr, X_HI) * CORE + lax.rem(core + cr, CORE)) * TOK
        column = pl.ds(pl.multiple_of(column, TOK), TOK)
        return jnp.dot(joined[rows, :], turned[:, column], preferred_element_type=f32)

    size = 128

    def step(i, carry):
        rows = pl.ds(pl.multiple_of(i * size, size), size)
        for xr in range(X_HI):
            near[rows, xr * TOK : (xr + 1) * TOK] = product(xr, 1, rows).astype(bf16)
        keep[rows, :] = product(0, 0, rows)
        far[rows, :] = product(1, 0, rows)
        return carry

    lax.fori_loop(0, 2 * TOK // size, step, 0)


def project(w, shards):
    rows = shards[0].shape[0]
    return pl.pallas_call(
        project_kernel,
        out_shape=(
            jax.ShapeDtypeStruct((rows, TOK), f32),
            jax.ShapeDtypeStruct((rows, 2 * TOK), bf16),
            jax.ShapeDtypeStruct((rows, TOK), f32),
        ),
        in_specs=[vmem()] * (1 + Z),
        out_specs=(vmem(),) * 3,
        scratch_shapes=[
            pltpu.VMEM((rows, Z * HD), bf16),
            pltpu.VMEM((Z * HD, w.shape[2]), bf16),
        ],
        compiler_params=limit(16),
    )(w, *shards)


def shards(hidden, gain, embed, qkv_weight, out_weight, ref_ids, var_pos, var_base):
    tok_rows, width_part = hidden.shape
    full_width = out_weight.shape[1]
    x_hi, z, core = lax.axis_index("x_hi"), lax.axis_index("z"), lax.axis_index("core")
    my_block = lax.axis_index("x_lo") * Y + lax.axis_index("y")
    chip_slice = x_hi * Z + z

    with jax.named_scope("inputs"):
        rows, onehot, variant = make_variant(var_pos, var_base, ref_ids, hidden, embed)
        rows, qkv_weight = lax.optimization_barrier((rows, qkv_weight))
        rows_sis = shift(rows, "core", CORE, 1)
        send_first, own_first = first_columns(qkv_weight)
        sis_first = shift(send_first, "core", CORE, 1)
        rows_sis, send_first, qkv_weight = lax.optimization_barrier((rows_sis, send_first, qkv_weight))
        send_second, own_second, share = second_columns(qkv_weight, out_weight)
        sis_second = shift(send_second, "core", CORE, 1)
        shared = lax.all_to_all(share, "z", 0, 0, tiled=True)
        start = chip_slice * 2 * width_part
        gains = lax.dynamic_slice(gain.reshape(1, full_width), (0, start), (1, 2 * width_part))

    with jax.named_scope("projection"):
        near_up, up, down, near_down = partials(FIRST, rows, rows_sis, gains, own_first, sis_first)
        up, down = shift(up, "z", Z, 1), shift(down, "z", Z, -1)
        up, down, shared = lax.optimization_barrier((up, down, shared))
        out_w = lax.all_gather(shared, CTX, axis=1, tiled=True)
        up, down = ring_add(first_kernel, up, down, near_up, near_down)
        up, rows, down = lax.optimization_barrier((up, rows, down))
        up, down = shift(up, "z", Z, 1), shift(down, "z", Z, -1)
        parts = partials(SECOND, rows, rows_sis, gains, own_second, sis_second)
        up, down, parts = lax.optimization_barrier((up, down, parts))
        parts = dict(zip(SECOND, parts))
        up, down = ring_add(next_kernel, up, down, parts[2], parts[6])
        up, down = shift(up, "z", Z, 1), shift(down, "z", Z, -1)
        up, down = ring_add(next_kernel, up, down, parts[1], parts[7])
        up, down = shift(up, "z", Z, 1), shift(down, "z", Z, -1)
        mine, other = ring_last(up, down, parts[0])
        other = shift(other, "x_hi", X_HI, 1)

    with jax.named_scope("tables"):
        positions = jnp.concatenate([my_block * tok_rows + jnp.arange(tok_rows), var_pos])
        exponent = jnp.arange(HD // 2).astype(f32) * (-2.0 / HD)
        inv_freq = jnp.power(f32(rope_base), exponent)
        angle = positions.astype(f32)[:, None] * inv_freq[None, :]
        cosine, sine = jnp.cos(angle), jnp.sin(angle)
        cosine = jnp.concatenate([cosine, cosine], axis=1)
        sine = jnp.concatenate([-sine, sine], axis=1)

    with jax.named_scope("attention"):
        payload, queries = finish(full_width, mine, other, cosine, sine, onehot)
        blocks = lax.all_to_all(payload, CTX, 0, 0, tiled=True)
        attn = attend(queries, blocks)
        attn, out_w = lax.optimization_barrier((attn, out_w))

    with jax.named_scope("output"):
        pieces = [attn] + [None] * (Z - 1)
        for d in (1, 2, 3):
            pieces[d] = shift(pieces[d - 1], "z", Z, 1)
            pieces[Z - d] = shift(pieces[(Z - d + 1) % Z], "z", Z, -1)
            if d == 1:
                pieces[Z // 2] = shift(attn, "z", Z, Z // 2)
        keep, near, far = project(out_w, pieces)
        near = shift(near, "core", CORE, 1).astype(f32)
        far = (far + near[:, width_part:]).astype(bf16)
        far = shift(far, "x_hi", X_HI, 1).astype(f32)
        branch = (keep + near[:, :width_part] + far).reshape(2, tok_rows, width_part)
        seqs = jnp.stack([hidden, variant]).astype(f32)
        return (seqs + branch).astype(bf16)


def solution(mesh):
    fine = Mesh(mesh.devices.reshape(X_HI, Z, CORE, X_LO, Y), (*FSDP, *CTX))
    in_specs = (
        P(CTX, FSDP),
        P(),
        P(None, FSDP),
        P(FSDP, None),
        P(FSDP, None),
        P(CTX),
        P(CTX),
        P(CTX),
    )
    out_specs = P(None, CTX, FSDP)
    return jax.shard_map(shards, mesh=fine, in_specs=in_specs, out_specs=out_specs, check_vma=False)
```

```python
import functools

import jax
import jax.numpy as jnp
from jax import lax
from jax.experimental import pallas as pl
from jax.experimental.pallas import tpu as pltpu
from jax.sharding import Mesh, PartitionSpec as P

epsilon = 1e-05
rope_base = 10000.0

X_HI, Z, CORE, X_LO, Y = 2, 8, 2, 2, 4
FSDP = ("x_hi", "z", "core")
CTX = ("x_lo", "y")
BLOCKS = X_LO * Y
HD = 128
QKV = 3 * HD
TOK = 256
VAR = 16
ROWS = TOK + VAR
SUM_ROWS = ROWS + 16
PAY = ROWS + VAR
bf16 = jnp.bfloat16
f32 = jnp.float32
MIB = 1024 * 1024


def shift(value, axis, size, distance):
    return lax.ppermute(value, axis, [(i, (i + distance) % size) for i in range(size)])


def shift_diagonal(value, distance):
    route = [
        (x * Z + z, (1 - x) * Z + (z + distance) % Z) for x in range(X_HI) for z in range(Z)
    ]
    return lax.ppermute(value, ("x_hi", "z"), route)


def vmem():
    return pl.BlockSpec(memory_space=pltpu.VMEM)


def anywhere():
    return pl.BlockSpec(memory_space=pl.ANY)


def hbm():
    return pl.BlockSpec(memory_space=pltpu.HBM)


def limit(mib):
    return pltpu.CompilerParams(vmem_limit_bytes=mib * MIB)


FIRST = (3, 4, 5)
SECOND = (6, 7, 0, 1, 2)


def variant_kernel(pos, base, ids, hidden, embed, rows, onehot, variant):
    first = (lax.axis_index("x_lo") * Y + lax.axis_index("y")) * TOK
    vocab = embed.shape[0]
    spot = lax.broadcasted_iota(jnp.int32, (VAR, TOK), 0)
    lane = lax.broadcasted_iota(jnp.int32, (VAR, TOK), 1)
    word_spot = lax.broadcasted_iota(jnp.int32, (VAR, vocab), 0)
    word = lax.broadcasted_iota(jnp.int32, (VAR, vocab), 1)
    places = jnp.zeros((VAR, TOK), f32)
    words = jnp.zeros((VAR, vocab), f32)
    for j in range(VAR):
        place = pos[j] - first
        places = jnp.where((spot == j) & (lane == place), 1.0, places)
        new = jnp.where(word == base[j], 1.0, 0.0)
        old = jnp.where(word == ids[place], 1.0, 0.0)
        words = jnp.where(word_spot == j, new - old, words)
    places = places.astype(bf16)
    change = jnp.dot(words.astype(bf16), embed[...], preferred_element_type=f32)
    picked = jnp.dot(places, hidden[...], preferred_element_type=f32)
    changed_rows = (picked + change).astype(bf16)
    rows[:TOK] = hidden[...]
    rows[TOK:] = changed_rows
    onehot[...] = places
    contract = (((0,), (0,)), ((), ()))
    placed = lax.dot_general(places, changed_rows, contract, preferred_element_type=f32)
    ones = jnp.ones((VAR, hidden.shape[1]), bf16)
    changed = lax.dot_general(places, ones, contract, preferred_element_type=f32)
    variant[...] = jnp.where(changed > 0.5, placed, hidden[...].astype(f32)).astype(bf16)


def make_variant(pos, base, ids, hidden, embed):
    width = hidden.shape[1]
    smem = pl.BlockSpec(memory_space=pltpu.SMEM)
    return pl.pallas_call(
        variant_kernel,
        out_shape=(
            jax.ShapeDtypeStruct((ROWS, width), bf16),
            jax.ShapeDtypeStruct((VAR, TOK), bf16),
            jax.ShapeDtypeStruct((TOK, width), bf16),
        ),
        in_specs=[smem, smem, smem, vmem(), vmem()],
        out_specs=(vmem(),) * 3,
        compiler_params=limit(4),
    )(*(pltpu.with_memory_space_constraint(v, pltpu.HBM) for v in (pos, base, ids, hidden, embed)))


def column_copies(ks, w, send, own, sems):
    z, core, x_hi = lax.axis_index("z"), lax.axis_index("core"), lax.axis_index("x_hi")
    copies = []
    for index, (whose, out) in enumerate(((1 - core, send), (core, own))):
        for i, k in enumerate(ks):
            for xr in range(X_HI):
                head_pair = lax.rem(x_hi + xr, X_HI) * Z + lax.rem(z + k, Z)
                slot = i * X_HI + xr
                start = pl.multiple_of((head_pair * 2 + whose) * QKV, HD)
                copies.append(
                    pltpu.make_async_copy(
                        w.at[:, pl.ds(start, QKV)],
                        out.at[:, slot * QKV : (slot + 1) * QKV],
                        sems.at[index, slot],
                    )
                )
    return copies


def columns_kernel(ks, w, send, own, sems):
    copies = column_copies(ks, w, send, own, sems)
    for copy in copies:
        copy.start()
    for copy in copies:
        copy.wait()


def pick_columns(ks, w):
    columns = jax.ShapeDtypeStruct((w.shape[0], len(ks) * X_HI * QKV), bf16)
    return pl.pallas_call(
        functools.partial(columns_kernel, ks),
        out_shape=(columns, columns),
        in_specs=[hbm()],
        out_specs=(vmem(), vmem()),
        scratch_shapes=[pltpu.SemaphoreType.DMA((2, len(ks) * X_HI))],
        compiler_params=limit(8),
    )(pltpu.with_memory_space_constraint(w, pltpu.HBM))


def share_kernel(w, out, buffer, sems, out_sem):
    my_block = lax.axis_index("x_lo") * Y + lax.axis_index("y")
    size, width = buffer.shape[1], buffer.shape[2] // X_HI
    rows = pl.ds(pl.multiple_of(my_block * size, size), size)
    copies = []
    for k in range(Z):
        for x in range(X_HI):
            start = (x * Z + k) * width
            copies.append(
                pltpu.make_async_copy(
                    w.at[rows, start : start + width],
                    buffer.at[k, :, x * width : (x + 1) * width],
                    sems.at[k, x],
                )
            )
    for copy in copies:
        copy.start()
    for copy in copies:
        copy.wait()
    copy = pltpu.make_async_copy(buffer, out, out_sem)
    copy.start()
    copy.wait()


def share_rows(w):
    shape = (Z, w.shape[0] // BLOCKS, w.shape[1] // Z)
    return pl.pallas_call(
        share_kernel,
        out_shape=jax.ShapeDtypeStruct(shape, bf16),
        in_specs=[hbm()],
        out_specs=hbm(),
        scratch_shapes=[
            pltpu.VMEM(shape, bf16),
            pltpu.SemaphoreType.DMA((Z, X_HI)),
            pltpu.SemaphoreType.DMA(()),
        ],
        compiler_params=limit(4),
    )(pltpu.with_memory_space_constraint(w, pltpu.HBM))


def two_rows(row, width):
    high = row.astype(bf16)
    low = (row - high.astype(f32)).astype(bf16)
    line = lax.broadcasted_iota(jnp.int32, (16, width), 0)
    both = jnp.where(line == 0, high.astype(f32), jnp.where(line == 1, low.astype(f32), 0.0))
    return both.astype(bf16)


def one_row(rows):
    return jnp.sum(rows.astype(f32), axis=0, keepdims=True)


def partial_products(own, sis, gains, w_own, w_sis):
    core = lax.axis_index("core")
    own_rows, sis_rows = own[...].astype(f32), sis[...].astype(f32)
    left, right = gains[:, :TOK].astype(f32), gains[:, TOK:].astype(f32)
    x_own = (own_rows * jnp.where(core == 0, left, right)).astype(bf16)
    x_sis = (sis_rows * jnp.where(core == 0, right, left)).astype(bf16)
    squares = jnp.sum(own_rows * own_rows + sis_rows * sis_rows, axis=1, keepdims=True)
    line = lax.broadcasted_iota(jnp.int32, (ROWS, QKV), 0)
    lane = lax.broadcasted_iota(jnp.int32, (ROWS, QKV), 1)
    row = jnp.sum(jnp.where(line == lane, squares, 0.0), axis=0, keepdims=True)
    tail = two_rows(row, QKV)

    def product(slot, out):
        cols = slice(slot * QKV, (slot + 1) * QKV)
        acc = jnp.dot(x_own, w_own[:, cols], preferred_element_type=f32)
        acc = acc + jnp.dot(x_sis, w_sis[:, cols], preferred_element_type=f32)
        out[:ROWS, :] = acc.astype(bf16)
        out[ROWS:, :] = tail

    return product


def first_partial_kernel(own, sis, gains, w_own, w_sis, up, down, near, near_far):
    product = partial_products(own, sis, gains, w_own, w_sis)
    slot = FIRST.index(4) * X_HI
    product(slot, up)
    product(slot + 1, down)
    for i, k in enumerate((3, 5)):
        slot = FIRST.index(k) * X_HI
        product(slot, near.at[i])
        product(slot + 1, near_far.at[i])


def second_partial_kernel(own, sis, gains, w_own, w_sis, mid, mid_far, last, last_far):
    product = partial_products(own, sis, gains, w_own, w_sis)
    for ks, out, out_far in (((2, 6), mid, mid_far), ((1, 7, 0), last, last_far)):
        for i, k in enumerate(ks):
            slot = SECOND.index(k) * X_HI
            product(slot, out.at[i])
            product(slot + 1, out_far.at[i])


def partials(kernel, counts, own, sis, gains, w_own, w_sis):
    part = (SUM_ROWS, QKV)
    shapes = [jax.ShapeDtypeStruct((n, *part) if n else part, bf16) for n in counts]
    return pl.pallas_call(
        kernel,
        out_shape=tuple(shapes),
        in_specs=[vmem()] * 5,
        out_specs=(vmem(),) * len(shapes),
        compiler_params=limit(20),
        cost_estimate=pl.CostEstimate(
            flops=4 * ROWS * w_own.size, bytes_accessed=8 * w_own.size, transcendentals=0
        ),
    )(own, sis, gains, w_own, w_sis)


def add_kernel(up, down, near, far, out_up, out_down):
    for i, (term, out) in enumerate(((up, out_up), (down, out_down))):
        terms = (term, near.at[i], far.at[i])
        body = sum(t[:ROWS].astype(f32) for t in terms)
        row = sum(one_row(t[ROWS:]) for t in terms)
        out[:ROWS] = body.astype(bf16)
        out[ROWS:] = two_rows(row, QKV)


def ring_add(up, down, near, far):
    out = jax.ShapeDtypeStruct((SUM_ROWS, QKV), bf16)
    return pl.pallas_call(
        add_kernel,
        out_shape=(out, out),
        in_specs=[vmem()] * 4,
        out_specs=(vmem(), vmem()),
        compiler_params=limit(8),
    )(up, down, near, far)


def rotated(x, cosine, sine):
    return x * cosine + pltpu.roll(x, HD // 2, 1) * sine


def finish_kernel(full_width, up, down, near, far, cosine, sine, onehot, payload, queries):
    terms = (up, down, near.at[2], far.at[2])
    row = sum(one_row(t[ROWS:]) for t in terms)
    line = lax.broadcasted_iota(jnp.int32, (ROWS, QKV), 0)
    lane = lax.broadcasted_iota(jnp.int32, (ROWS, QKV), 1)
    squares = jnp.sum(jnp.where(line == lane, row, 0.0), axis=1, keepdims=True)
    inv_rms = lax.rsqrt(squares / full_width + epsilon)
    proj = sum(t[:ROWS].astype(f32) for t in terms) * inv_rms
    query = rotated(proj[:, :HD], cosine[...], sine[...]).astype(bf16)
    key = rotated(proj[:, HD : 2 * HD], cosine[...], sine[...]).astype(bf16)
    value = proj[:, 2 * HD :].astype(bf16)
    spots = onehot[...]

    def step(b, carry):
        payload[b, :ROWS, :HD] = key
        payload[b, :ROWS, HD:] = value
        payload[b, ROWS:, :] = spots
        return carry

    lax.fori_loop(0, BLOCKS, step, 0)
    contract = (((0,), (0,)), ((), ()))
    ones = jnp.ones((VAR, HD), bf16)
    changed = lax.dot_general(spots, ones, contract, preferred_element_type=f32)
    placed = lax.dot_general(spots, query[TOK:], contract, preferred_element_type=f32)
    base = query[:TOK]
    queries[:TOK] = base
    queries[TOK:] = jnp.where(changed > 0.5, placed, base.astype(f32)).astype(bf16)


def finish(full_width, up, down, near, far, cosine, sine, onehot):
    return pl.pallas_call(
        functools.partial(finish_kernel, full_width),
        out_shape=(
            jax.ShapeDtypeStruct((BLOCKS, PAY, 2 * HD), bf16),
            jax.ShapeDtypeStruct((2 * TOK, HD), bf16),
        ),
        in_specs=[vmem()] * 7,
        out_specs=(vmem(), vmem()),
        compiler_params=limit(12),
    )(up, down, near, far, cosine, sine, onehot)


def attend_kernel(queries, blocks, out, scores, peak, denom, total, var_kv, spots):
    my_block = lax.axis_index("x_lo") * Y + lax.axis_index("y")
    scale = 1.0 / HD**0.5
    by_cols = (((1,), (1,)), ((), ()))
    lowest = -jnp.inf
    query = queries[...]

    def score_block(j, own):
        score = lax.dot_general(
            query, blocks[j, :TOK, :HD], by_cols, preferred_element_type=f32
        ) * scale
        gone = jnp.sum(blocks[j, ROWS:, :].astype(f32), axis=0, keepdims=True) > 0.5
        line = lax.broadcasted_iota(jnp.int32, (2 * TOK, TOK), 0)
        hidden = (line >= TOK) & gone
        if own:
            lane = lax.broadcasted_iota(jnp.int32, (2 * TOK, TOK), 1)
            hidden = hidden | (lax.rem(line, TOK) < lane)
        return jnp.where(hidden, lowest, score)

    score = score_block(my_block, True)
    scores[my_block] = score
    peak[...] = jnp.maximum(score[:, :HD], score[:, HD:])

    def first(j, carry):
        score = score_block(j, False)
        scores[j] = score
        peak[...] = jnp.maximum(peak[...], jnp.maximum(score[:, :HD], score[:, HD:]))
        return carry

    lax.fori_loop(0, my_block, first, 0)

    for j in range(BLOCKS):
        var_kv[j * VAR : (j + 1) * VAR, :] = blocks[j, TOK:ROWS, :]
        spots[j * VAR : (j + 1) * VAR, :] = blocks[j, ROWS:, :]
    row = lax.broadcasted_iota(jnp.int32, (TOK, TOK), 0)
    col = lax.broadcasted_iota(jnp.int32, (TOK, TOK), 1)
    reached = lax.dot_general(
        jnp.where(row >= col, 1.0, 0.0).astype(bf16), spots[...], by_cols, preferred_element_type=f32
    )
    source = lax.broadcasted_iota(jnp.int32, (TOK, BLOCKS * VAR), 1) // VAR
    seen = (source < my_block) | ((source == my_block) & (reached > 0.5))
    more = lax.dot_general(
        query[TOK:], var_kv[:, :HD], by_cols, preferred_element_type=f32
    ) * scale
    more = jnp.where(seen, more, lowest)
    peak[TOK:, :] = jnp.maximum(peak[TOK:, :], more)
    top = jnp.max(peak[...], axis=1, keepdims=True)
    peak[...] = jnp.broadcast_to(top, (2 * TOK, HD))

    more = jnp.exp(more - top[TOK:])
    denom[:TOK, :] = jnp.zeros((TOK, HD), f32)
    denom[TOK:, :] = more
    total[:TOK, :] = jnp.zeros((TOK, HD), f32)
    total[TOK:, :] = jnp.dot(more.astype(bf16), var_kv[:, HD:], preferred_element_type=f32)

    def second(j, carry):
        best = peak[...]
        left = jnp.exp(scores[j, :, :HD] - best)
        right = jnp.exp(scores[j, :, HD:] - best)
        denom[...] = denom[...] + left + right
        probs = jnp.concatenate([left.astype(bf16), right.astype(bf16)], axis=1)
        total[...] = total[...] + jnp.dot(
            probs, blocks[j, :TOK, HD:], preferred_element_type=f32
        )
        return carry

    lax.fori_loop(0, my_block + 1, second, 0)
    out[...] = (total[...] / jnp.sum(denom[...], axis=1, keepdims=True)).astype(bf16)


def attend(queries, blocks):
    return pl.pallas_call(
        attend_kernel,
        out_shape=jax.ShapeDtypeStruct((2 * TOK, HD), bf16),
        in_specs=[vmem(), vmem()],
        out_specs=vmem(),
        scratch_shapes=[
            pltpu.VMEM((BLOCKS, 2 * TOK, TOK), f32),
            pltpu.VMEM((2 * TOK, HD), f32),
            pltpu.VMEM((2 * TOK, HD), f32),
            pltpu.VMEM((2 * TOK, HD), f32),
            pltpu.VMEM((BLOCKS * VAR, 2 * HD), bf16),
            pltpu.VMEM((BLOCKS * VAR, TOK), bf16),
        ],
        compiler_params=limit(16),
    )(queries, blocks)


def arrange_kernel(w, out, sems):
    z = lax.axis_index("z")
    copies = []
    for d in range(Z):
        source = lax.rem(z + Z - d, Z)
        copies.append(
            pltpu.make_async_copy(w.at[source], out.at[d * HD : (d + 1) * HD, :], sems.at[d])
        )
    for copy in copies:
        copy.start()
    for copy in copies:
        copy.wait()


def arrange(w):
    return pl.pallas_call(
        arrange_kernel,
        out_shape=jax.ShapeDtypeStruct((Z * HD, w.shape[2]), bf16),
        in_specs=[hbm()],
        out_specs=vmem(),
        scratch_shapes=[pltpu.SemaphoreType.DMA((Z,))],
        compiler_params=limit(4),
    )(pltpu.with_memory_space_constraint(w, pltpu.HBM))


def project_kernel(turned, *refs):
    shards, (keep, near, far), joined = refs[:Z], refs[Z : Z + 3], refs[-1]
    core, x_hi = lax.axis_index("core"), lax.axis_index("x_hi")
    for d in range(Z):
        joined[:, d * HD : (d + 1) * HD] = shards[d][...]

    def product(xr, cr, rows):
        column = (lax.rem(x_hi + xr, X_HI) * CORE + lax.rem(core + cr, CORE)) * TOK
        column = pl.ds(pl.multiple_of(column, TOK), TOK)
        return jnp.dot(joined[rows, :], turned[:, column], preferred_element_type=f32)

    size = 128

    def step(i, carry):
        rows = pl.ds(pl.multiple_of(i * size, size), size)
        for xr in range(X_HI):
            near[rows, xr * TOK : (xr + 1) * TOK] = product(xr, 1, rows).astype(bf16)
        keep[rows, :] = product(0, 0, rows)
        far[rows, :] = product(1, 0, rows)
        return carry

    lax.fori_loop(0, 2 * TOK // size, step, 0)


def project(w, shards):
    rows = shards[0].shape[0]
    return pl.pallas_call(
        project_kernel,
        out_shape=(
            jax.ShapeDtypeStruct((rows, TOK), f32),
            jax.ShapeDtypeStruct((rows, 2 * TOK), bf16),
            jax.ShapeDtypeStruct((rows, TOK), f32),
        ),
        in_specs=[vmem()] * (1 + Z),
        out_specs=(vmem(),) * 3,
        scratch_shapes=[pltpu.VMEM((rows, Z * HD), bf16)],
        compiler_params=limit(16),
    )(w, *shards)


def shards(hidden, gain, embed, qkv_weight, out_weight, ref_ids, var_pos, var_base):
    tok_rows, width_part = hidden.shape
    full_width = out_weight.shape[1]
    x_hi, z, core = lax.axis_index("x_hi"), lax.axis_index("z"), lax.axis_index("core")
    my_block = lax.axis_index("x_lo") * Y + lax.axis_index("y")
    chip_slice = x_hi * Z + z

    with jax.named_scope("inputs"):
        rows, onehot, variant = make_variant(var_pos, var_base, ref_ids, hidden, embed)
        rows, qkv_weight = lax.optimization_barrier((rows, qkv_weight))
        rows_sis = shift(rows, "core", CORE, 1)
        send_first, own_first = pick_columns(FIRST, qkv_weight)
        sis_first = shift(send_first, "core", CORE, 1)
        own_first, out_weight = lax.optimization_barrier((own_first, out_weight))
        share = share_rows(out_weight)
        shared = lax.all_to_all(share, "z", 0, 0, tiled=True)
        rows_sis, sis_first, shared, qkv_weight = lax.optimization_barrier(
            (rows_sis, sis_first, shared, qkv_weight)
        )
        out_w = lax.all_gather(shared, CTX, axis=1, tiled=True)
        send_second, own_second = pick_columns(SECOND, qkv_weight)
        own_first, own_second = lax.optimization_barrier((own_first, own_second))
        sis_second = shift(send_second, "core", CORE, 1)
        start = chip_slice * 2 * width_part
        gains = lax.dynamic_slice(gain.reshape(1, full_width), (0, start), (1, 2 * width_part))

    with jax.named_scope("projection"):
        up, down, near, near_far = partials(
            first_partial_kernel, (0, 0, 2, 2), rows, rows_sis, gains, own_first, sis_first
        )
        up = shift(up, "z", Z, 1)
        down = shift_diagonal(down, -1)
        near_far = shift(near_far, "x_hi", X_HI, 1)
        mid, mid_far, last, last_far = partials(
            second_partial_kernel, (2, 2, 3, 3), rows, rows_sis, gains, own_second, sis_second
        )
        mid_far = shift(mid_far, "x_hi", X_HI, 1)
        last_far = shift(last_far, "x_hi", X_HI, 1)
        up, down, near_far, mid = lax.optimization_barrier((up, down, near_far, mid))
        up, down = ring_add(up, down, near, near_far)
        up, down = shift(up, "z", Z, 1), shift(down, "z", Z, -1)
        up, down = ring_add(up, down, mid, mid_far)
        up, down = shift(up, "z", Z, 1), shift(down, "z", Z, -1)
        up, down = ring_add(up, down, last, last_far)
        up, down = shift(up, "z", Z, 1), shift(down, "z", Z, -1)

    with jax.named_scope("tables"):
        positions = jnp.concatenate([my_block * tok_rows + jnp.arange(tok_rows), var_pos])
        exponent = jnp.arange(HD // 2).astype(f32) * (-2.0 / HD)
        inv_freq = jnp.power(f32(rope_base), exponent)
        angle = positions.astype(f32)[:, None] * inv_freq[None, :]
        cosine, sine = jnp.cos(angle), jnp.sin(angle)
        cosine = jnp.concatenate([cosine, cosine], axis=1)
        sine = jnp.concatenate([-sine, sine], axis=1)

    with jax.named_scope("attention"):
        payload, queries = finish(full_width, up, down, last, last_far, cosine, sine, onehot)
        blocks = lax.all_to_all(payload, CTX, 0, 0, tiled=True)
        attn = attend(queries, blocks)
        attn, out_w = lax.optimization_barrier((attn, out_w))

    with jax.named_scope("output"):
        pieces = [attn] + [None] * (Z - 1)
        for d in (1, 2, 3):
            pieces[d] = shift(pieces[d - 1], "z", Z, 1)
            pieces[Z - d] = shift(pieces[(Z - d + 1) % Z], "z", Z, -1)
            if d == 1:
                pieces[Z // 2] = shift(attn, "z", Z, Z // 2)
                out_w, pieces[1], pieces[7] = lax.optimization_barrier(
                    (arrange(out_w), pieces[1], pieces[7])
                )
        keep, near, far = project(out_w, pieces)
        near = shift(near, "core", CORE, 1).astype(f32)
        far = (far + near[:, width_part:]).astype(bf16)
        far = shift(far, "x_hi", X_HI, 1).astype(f32)
        branch = (keep + near[:, :width_part] + far).reshape(2, tok_rows, width_part)
        seqs = jnp.stack([hidden, variant]).astype(f32)
        return (seqs + branch).astype(bf16)


def solution(mesh):
    fine = Mesh(mesh.devices.reshape(X_HI, Z, CORE, X_LO, Y), (*FSDP, *CTX))
    in_specs = (
        P(CTX, FSDP),
        P(),
        P(None, FSDP),
        P(FSDP, None),
        P(FSDP, None),
        P(CTX),
        P(CTX),
        P(CTX),
    )
    out_specs = P(None, CTX, FSDP)
    return jax.shard_map(shards, mesh=fine, in_specs=in_specs, out_specs=out_specs, check_vma=False)
```

```python
import functools

import jax
import jax.numpy as jnp
from jax import lax
from jax.experimental import pallas as pl
from jax.experimental.pallas import tpu as pltpu
from jax.sharding import Mesh, PartitionSpec as P

epsilon = 1e-05
rope_base = 10000.0

X_HI, Z, CORE, X_LO, Y = 2, 8, 2, 2, 4
FSDP = ("x_hi", "z", "core")
CTX = ("x_lo", "y")
BLOCKS = X_LO * Y
HD = 128
QKV = 3 * HD
TOK = 256
VAR = 16
ROWS = TOK + VAR
SUM_ROWS = ROWS + 16
PAY = ROWS + VAR
bf16 = jnp.bfloat16
f32 = jnp.float32
MIB = 1024 * 1024


def shift(value, axis, size, distance):
    return lax.ppermute(value, axis, [(i, (i + distance) % size) for i in range(size)])


def vmem():
    return pl.BlockSpec(memory_space=pltpu.VMEM)


def anywhere():
    return pl.BlockSpec(memory_space=pl.ANY)


def hbm():
    return pl.BlockSpec(memory_space=pltpu.HBM)


def limit(mib):
    return pltpu.CompilerParams(vmem_limit_bytes=mib * MIB)


FIRST = (3, 4, 5)
SECOND = (6, 7, 0, 1, 2)


def variant_kernel(
    pos, base, ids, hidden, embed, rows, onehot, variant, spots, block, sems
):
    first = (lax.axis_index("x_lo") * Y + lax.axis_index("y")) * TOK
    vocab = embed.shape[0]
    spot = lax.broadcasted_iota(jnp.int32, (VAR, TOK), 0)
    lane = lax.broadcasted_iota(jnp.int32, (VAR, TOK), 1)
    word_spot = lax.broadcasted_iota(jnp.int32, (VAR, vocab), 0)
    word = lax.broadcasted_iota(jnp.int32, (VAR, vocab), 1)
    places = jnp.zeros((VAR, TOK), f32)
    words = jnp.zeros((VAR, vocab), f32)
    for j in range(VAR):
        place = pos[j] - first
        places = jnp.where((spot == j) & (lane == place), 1.0, places)
        new = jnp.where(word == base[j], 1.0, 0.0)
        old = jnp.where(word == ids[place], 1.0, 0.0)
        words = jnp.where(word_spot == j, new - old, words)
    places = places.astype(bf16)
    change = jnp.dot(words.astype(bf16), embed[...], preferred_element_type=f32)
    picked = jnp.dot(places, hidden[...], preferred_element_type=f32)
    changed_rows = (picked + change).astype(bf16)
    rows[:TOK] = hidden[...]
    rows[TOK:] = changed_rows
    spots[...] = places
    first_copy = pltpu.make_async_copy(spots, onehot, sems.at[0])
    first_copy.start()
    contract = (((0,), (0,)), ((), ()))
    placed = lax.dot_general(places, changed_rows, contract, preferred_element_type=f32)
    ones = jnp.ones((VAR, hidden.shape[1]), bf16)
    changed = lax.dot_general(places, ones, contract, preferred_element_type=f32)
    block[...] = jnp.where(changed > 0.5, placed, hidden[...].astype(f32)).astype(bf16)
    second_copy = pltpu.make_async_copy(block, variant, sems.at[1])
    second_copy.start()
    first_copy.wait()
    second_copy.wait()


def make_variant(pos, base, ids, hidden, embed):
    width = hidden.shape[1]
    smem = pl.BlockSpec(memory_space=pltpu.SMEM)
    return pl.pallas_call(
        variant_kernel,
        out_shape=(
            jax.ShapeDtypeStruct((ROWS, width), bf16),
            pltpu.HBM((VAR, TOK), bf16),
            pltpu.HBM((TOK, width), bf16),
        ),
        in_specs=[smem, smem, smem, vmem(), vmem()],
        out_specs=(vmem(), hbm(), hbm()),
        scratch_shapes=[
            pltpu.VMEM((VAR, TOK), bf16),
            pltpu.VMEM((TOK, width), bf16),
            pltpu.SemaphoreType.DMA((2,)),
        ],
        compiler_params=limit(4),
    )(*(pltpu.with_memory_space_constraint(v, pltpu.HBM) for v in (pos, base, ids, hidden, embed)))


def column_copies(ks, w, send, own, sems):
    z, core, x_hi = lax.axis_index("z"), lax.axis_index("core"), lax.axis_index("x_hi")
    copies = []
    for index, (whose, out) in enumerate(((1 - core, send), (core, own))):
        for i, k in enumerate(ks):
            for xr in range(X_HI):
                head_pair = lax.rem(x_hi + xr, X_HI) * Z + lax.rem(z + k, Z)
                slot = i * X_HI + xr
                start = pl.multiple_of((head_pair * 2 + whose) * QKV, HD)
                copies.append(
                    pltpu.make_async_copy(
                        w.at[:, pl.ds(start, QKV)],
                        out.at[:, slot * QKV : (slot + 1) * QKV],
                        sems.at[index, slot],
                    )
                )
    return copies


def first_columns_kernel(w, send, own, sems):
    copies = column_copies(FIRST, w, send, own, sems)
    for copy in copies:
        copy.start()
    for copy in copies:
        copy.wait()


def first_columns(w):
    columns = jax.ShapeDtypeStruct((w.shape[0], len(FIRST) * X_HI * QKV), bf16)
    return pl.pallas_call(
        first_columns_kernel,
        out_shape=(columns, columns),
        in_specs=[hbm()],
        out_specs=(vmem(), vmem()),
        scratch_shapes=[pltpu.SemaphoreType.DMA((2, len(FIRST) * X_HI))],
        compiler_params=limit(8),
    )(pltpu.with_memory_space_constraint(w, pltpu.HBM))


def second_columns_kernel(w, out_weight, send, own, share, buffer, sems, share_sems, out_sem):
    my_block = lax.axis_index("x_lo") * Y + lax.axis_index("y")
    size, width = buffer.shape[1], buffer.shape[2] // X_HI
    share_copies = []
    for k in range(Z):
        for x in range(X_HI):
            start = (x * Z + k) * width
            share_copies.append(
                pltpu.make_async_copy(
                    out_weight.at[
                        pl.ds(pl.multiple_of(my_block * size, size), size), start : start + width
                    ],
                    buffer.at[k, :, x * width : (x + 1) * width],
                    share_sems.at[k, x],
                )
            )
    copies = column_copies(SECOND, w, send, own, sems)
    for copy in share_copies + copies:
        copy.start()
    for copy in share_copies:
        copy.wait()
    out_copy = pltpu.make_async_copy(buffer, share, out_sem)
    out_copy.start()
    for copy in copies:
        copy.wait()
    out_copy.wait()


def second_columns(w, out_weight):
    columns = jax.ShapeDtypeStruct((w.shape[0], len(SECOND) * X_HI * QKV), bf16)
    shape = (Z, out_weight.shape[0] // BLOCKS, out_weight.shape[1] // Z)
    return pl.pallas_call(
        second_columns_kernel,
        out_shape=(columns, columns, pltpu.HBM(shape, bf16)),
        in_specs=[hbm(), hbm()],
        out_specs=(vmem(), vmem(), hbm()),
        scratch_shapes=[
            pltpu.VMEM(shape, bf16),
            pltpu.SemaphoreType.DMA((2, len(SECOND) * X_HI)),
            pltpu.SemaphoreType.DMA((Z, X_HI)),
            pltpu.SemaphoreType.DMA(()),
        ],
        compiler_params=limit(12),
    )(
        pltpu.with_memory_space_constraint(w, pltpu.HBM),
        pltpu.with_memory_space_constraint(out_weight, pltpu.HBM),
    )


def two_rows(row, width):
    high = row.astype(bf16)
    low = (row - high.astype(f32)).astype(bf16)
    line = lax.broadcasted_iota(jnp.int32, (16, width), 0)
    both = jnp.where(line == 0, high.astype(f32), jnp.where(line == 1, low.astype(f32), 0.0))
    return both.astype(bf16)


def one_row(rows):
    return jnp.sum(rows.astype(f32), axis=0, keepdims=True)


def partial_kernel(ks, own, sis, gains, w_own, w_sis, *outs):
    width = X_HI * QKV
    core = lax.axis_index("core")
    own_rows, sis_rows = own[...].astype(f32), sis[...].astype(f32)
    left, right = gains[:, :TOK].astype(f32), gains[:, TOK:].astype(f32)
    x_own = (own_rows * jnp.where(core == 0, left, right)).astype(bf16)
    x_sis = (sis_rows * jnp.where(core == 0, right, left)).astype(bf16)
    squares = jnp.sum(own_rows * own_rows + sis_rows * sis_rows, axis=1, keepdims=True)
    line = lax.broadcasted_iota(jnp.int32, (ROWS, QKV), 0)
    lane = lax.broadcasted_iota(jnp.int32, (ROWS, QKV), 1)
    row = jnp.sum(jnp.where(line == lane, squares, 0.0), axis=0, keepdims=True)
    tail = two_rows(row, QKV)

    def product(slot, count):
        cols = slice(slot * QKV, (slot + count) * QKV)
        acc = jnp.dot(x_own, w_own[:, cols], preferred_element_type=f32)
        acc = acc + jnp.dot(x_sis, w_sis[:, cols], preferred_element_type=f32)
        return acc.astype(bf16)

    def full(slot, out):
        out[:ROWS, :] = product(slot, X_HI)
        out[ROWS:, :QKV] = tail
        out[ROWS:, QKV:] = tail

    if ks == FIRST:
        near_up, up, down, near_down, buffer, sems = outs
        copies = []
        for i, near in enumerate((near_up, near_down)):
            full(FIRST.index((3, 5)[i]) * X_HI, buffer.at[i])
            copies.append(pltpu.make_async_copy(buffer.at[i], near, sems.at[i]))
            copies[i].start()
        for xr, out in enumerate((up, down)):
            out[:ROWS, :] = product(FIRST.index(Z // 2) * X_HI + xr, 1)
            out[ROWS:, :] = tail
        for copy in copies:
            copy.wait()
    else:
        for i, out in enumerate(outs):
            full(i * X_HI, out)


def partials(ks, own, sis, gains, w_own, w_sis):
    half = jax.ShapeDtypeStruct((SUM_ROWS, QKV), bf16)
    full = jax.ShapeDtypeStruct((SUM_ROWS, X_HI * QKV), bf16)
    if ks == FIRST:
        away = pltpu.HBM(full.shape, bf16)
        shapes, specs = (away, half, half, away), (hbm(), vmem(), vmem(), hbm())
        scratch = [pltpu.VMEM((2, *full.shape), bf16), pltpu.SemaphoreType.DMA((2,))]
    else:
        shapes, specs, scratch = (full,) * len(ks), (vmem(),) * len(ks), []
    return pl.pallas_call(
        functools.partial(partial_kernel, ks),
        out_shape=shapes,
        in_specs=[vmem()] * 5,
        out_specs=specs,
        scratch_shapes=scratch,
        compiler_params=limit(20),
        cost_estimate=pl.CostEstimate(
            flops=4 * ROWS * w_own.size, bytes_accessed=8 * w_own.size, transcendentals=0
        ),
    )(own, sis, gains, w_own, w_sis)


def store_sum(out, cols, terms):
    body = sum(term[:ROWS].astype(f32) for term in terms)
    row = sum(one_row(term[ROWS:]) for term in terms)
    out[:ROWS, cols] = body.astype(bf16)
    out[ROWS:, cols] = two_rows(row, row.shape[1])


def first_kernel(up, down, near_up, near_down, out_up, out_down):
    left, right = slice(0, QKV), slice(QKV, 2 * QKV)
    store_sum(out_up, left, [up[...], near_up[:, left]])
    out_up[:, right] = near_up[:, right]
    out_down[:, left] = near_down[:, left]
    store_sum(out_down, right, [down[...], near_down[:, right]])


def next_kernel(up, down, near_up, near_down, out_up, out_down):
    every = slice(0, 2 * QKV)
    store_sum(out_up, every, [up[...], near_up[...]])
    store_sum(out_down, every, [down[...], near_down[...]])


def ring_add(kernel, up, down, near_up, near_down):
    out = jax.ShapeDtypeStruct((SUM_ROWS, X_HI * QKV), bf16)
    return pl.pallas_call(
        kernel,
        out_shape=(out, out),
        in_specs=[vmem()] * 4,
        out_specs=(vmem(), vmem()),
        compiler_params=limit(8),
    )(up, down, near_up, near_down)


def last_kernel(up, down, near, mine, other):
    own, far = slice(0, QKV), slice(QKV, 2 * QKV)
    terms = [up, down, near]
    mine[:ROWS] = sum(term[:ROWS, own].astype(f32) for term in terms)
    row = sum(one_row(term[ROWS:, own]) for term in terms)
    mine[ROWS:] = jnp.broadcast_to(row, (8, QKV))
    store_sum(other, slice(0, QKV), [term[:, far] for term in terms])


def ring_last(up, down, near):
    return pl.pallas_call(
        last_kernel,
        out_shape=(
            jax.ShapeDtypeStruct((ROWS + 8, QKV), f32),
            jax.ShapeDtypeStruct((SUM_ROWS, QKV), bf16),
        ),
        in_specs=[vmem()] * 3,
        out_specs=(vmem(), vmem()),
        compiler_params=limit(8),
    )(up, down, near)


def rotated(x, cosine, sine):
    return x * cosine + pltpu.roll(x, HD // 2, 1) * sine


def finish_kernel(full_width, mine, other, cosine, sine, onehot, payload, queries):
    row = mine[ROWS : ROWS + 1, :] + one_row(other[ROWS:, :])
    line = lax.broadcasted_iota(jnp.int32, (ROWS, QKV), 0)
    lane = lax.broadcasted_iota(jnp.int32, (ROWS, QKV), 1)
    squares = jnp.sum(jnp.where(line == lane, row, 0.0), axis=1, keepdims=True)
    inv_rms = lax.rsqrt(squares / full_width + epsilon)
    proj = (mine[:ROWS, :] + other[:ROWS, :].astype(f32)) * inv_rms
    query = rotated(proj[:, :HD], cosine[...], sine[...]).astype(bf16)
    key = rotated(proj[:, HD : 2 * HD], cosine[...], sine[...]).astype(bf16)
    value = proj[:, 2 * HD :].astype(bf16)
    spots = onehot[...]

    def step(b, carry):
        payload[b, :ROWS, :HD] = key
        payload[b, :ROWS, HD:] = value
        payload[b, ROWS:, :] = spots
        return carry

    lax.fori_loop(0, BLOCKS, step, 0)
    contract = (((0,), (0,)), ((), ()))
    ones = jnp.ones((VAR, HD), bf16)
    changed = lax.dot_general(spots, ones, contract, preferred_element_type=f32)
    placed = lax.dot_general(spots, query[TOK:], contract, preferred_element_type=f32)
    base = query[:TOK]
    queries[:TOK] = base
    queries[TOK:] = jnp.where(changed > 0.5, placed, base.astype(f32)).astype(bf16)


def finish(full_width, mine, other, cosine, sine, onehot):
    return pl.pallas_call(
        functools.partial(finish_kernel, full_width),
        out_shape=(
            jax.ShapeDtypeStruct((BLOCKS, PAY, 2 * HD), bf16),
            jax.ShapeDtypeStruct((2 * TOK, HD), bf16),
        ),
        in_specs=[vmem()] * 5,
        out_specs=(vmem(), vmem()),
        compiler_params=limit(12),
    )(mine, other, cosine, sine, pltpu.with_memory_space_constraint(onehot, pltpu.HBM))


def attend_kernel(queries, blocks, out, scores, peak, denom, total, var_kv, spots):
    my_block = lax.axis_index("x_lo") * Y + lax.axis_index("y")
    scale = 1.0 / HD**0.5
    by_cols = (((1,), (1,)), ((), ()))
    lowest = -jnp.inf
    query = queries[...]

    def score_block(j, own):
        score = lax.dot_general(
            query, blocks[j, :TOK, :HD], by_cols, preferred_element_type=f32
        ) * scale
        gone = jnp.sum(blocks[j, ROWS:, :].astype(f32), axis=0, keepdims=True) > 0.5
        line = lax.broadcasted_iota(jnp.int32, (2 * TOK, TOK), 0)
        hidden = (line >= TOK) & gone
        if own:
            lane = lax.broadcasted_iota(jnp.int32, (2 * TOK, TOK), 1)
            hidden = hidden | (lax.rem(line, TOK) < lane)
        return jnp.where(hidden, lowest, score)

    score = score_block(my_block, True)
    scores[my_block] = score
    peak[...] = jnp.maximum(score[:, :HD], score[:, HD:])

    def first(j, carry):
        score = score_block(j, False)
        scores[j] = score
        peak[...] = jnp.maximum(peak[...], jnp.maximum(score[:, :HD], score[:, HD:]))
        return carry

    lax.fori_loop(0, my_block, first, 0)

    for j in range(BLOCKS):
        var_kv[j * VAR : (j + 1) * VAR, :] = blocks[j, TOK:ROWS, :]
        spots[j * VAR : (j + 1) * VAR, :] = blocks[j, ROWS:, :]
    row = lax.broadcasted_iota(jnp.int32, (TOK, TOK), 0)
    col = lax.broadcasted_iota(jnp.int32, (TOK, TOK), 1)
    reached = lax.dot_general(
        jnp.where(row >= col, 1.0, 0.0).astype(bf16), spots[...], by_cols, preferred_element_type=f32
    )
    source = lax.broadcasted_iota(jnp.int32, (TOK, BLOCKS * VAR), 1) // VAR
    seen = (source < my_block) | ((source == my_block) & (reached > 0.5))
    more = lax.dot_general(
        query[TOK:], var_kv[:, :HD], by_cols, preferred_element_type=f32
    ) * scale
    more = jnp.where(seen, more, lowest)
    peak[TOK:, :] = jnp.maximum(peak[TOK:, :], more)
    top = jnp.max(peak[...], axis=1, keepdims=True)
    peak[...] = jnp.broadcast_to(top, (2 * TOK, HD))

    more = jnp.exp(more - top[TOK:])
    denom[:TOK, :] = jnp.zeros((TOK, HD), f32)
    denom[TOK:, :] = more
    total[:TOK, :] = jnp.zeros((TOK, HD), f32)
    total[TOK:, :] = jnp.dot(more.astype(bf16), var_kv[:, HD:], preferred_element_type=f32)

    def second(j, carry):
        best = peak[...]
        left = jnp.exp(scores[j, :, :HD] - best)
        right = jnp.exp(scores[j, :, HD:] - best)
        denom[...] = denom[...] + left + right
        probs = jnp.concatenate([left.astype(bf16), right.astype(bf16)], axis=1)
        total[...] = total[...] + jnp.dot(
            probs, blocks[j, :TOK, HD:], preferred_element_type=f32
        )
        return carry

    lax.fori_loop(0, my_block + 1, second, 0)
    out[...] = (total[...] / jnp.sum(denom[...], axis=1, keepdims=True)).astype(bf16)


def attend(queries, blocks):
    return pl.pallas_call(
        attend_kernel,
        out_shape=jax.ShapeDtypeStruct((2 * TOK, HD), bf16),
        in_specs=[vmem(), vmem()],
        out_specs=vmem(),
        scratch_shapes=[
            pltpu.VMEM((BLOCKS, 2 * TOK, TOK), f32),
            pltpu.VMEM((2 * TOK, HD), f32),
            pltpu.VMEM((2 * TOK, HD), f32),
            pltpu.VMEM((2 * TOK, HD), f32),
            pltpu.VMEM((BLOCKS * VAR, 2 * HD), bf16),
            pltpu.VMEM((BLOCKS * VAR, TOK), bf16),
        ],
        compiler_params=limit(16),
    )(queries, blocks)


def arrange_kernel(w, out, sems):
    z = lax.axis_index("z")
    copies = []
    for d in range(Z):
        source = lax.rem(z + Z - d, Z)
        copies.append(
            pltpu.make_async_copy(w.at[source], out.at[d * HD : (d + 1) * HD, :], sems.at[d])
        )
    for copy in copies:
        copy.start()
    for copy in copies:
        copy.wait()


def arrange(w):
    return pl.pallas_call(
        arrange_kernel,
        out_shape=jax.ShapeDtypeStruct((Z * HD, w.shape[2]), bf16),
        in_specs=[hbm()],
        out_specs=vmem(),
        scratch_shapes=[pltpu.SemaphoreType.DMA((Z,))],
        compiler_params=limit(4),
    )(pltpu.with_memory_space_constraint(w, pltpu.HBM))


def project_kernel(turned, *refs):
    shards, (keep, near, far), joined = refs[:Z], refs[Z : Z + 3], refs[-1]
    core, x_hi = lax.axis_index("core"), lax.axis_index("x_hi")
    for d in range(Z):
        joined[:, d * HD : (d + 1) * HD] = shards[d][...]

    def product(xr, cr, rows):
        column = (lax.rem(x_hi + xr, X_HI) * CORE + lax.rem(core + cr, CORE)) * TOK
        column = pl.ds(pl.multiple_of(column, TOK), TOK)
        return jnp.dot(joined[rows, :], turned[:, column], preferred_element_type=f32)

    size = 128

    def step(i, carry):
        rows = pl.ds(pl.multiple_of(i * size, size), size)
        for xr in range(X_HI):
            near[rows, xr * TOK : (xr + 1) * TOK] = product(xr, 1, rows).astype(bf16)
        keep[rows, :] = product(0, 0, rows)
        far[rows, :] = product(1, 0, rows)
        return carry

    lax.fori_loop(0, 2 * TOK // size, step, 0)


def project(w, shards):
    rows = shards[0].shape[0]
    return pl.pallas_call(
        project_kernel,
        out_shape=(
            jax.ShapeDtypeStruct((rows, TOK), f32),
            jax.ShapeDtypeStruct((rows, 2 * TOK), bf16),
            jax.ShapeDtypeStruct((rows, TOK), f32),
        ),
        in_specs=[vmem()] * (1 + Z),
        out_specs=(vmem(),) * 3,
        scratch_shapes=[pltpu.VMEM((rows, Z * HD), bf16)],
        compiler_params=limit(16),
    )(w, *shards)


def shards(hidden, gain, embed, qkv_weight, out_weight, ref_ids, var_pos, var_base):
    tok_rows, width_part = hidden.shape
    full_width = out_weight.shape[1]
    x_hi, z, core = lax.axis_index("x_hi"), lax.axis_index("z"), lax.axis_index("core")
    my_block = lax.axis_index("x_lo") * Y + lax.axis_index("y")
    chip_slice = x_hi * Z + z

    with jax.named_scope("inputs"):
        rows, onehot, variant = make_variant(var_pos, var_base, ref_ids, hidden, embed)
        rows, qkv_weight = lax.optimization_barrier((rows, qkv_weight))
        rows_sis = shift(rows, "core", CORE, 1)
        send_first, own_first = first_columns(qkv_weight)
        sis_first = shift(send_first, "core", CORE, 1)
        rows_sis, send_first, qkv_weight = lax.optimization_barrier((rows_sis, send_first, qkv_weight))
        send_second, own_second, share = second_columns(qkv_weight, out_weight)
        sis_second = shift(send_second, "core", CORE, 1)
        shared = lax.all_to_all(share, "z", 0, 0, tiled=True)
        start = chip_slice * 2 * width_part
        gains = lax.dynamic_slice(gain.reshape(1, full_width), (0, start), (1, 2 * width_part))

    with jax.named_scope("projection"):
        near_up, up, down, near_down = partials(FIRST, rows, rows_sis, gains, own_first, sis_first)
        up, down = shift(up, "z", Z, 1), shift(down, "z", Z, -1)
        near_up = pltpu.with_memory_space_constraint(near_up, pltpu.HBM)
        near_down = pltpu.with_memory_space_constraint(near_down, pltpu.HBM)
        up, down, shared = lax.optimization_barrier((up, down, shared))
        out_w = lax.all_gather(shared, CTX, axis=1, tiled=True)
        up, down = ring_add(first_kernel, up, down, near_up, near_down)
        up, rows, down = lax.optimization_barrier((up, rows, down))
        up, down = shift(up, "z", Z, 1), shift(down, "z", Z, -1)
        parts = partials(SECOND, rows, rows_sis, gains, own_second, sis_second)
        up, down, parts = lax.optimization_barrier((up, down, parts))
        parts = dict(zip(SECOND, parts))
        up, down = ring_add(next_kernel, up, down, parts[2], parts[6])
        up, down = shift(up, "z", Z, 1), shift(down, "z", Z, -1)
        up, down = ring_add(next_kernel, up, down, parts[1], parts[7])
        up, down = shift(up, "z", Z, 1), shift(down, "z", Z, -1)
        mine, other = ring_last(up, down, parts[0])
        other = shift(other, "x_hi", X_HI, 1)

    with jax.named_scope("tables"):
        positions = jnp.concatenate([my_block * tok_rows + jnp.arange(tok_rows), var_pos])
        exponent = jnp.arange(HD // 2).astype(f32) * (-2.0 / HD)
        inv_freq = jnp.power(f32(rope_base), exponent)
        angle = positions.astype(f32)[:, None] * inv_freq[None, :]
        cosine, sine = jnp.cos(angle), jnp.sin(angle)
        cosine = jnp.concatenate([cosine, cosine], axis=1)
        sine = jnp.concatenate([-sine, sine], axis=1)

    with jax.named_scope("attention"):
        payload, queries = finish(full_width, mine, other, cosine, sine, onehot)
        blocks = lax.all_to_all(payload, CTX, 0, 0, tiled=True)
        attn = attend(queries, blocks)
        attn, out_w = lax.optimization_barrier((attn, out_w))

    with jax.named_scope("output"):
        pieces = [attn] + [None] * (Z - 1)
        for d in (1, 2, 3):
            pieces[d] = shift(pieces[d - 1], "z", Z, 1)
            pieces[Z - d] = shift(pieces[(Z - d + 1) % Z], "z", Z, -1)
            if d == 1:
                pieces[Z // 2] = shift(attn, "z", Z, Z // 2)
                out_w, pieces[1], pieces[7] = lax.optimization_barrier(
                    (arrange(out_w), pieces[1], pieces[7])
                )
        keep, near, far = project(out_w, pieces)
        near = shift(near, "core", CORE, 1).astype(f32)
        far = (far + near[:, width_part:]).astype(bf16)
        far = shift(far, "x_hi", X_HI, 1).astype(f32)
        branch = (keep + near[:, :width_part] + far).reshape(2, tok_rows, width_part)
        seqs = jnp.stack([hidden, variant]).astype(f32)
        return (seqs + branch).astype(bf16)


def solution(mesh):
    fine = Mesh(mesh.devices.reshape(X_HI, Z, CORE, X_LO, Y), (*FSDP, *CTX))
    in_specs = (
        P(CTX, FSDP),
        P(),
        P(None, FSDP),
        P(FSDP, None),
        P(FSDP, None),
        P(CTX),
        P(CTX),
        P(CTX),
    )
    out_specs = P(None, CTX, FSDP)
    return jax.shard_map(shards, mesh=fine, in_specs=in_specs, out_specs=out_specs, check_vma=False)
```

```python
import functools

import jax
import jax.numpy as jnp
from jax import lax
from jax.experimental import pallas as pl
from jax.experimental.pallas import tpu as pltpu
from jax.sharding import Mesh, PartitionSpec as P

epsilon = 1e-05
rope_base = 10000.0

X_HI, Z, CORE, X_LO, Y = 2, 8, 2, 2, 4
FSDP = ("x_hi", "z", "core")
CTX = ("x_lo", "y")
BLOCKS = X_LO * Y
HD = 128
QKV = 3 * HD
TOK = 256
VAR = 16
ROWS = TOK + VAR
SUM_ROWS = ROWS + 16
PAY = ROWS + VAR
bf16 = jnp.bfloat16
f32 = jnp.float32
MIB = 1024 * 1024


def shift(value, axis, size, distance):
    return lax.ppermute(value, axis, [(i, (i + distance) % size) for i in range(size)])


def vmem():
    return pl.BlockSpec(memory_space=pltpu.VMEM)


def anywhere():
    return pl.BlockSpec(memory_space=pl.ANY)


def hbm():
    return pl.BlockSpec(memory_space=pltpu.HBM)


def limit(mib):
    return pltpu.CompilerParams(vmem_limit_bytes=mib * MIB)


FIRST = (4,)
SECOND = (3, 5, 2, 6, 1, 7, 0)


def variant_kernel(
    pos, base, ids, hidden, embed, w, rows, onehot, variant, share, spots, block, buffer, sems, share_sems
):
    my_block = lax.axis_index("x_lo") * Y + lax.axis_index("y")
    size, half = buffer.shape[1], buffer.shape[2] // X_HI
    share_rows = pl.ds(pl.multiple_of(my_block * size, size), size)
    copies = []
    for k in range(Z):
        for x in range(X_HI):
            start = (x * Z + k) * half
            copies.append(
                pltpu.make_async_copy(
                    w.at[share_rows, start : start + half],
                    buffer.at[k, :, x * half : (x + 1) * half],
                    share_sems.at[k, x],
                )
            )
    for copy in copies:
        copy.start()
    first = (lax.axis_index("x_lo") * Y + lax.axis_index("y")) * TOK
    vocab = embed.shape[0]
    spot = lax.broadcasted_iota(jnp.int32, (VAR, TOK), 0)
    lane = lax.broadcasted_iota(jnp.int32, (VAR, TOK), 1)
    word_spot = lax.broadcasted_iota(jnp.int32, (VAR, vocab), 0)
    word = lax.broadcasted_iota(jnp.int32, (VAR, vocab), 1)
    places = jnp.zeros((VAR, TOK), f32)
    words = jnp.zeros((VAR, vocab), f32)
    for j in range(VAR):
        place = pos[j] - first
        places = jnp.where((spot == j) & (lane == place), 1.0, places)
        new = jnp.where(word == base[j], 1.0, 0.0)
        old = jnp.where(word == ids[place], 1.0, 0.0)
        words = jnp.where(word_spot == j, new - old, words)
    places = places.astype(bf16)
    change = jnp.dot(words.astype(bf16), embed[...], preferred_element_type=f32)
    picked = jnp.dot(places, hidden[...], preferred_element_type=f32)
    changed_rows = (picked + change).astype(bf16)
    rows[:TOK] = hidden[...]
    rows[TOK:] = changed_rows
    spots[...] = places
    for copy in copies:
        copy.wait()
    share_copy = pltpu.make_async_copy(buffer, share, sems.at[2])
    share_copy.start()
    first_copy = pltpu.make_async_copy(spots, onehot, sems.at[0])
    first_copy.start()
    contract = (((0,), (0,)), ((), ()))
    placed = lax.dot_general(places, changed_rows, contract, preferred_element_type=f32)
    ones = jnp.ones((VAR, hidden.shape[1]), bf16)
    changed = lax.dot_general(places, ones, contract, preferred_element_type=f32)
    block[...] = jnp.where(changed > 0.5, placed, hidden[...].astype(f32)).astype(bf16)
    second_copy = pltpu.make_async_copy(block, variant, sems.at[1])
    second_copy.start()
    first_copy.wait()
    second_copy.wait()
    share_copy.wait()


def make_variant(pos, base, ids, hidden, embed, w):
    width = hidden.shape[1]
    shape = (Z, w.shape[0] // BLOCKS, w.shape[1] // Z)
    args = (pos, base, ids, hidden, embed, w)
    smem = pl.BlockSpec(memory_space=pltpu.SMEM)
    return pl.pallas_call(
        variant_kernel,
        out_shape=(
            jax.ShapeDtypeStruct((ROWS, width), bf16),
            pltpu.HBM((VAR, TOK), bf16),
            pltpu.HBM((TOK, width), bf16),
            pltpu.HBM(shape, bf16),
        ),
        in_specs=[smem, smem, smem, vmem(), vmem(), hbm()],
        out_specs=(vmem(), hbm(), hbm(), hbm()),
        scratch_shapes=[
            pltpu.VMEM((VAR, TOK), bf16),
            pltpu.VMEM((TOK, width), bf16),
            pltpu.VMEM(shape, bf16),
            pltpu.SemaphoreType.DMA((3,)),
            pltpu.SemaphoreType.DMA((Z, X_HI)),
        ],
        compiler_params=limit(4),
    )(*(pltpu.with_memory_space_constraint(v, pltpu.HBM) for v in args))


def column_copies(ks, w, send, own, sems):
    z, core, x_hi = lax.axis_index("z"), lax.axis_index("core"), lax.axis_index("x_hi")
    copies = []
    for index, (whose, out) in enumerate(((1 - core, send), (core, own))):
        for i, k in enumerate(ks):
            for xr in range(X_HI):
                head_pair = lax.rem(x_hi + xr, X_HI) * Z + lax.rem(z + k, Z)
                slot = i * X_HI + xr
                start = pl.multiple_of((head_pair * 2 + whose) * QKV, HD)
                copies.append(
                    pltpu.make_async_copy(
                        w.at[:, pl.ds(start, QKV)],
                        out.at[:, slot * QKV : (slot + 1) * QKV],
                        sems.at[index, slot],
                    )
                )
    return copies


def columns_kernel(ks, w, send, own, sems):
    copies = column_copies(ks, w, send, own, sems)
    for copy in copies:
        copy.start()
    for copy in copies:
        copy.wait()


def pick_columns(ks, w):
    columns = jax.ShapeDtypeStruct((w.shape[0], len(ks) * X_HI * QKV), bf16)
    return pl.pallas_call(
        functools.partial(columns_kernel, ks),
        out_shape=(columns, columns),
        in_specs=[hbm()],
        out_specs=(vmem(), vmem()),
        scratch_shapes=[pltpu.SemaphoreType.DMA((2, len(ks) * X_HI))],
        compiler_params=limit(12),
    )(pltpu.with_memory_space_constraint(w, pltpu.HBM))


def two_rows(row, width):
    high = row.astype(bf16)
    low = (row - high.astype(f32)).astype(bf16)
    line = lax.broadcasted_iota(jnp.int32, (16, width), 0)
    both = jnp.where(line == 0, high.astype(f32), jnp.where(line == 1, low.astype(f32), 0.0))
    return both.astype(bf16)


def one_row(rows):
    return jnp.sum(rows.astype(f32), axis=0, keepdims=True)


def partial_kernel(ks, own, sis, gains, w_own, w_sis, *outs):
    width = X_HI * QKV
    core = lax.axis_index("core")
    own_rows, sis_rows = own[...].astype(f32), sis[...].astype(f32)
    left, right = gains[:, :TOK].astype(f32), gains[:, TOK:].astype(f32)
    x_own = (own_rows * jnp.where(core == 0, left, right)).astype(bf16)
    x_sis = (sis_rows * jnp.where(core == 0, right, left)).astype(bf16)
    squares = jnp.sum(own_rows * own_rows + sis_rows * sis_rows, axis=1, keepdims=True)
    line = lax.broadcasted_iota(jnp.int32, (ROWS, QKV), 0)
    lane = lax.broadcasted_iota(jnp.int32, (ROWS, QKV), 1)
    row = jnp.sum(jnp.where(line == lane, squares, 0.0), axis=0, keepdims=True)
    tail = two_rows(row, QKV)

    def product(slot, count):
        cols = slice(slot * QKV, (slot + count) * QKV)
        acc = jnp.dot(x_own, w_own[:, cols], preferred_element_type=f32)
        acc = acc + jnp.dot(x_sis, w_sis[:, cols], preferred_element_type=f32)
        return acc.astype(bf16)

    def full(slot, out):
        out[:ROWS, :] = product(slot, X_HI)
        out[ROWS:, :QKV] = tail
        out[ROWS:, QKV:] = tail

    if ks == FIRST:
        for xr, out in enumerate(outs):
            out[:ROWS, :] = product(xr, 1)
            out[ROWS:, :] = tail
    else:
        outs, buffer, sems = outs[:-2], outs[-2], outs[-1]
        copies = []
        for i, out in enumerate(outs):
            full(i * X_HI, buffer.at[i])
            copies.append(pltpu.make_async_copy(buffer.at[i], out, sems.at[i]))
            copies[i].start()
        for copy in copies:
            copy.wait()


def partials(ks, own, sis, gains, w_own, w_sis):
    half = jax.ShapeDtypeStruct((SUM_ROWS, QKV), bf16)
    full = jax.ShapeDtypeStruct((SUM_ROWS, X_HI * QKV), bf16)
    if ks == FIRST:
        shapes, specs, scratch = (half, half), (vmem(), vmem()), []
    else:
        shapes, specs = (pltpu.HBM(full.shape, bf16),) * len(ks), (hbm(),) * len(ks)
        scratch = [pltpu.VMEM((len(ks), *full.shape), bf16), pltpu.SemaphoreType.DMA((len(ks),))]
    return pl.pallas_call(
        functools.partial(partial_kernel, ks),
        out_shape=shapes,
        in_specs=[vmem()] * 5,
        out_specs=specs,
        scratch_shapes=scratch,
        compiler_params=limit(20),
        cost_estimate=pl.CostEstimate(
            flops=4 * ROWS * w_own.size, bytes_accessed=8 * w_own.size, transcendentals=0
        ),
    )(own, sis, gains, w_own, w_sis)


def store_sum(out, cols, terms):
    body = sum(term[:ROWS].astype(f32) for term in terms)
    row = sum(one_row(term[ROWS:]) for term in terms)
    out[:ROWS, cols] = body.astype(bf16)
    out[ROWS:, cols] = two_rows(row, row.shape[1])


def first_kernel(up, down, near_up, near_down, out_up, out_down):
    left, right = slice(0, QKV), slice(QKV, 2 * QKV)
    store_sum(out_up, left, [up[...], near_up[:, left]])
    out_up[:, right] = near_up[:, right]
    out_down[:, left] = near_down[:, left]
    store_sum(out_down, right, [down[...], near_down[:, right]])


def next_kernel(up, down, near_up, near_down, out_up, out_down):
    every = slice(0, 2 * QKV)
    store_sum(out_up, every, [up[...], near_up[...]])
    store_sum(out_down, every, [down[...], near_down[...]])


def ring_add(kernel, up, down, near_up, near_down):
    out = jax.ShapeDtypeStruct((SUM_ROWS, X_HI * QKV), bf16)
    return pl.pallas_call(
        kernel,
        out_shape=(out, out),
        in_specs=[vmem()] * 4,
        out_specs=(vmem(), vmem()),
        compiler_params=limit(8),
    )(up, down, near_up, near_down)


def last_kernel(up, down, near, mine, other):
    own, far = slice(0, QKV), slice(QKV, 2 * QKV)
    terms = [up, down, near]
    mine[:ROWS] = sum(term[:ROWS, own].astype(f32) for term in terms)
    row = sum(one_row(term[ROWS:, own]) for term in terms)
    mine[ROWS:] = jnp.broadcast_to(row, (8, QKV))
    store_sum(other, slice(0, QKV), [term[:, far] for term in terms])


def ring_last(up, down, near):
    return pl.pallas_call(
        last_kernel,
        out_shape=(
            jax.ShapeDtypeStruct((ROWS + 8, QKV), f32),
            jax.ShapeDtypeStruct((SUM_ROWS, QKV), bf16),
        ),
        in_specs=[vmem()] * 3,
        out_specs=(vmem(), vmem()),
        compiler_params=limit(8),
    )(up, down, near)


def rotated(x, cosine, sine):
    return x * cosine + pltpu.roll(x, HD // 2, 1) * sine


def finish_kernel(full_width, mine, other, cosine, sine, onehot, payload, queries):
    row = mine[ROWS : ROWS + 1, :] + one_row(other[ROWS:, :])
    line = lax.broadcasted_iota(jnp.int32, (ROWS, QKV), 0)
    lane = lax.broadcasted_iota(jnp.int32, (ROWS, QKV), 1)
    squares = jnp.sum(jnp.where(line == lane, row, 0.0), axis=1, keepdims=True)
    inv_rms = lax.rsqrt(squares / full_width + epsilon)
    proj = (mine[:ROWS, :] + other[:ROWS, :].astype(f32)) * inv_rms
    query = rotated(proj[:, :HD], cosine[...], sine[...]).astype(bf16)
    key = rotated(proj[:, HD : 2 * HD], cosine[...], sine[...]).astype(bf16)
    value = proj[:, 2 * HD :].astype(bf16)
    spots = onehot[...]

    def step(b, carry):
        payload[b, :ROWS, :HD] = key
        payload[b, :ROWS, HD:] = value
        payload[b, ROWS:, :] = spots
        return carry

    lax.fori_loop(0, BLOCKS, step, 0)
    contract = (((0,), (0,)), ((), ()))
    ones = jnp.ones((VAR, HD), bf16)
    changed = lax.dot_general(spots, ones, contract, preferred_element_type=f32)
    placed = lax.dot_general(spots, query[TOK:], contract, preferred_element_type=f32)
    base = query[:TOK]
    queries[:TOK] = base
    queries[TOK:] = jnp.where(changed > 0.5, placed, base.astype(f32)).astype(bf16)


def finish(full_width, mine, other, cosine, sine, onehot):
    return pl.pallas_call(
        functools.partial(finish_kernel, full_width),
        out_shape=(
            jax.ShapeDtypeStruct((BLOCKS, PAY, 2 * HD), bf16),
            jax.ShapeDtypeStruct((2 * TOK, HD), bf16),
        ),
        in_specs=[vmem()] * 5,
        out_specs=(vmem(), vmem()),
        compiler_params=limit(12),
    )(mine, other, cosine, sine, pltpu.with_memory_space_constraint(onehot, pltpu.HBM))


def attend_kernel(queries, blocks, out, scores, peak, denom, total, var_kv, spots):
    my_block = lax.axis_index("x_lo") * Y + lax.axis_index("y")
    scale = 1.0 / HD**0.5
    by_cols = (((1,), (1,)), ((), ()))
    lowest = -jnp.inf
    query = queries[...]

    def score_block(j, own):
        score = lax.dot_general(
            query, blocks[j, :TOK, :HD], by_cols, preferred_element_type=f32
        ) * scale
        gone = jnp.sum(blocks[j, ROWS:, :].astype(f32), axis=0, keepdims=True) > 0.5
        line = lax.broadcasted_iota(jnp.int32, (2 * TOK, TOK), 0)
        hidden = (line >= TOK) & gone
        if own:
            lane = lax.broadcasted_iota(jnp.int32, (2 * TOK, TOK), 1)
            hidden = hidden | (lax.rem(line, TOK) < lane)
        return jnp.where(hidden, lowest, score)

    score = score_block(my_block, True)
    scores[my_block] = score
    peak[...] = jnp.maximum(score[:, :HD], score[:, HD:])

    def first(j, carry):
        score = score_block(j, False)
        scores[j] = score
        peak[...] = jnp.maximum(peak[...], jnp.maximum(score[:, :HD], score[:, HD:]))
        return carry

    lax.fori_loop(0, my_block, first, 0)

    for j in range(BLOCKS):
        var_kv[j * VAR : (j + 1) * VAR, :] = blocks[j, TOK:ROWS, :]
        spots[j * VAR : (j + 1) * VAR, :] = blocks[j, ROWS:, :]
    row = lax.broadcasted_iota(jnp.int32, (TOK, TOK), 0)
    col = lax.broadcasted_iota(jnp.int32, (TOK, TOK), 1)
    reached = lax.dot_general(
        jnp.where(row >= col, 1.0, 0.0).astype(bf16), spots[...], by_cols, preferred_element_type=f32
    )
    source = lax.broadcasted_iota(jnp.int32, (TOK, BLOCKS * VAR), 1) // VAR
    seen = (source < my_block) | ((source == my_block) & (reached > 0.5))
    more = lax.dot_general(
        query[TOK:], var_kv[:, :HD], by_cols, preferred_element_type=f32
    ) * scale
    more = jnp.where(seen, more, lowest)
    peak[TOK:, :] = jnp.maximum(peak[TOK:, :], more)
    top = jnp.max(peak[...], axis=1, keepdims=True)
    peak[...] = jnp.broadcast_to(top, (2 * TOK, HD))

    more = jnp.exp(more - top[TOK:])
    denom[:TOK, :] = jnp.zeros((TOK, HD), f32)
    denom[TOK:, :] = more
    total[:TOK, :] = jnp.zeros((TOK, HD), f32)
    total[TOK:, :] = jnp.dot(more.astype(bf16), var_kv[:, HD:], preferred_element_type=f32)

    def second(j, carry):
        best = peak[...]
        left = jnp.exp(scores[j, :, :HD] - best)
        right = jnp.exp(scores[j, :, HD:] - best)
        denom[...] = denom[...] + left + right
        probs = jnp.concatenate([left.astype(bf16), right.astype(bf16)], axis=1)
        total[...] = total[...] + jnp.dot(
            probs, blocks[j, :TOK, HD:], preferred_element_type=f32
        )
        return carry

    lax.fori_loop(0, my_block + 1, second, 0)
    out[...] = (total[...] / jnp.sum(denom[...], axis=1, keepdims=True)).astype(bf16)


def attend(queries, blocks):
    return pl.pallas_call(
        attend_kernel,
        out_shape=jax.ShapeDtypeStruct((2 * TOK, HD), bf16),
        in_specs=[vmem(), vmem()],
        out_specs=vmem(),
        scratch_shapes=[
            pltpu.VMEM((BLOCKS, 2 * TOK, TOK), f32),
            pltpu.VMEM((2 * TOK, HD), f32),
            pltpu.VMEM((2 * TOK, HD), f32),
            pltpu.VMEM((2 * TOK, HD), f32),
            pltpu.VMEM((BLOCKS * VAR, 2 * HD), bf16),
            pltpu.VMEM((BLOCKS * VAR, TOK), bf16),
        ],
        compiler_params=limit(16),
    )(queries, blocks)


def arrange_kernel(w, out, sems):
    z = lax.axis_index("z")
    copies = []
    for d in range(Z):
        source = lax.rem(z + Z - d, Z)
        copies.append(
            pltpu.make_async_copy(w.at[source], out.at[d * HD : (d + 1) * HD, :], sems.at[d])
        )
    for copy in copies:
        copy.start()
    for copy in copies:
        copy.wait()


def arrange(w):
    return pl.pallas_call(
        arrange_kernel,
        out_shape=jax.ShapeDtypeStruct((Z * HD, w.shape[2]), bf16),
        in_specs=[hbm()],
        out_specs=vmem(),
        scratch_shapes=[pltpu.SemaphoreType.DMA((Z,))],
        compiler_params=limit(4),
    )(pltpu.with_memory_space_constraint(w, pltpu.HBM))


def project_kernel(turned, *refs):
    shards, (keep, near, far), joined = refs[:Z], refs[Z : Z + 3], refs[-1]
    core, x_hi = lax.axis_index("core"), lax.axis_index("x_hi")
    for d in range(Z):
        joined[:, d * HD : (d + 1) * HD] = shards[d][...]

    def product(xr, cr, rows):
        column = (lax.rem(x_hi + xr, X_HI) * CORE + lax.rem(core + cr, CORE)) * TOK
        column = pl.ds(pl.multiple_of(column, TOK), TOK)
        return jnp.dot(joined[rows, :], turned[:, column], preferred_element_type=f32)

    size = 128

    def step(i, carry):
        rows = pl.ds(pl.multiple_of(i * size, size), size)
        for xr in range(X_HI):
            near[rows, xr * TOK : (xr + 1) * TOK] = product(xr, 1, rows).astype(bf16)
        keep[rows, :] = product(0, 0, rows)
        far[rows, :] = product(1, 0, rows)
        return carry

    lax.fori_loop(0, 2 * TOK // size, step, 0)


def project(w, shards):
    rows = shards[0].shape[0]
    return pl.pallas_call(
        project_kernel,
        out_shape=(
            jax.ShapeDtypeStruct((rows, TOK), f32),
            jax.ShapeDtypeStruct((rows, 2 * TOK), bf16),
            jax.ShapeDtypeStruct((rows, TOK), f32),
        ),
        in_specs=[vmem()] * (1 + Z),
        out_specs=(vmem(),) * 3,
        scratch_shapes=[pltpu.VMEM((rows, Z * HD), bf16)],
        compiler_params=limit(16),
    )(w, *shards)


def shards(hidden, gain, embed, qkv_weight, out_weight, ref_ids, var_pos, var_base):
    tok_rows, width_part = hidden.shape
    full_width = out_weight.shape[1]
    x_hi, z, core = lax.axis_index("x_hi"), lax.axis_index("z"), lax.axis_index("core")
    my_block = lax.axis_index("x_lo") * Y + lax.axis_index("y")
    chip_slice = x_hi * Z + z

    with jax.named_scope("inputs"):
        rows, onehot, variant, share = make_variant(
            var_pos, var_base, ref_ids, hidden, embed, out_weight
        )
        rows, qkv_weight = lax.optimization_barrier((rows, qkv_weight))
        rows_sis = shift(rows, "core", CORE, 1)
        send_first, own_first = pick_columns(FIRST, qkv_weight)
        sis_first = shift(send_first, "core", CORE, 1)
        rows_sis, sis_first, qkv_weight, share = lax.optimization_barrier(
            (rows_sis, sis_first, qkv_weight, share)
        )
        send_second, own_second = pick_columns(SECOND, qkv_weight)
        sis_second = shift(send_second, "core", CORE, 1)
        shared = lax.all_to_all(share, "z", 0, 0, tiled=True)
        start = chip_slice * 2 * width_part
        gains = lax.dynamic_slice(gain.reshape(1, full_width), (0, start), (1, 2 * width_part))

    with jax.named_scope("projection"):
        sis_first = pltpu.with_memory_space_constraint(sis_first, pltpu.HBM)
        up, down = partials(FIRST, rows, rows_sis, gains, own_first, sis_first)
        up, down = shift(up, "z", Z, 1), shift(down, "z", Z, -1)
        parts = partials(SECOND, rows, rows_sis, gains, own_second, sis_second)
        near_up = pltpu.with_memory_space_constraint(parts[0], pltpu.HBM)
        near_down = pltpu.with_memory_space_constraint(parts[1], pltpu.HBM)
        up, down, shared, near_up = lax.optimization_barrier((up, down, shared, near_up))
        out_w = lax.all_gather(shared, CTX, axis=1, tiled=True)
        parts = dict(zip(SECOND, parts))
        up, down = ring_add(first_kernel, up, down, near_up, near_down)
        up, down = shift(up, "z", Z, 1), shift(down, "z", Z, -1)
        near_up = pltpu.with_memory_space_constraint(parts[2], pltpu.HBM)
        near_down = pltpu.with_memory_space_constraint(parts[6], pltpu.HBM)
        up, down = ring_add(next_kernel, up, down, near_up, near_down)
        up, down = shift(up, "z", Z, 1), shift(down, "z", Z, -1)
        up, down = ring_add(next_kernel, up, down, parts[1], parts[7])
        up, down = shift(up, "z", Z, 1), shift(down, "z", Z, -1)
        mine, other = ring_last(up, down, parts[0])
        other = shift(other, "x_hi", X_HI, 1)

    with jax.named_scope("tables"):
        positions = jnp.concatenate([my_block * tok_rows + jnp.arange(tok_rows), var_pos])
        exponent = jnp.arange(HD // 2).astype(f32) * (-2.0 / HD)
        inv_freq = jnp.power(f32(rope_base), exponent)
        angle = positions.astype(f32)[:, None] * inv_freq[None, :]
        cosine, sine = jnp.cos(angle), jnp.sin(angle)
        cosine = jnp.concatenate([cosine, cosine], axis=1)
        sine = jnp.concatenate([-sine, sine], axis=1)

    with jax.named_scope("attention"):
        payload, queries = finish(full_width, mine, other, cosine, sine, onehot)
        blocks = lax.all_to_all(payload, CTX, 0, 0, tiled=True)
        attn = attend(queries, blocks)
        attn, out_w = lax.optimization_barrier((attn, out_w))

    with jax.named_scope("output"):
        pieces = [attn] + [None] * (Z - 1)
        for d in (1, 2, 3):
            pieces[d] = shift(pieces[d - 1], "z", Z, 1)
            pieces[Z - d] = shift(pieces[(Z - d + 1) % Z], "z", Z, -1)
            if d == 1:
                pieces[Z // 2] = shift(attn, "z", Z, Z // 2)
                out_w, pieces[1], pieces[7] = lax.optimization_barrier(
                    (arrange(out_w), pieces[1], pieces[7])
                )
        keep, near, far = project(out_w, pieces)
        near = shift(near, "core", CORE, 1).astype(f32)
        far = (far + near[:, width_part:]).astype(bf16)
        far = shift(far, "x_hi", X_HI, 1).astype(f32)
        branch = (keep + near[:, :width_part] + far).reshape(2, tok_rows, width_part)
        seqs = jnp.stack([hidden, variant]).astype(f32)
        return (seqs + branch).astype(bf16)


def solution(mesh):
    fine = Mesh(mesh.devices.reshape(X_HI, Z, CORE, X_LO, Y), (*FSDP, *CTX))
    in_specs = (
        P(CTX, FSDP),
        P(),
        P(None, FSDP),
        P(FSDP, None),
        P(FSDP, None),
        P(CTX),
        P(CTX),
        P(CTX),
    )
    out_specs = P(None, CTX, FSDP)
    return jax.shard_map(shards, mesh=fine, in_specs=in_specs, out_specs=out_specs, check_vma=False)
```

```python
import functools

import jax
import jax.numpy as jnp
from jax import lax
from jax.experimental import pallas as pl
from jax.experimental.pallas import tpu as pltpu
from jax.sharding import Mesh, PartitionSpec as P

epsilon = 1e-05
rope_base = 10000.0

X_HI, Z, CORE, X_LO, Y = 2, 8, 2, 2, 4
FSDP = ("x_hi", "z", "core")
CTX = ("x_lo", "y")
BLOCKS = X_LO * Y
HD = 128
QKV = 3 * HD
TOK = 256
VAR = 16
ROWS = TOK + VAR
SUM_ROWS = ROWS + 16
PAY = ROWS + VAR
bf16 = jnp.bfloat16
f32 = jnp.float32
MIB = 1024 * 1024


def shift(value, axis, size, distance):
    return lax.ppermute(value, axis, [(i, (i + distance) % size) for i in range(size)])


def shift_diagonal(value, distance):
    route = [
        (x * Z + z, (1 - x) * Z + (z + distance) % Z) for x in range(X_HI) for z in range(Z)
    ]
    return lax.ppermute(value, ("x_hi", "z"), route)


def vmem():
    return pl.BlockSpec(memory_space=pltpu.VMEM)


def anywhere():
    return pl.BlockSpec(memory_space=pl.ANY)


def hbm():
    return pl.BlockSpec(memory_space=pltpu.HBM)


def limit(mib):
    return pltpu.CompilerParams(vmem_limit_bytes=mib * MIB)


FIRST = (4,)
SECOND = (3, 5, 2, 6, 1, 7, 0)


def variant_kernel(
    pos, base, ids, hidden, embed, w, rows, onehot, variant, share, spots, block, buffer, sems, share_sems
):
    my_block = lax.axis_index("x_lo") * Y + lax.axis_index("y")
    size, half = buffer.shape[1], buffer.shape[2] // X_HI
    share_rows = pl.ds(pl.multiple_of(my_block * size, size), size)
    copies = []
    for k in range(Z):
        for x in range(X_HI):
            start = (x * Z + k) * half
            copies.append(
                pltpu.make_async_copy(
                    w.at[share_rows, start : start + half],
                    buffer.at[k, :, x * half : (x + 1) * half],
                    share_sems.at[k, x],
                )
            )
    for copy in copies:
        copy.start()
    first = (lax.axis_index("x_lo") * Y + lax.axis_index("y")) * TOK
    vocab = embed.shape[0]
    spot = lax.broadcasted_iota(jnp.int32, (VAR, TOK), 0)
    lane = lax.broadcasted_iota(jnp.int32, (VAR, TOK), 1)
    word_spot = lax.broadcasted_iota(jnp.int32, (VAR, vocab), 0)
    word = lax.broadcasted_iota(jnp.int32, (VAR, vocab), 1)
    places = jnp.zeros((VAR, TOK), f32)
    words = jnp.zeros((VAR, vocab), f32)
    for j in range(VAR):
        place = pos[j] - first
        places = jnp.where((spot == j) & (lane == place), 1.0, places)
        new = jnp.where(word == base[j], 1.0, 0.0)
        old = jnp.where(word == ids[place], 1.0, 0.0)
        words = jnp.where(word_spot == j, new - old, words)
    places = places.astype(bf16)
    change = jnp.dot(words.astype(bf16), embed[...], preferred_element_type=f32)
    picked = jnp.dot(places, hidden[...], preferred_element_type=f32)
    changed_rows = (picked + change).astype(bf16)
    rows[:TOK] = hidden[...]
    rows[TOK:] = changed_rows
    spots[...] = places
    for copy in copies:
        copy.wait()
    share_copy = pltpu.make_async_copy(buffer, share, sems.at[2])
    share_copy.start()
    first_copy = pltpu.make_async_copy(spots, onehot, sems.at[0])
    first_copy.start()
    contract = (((0,), (0,)), ((), ()))
    placed = lax.dot_general(places, changed_rows, contract, preferred_element_type=f32)
    ones = jnp.ones((VAR, hidden.shape[1]), bf16)
    changed = lax.dot_general(places, ones, contract, preferred_element_type=f32)
    block[...] = jnp.where(changed > 0.5, placed, hidden[...].astype(f32)).astype(bf16)
    second_copy = pltpu.make_async_copy(block, variant, sems.at[1])
    second_copy.start()
    first_copy.wait()
    second_copy.wait()
    share_copy.wait()


def make_variant(pos, base, ids, hidden, embed, w):
    width = hidden.shape[1]
    shape = (Z, w.shape[0] // BLOCKS, w.shape[1] // Z)
    args = (pos, base, ids, hidden, embed, w)
    smem = pl.BlockSpec(memory_space=pltpu.SMEM)
    return pl.pallas_call(
        variant_kernel,
        out_shape=(
            jax.ShapeDtypeStruct((ROWS, width), bf16),
            pltpu.HBM((VAR, TOK), bf16),
            pltpu.HBM((TOK, width), bf16),
            pltpu.HBM(shape, bf16),
        ),
        in_specs=[smem, smem, smem, vmem(), vmem(), hbm()],
        out_specs=(vmem(), hbm(), hbm(), hbm()),
        scratch_shapes=[
            pltpu.VMEM((VAR, TOK), bf16),
            pltpu.VMEM((TOK, width), bf16),
            pltpu.VMEM(shape, bf16),
            pltpu.SemaphoreType.DMA((3,)),
            pltpu.SemaphoreType.DMA((Z, X_HI)),
        ],
        compiler_params=limit(4),
    )(*(pltpu.with_memory_space_constraint(v, pltpu.HBM) for v in args))


def column_copies(ks, w, send, own, sems):
    z, core, x_hi = lax.axis_index("z"), lax.axis_index("core"), lax.axis_index("x_hi")
    copies = []
    for index, (whose, out) in enumerate(((1 - core, send), (core, own))):
        for i, k in enumerate(ks):
            for xr in range(X_HI):
                head_pair = lax.rem(x_hi + xr, X_HI) * Z + lax.rem(z + k, Z)
                slot = i * X_HI + xr
                start = pl.multiple_of((head_pair * 2 + whose) * QKV, HD)
                copies.append(
                    pltpu.make_async_copy(
                        w.at[:, pl.ds(start, QKV)],
                        out.at[:, slot * QKV : (slot + 1) * QKV],
                        sems.at[index, slot],
                    )
                )
    return copies


def columns_kernel(ks, w, send, own, sems):
    copies = column_copies(ks, w, send, own, sems)
    for copy in copies:
        copy.start()
    for copy in copies:
        copy.wait()


def pick_columns(ks, w):
    columns = jax.ShapeDtypeStruct((w.shape[0], len(ks) * X_HI * QKV), bf16)
    return pl.pallas_call(
        functools.partial(columns_kernel, ks),
        out_shape=(columns, columns),
        in_specs=[hbm()],
        out_specs=(vmem(), vmem()),
        scratch_shapes=[pltpu.SemaphoreType.DMA((2, len(ks) * X_HI))],
        compiler_params=limit(12),
    )(pltpu.with_memory_space_constraint(w, pltpu.HBM))


def two_rows(row, width):
    high = row.astype(bf16)
    low = (row - high.astype(f32)).astype(bf16)
    line = lax.broadcasted_iota(jnp.int32, (16, width), 0)
    both = jnp.where(line == 0, high.astype(f32), jnp.where(line == 1, low.astype(f32), 0.0))
    return both.astype(bf16)


def one_row(rows):
    return jnp.sum(rows.astype(f32), axis=0, keepdims=True)


def partial_kernel(ks, own, sis, gains, w_own, w_sis, *outs):
    width = X_HI * QKV
    core = lax.axis_index("core")
    own_rows, sis_rows = own[...].astype(f32), sis[...].astype(f32)
    left, right = gains[:, :TOK].astype(f32), gains[:, TOK:].astype(f32)
    x_own = (own_rows * jnp.where(core == 0, left, right)).astype(bf16)
    x_sis = (sis_rows * jnp.where(core == 0, right, left)).astype(bf16)
    squares = jnp.sum(own_rows * own_rows + sis_rows * sis_rows, axis=1, keepdims=True)
    line = lax.broadcasted_iota(jnp.int32, (ROWS, QKV), 0)
    lane = lax.broadcasted_iota(jnp.int32, (ROWS, QKV), 1)
    row = jnp.sum(jnp.where(line == lane, squares, 0.0), axis=0, keepdims=True)
    tail = two_rows(row, QKV)

    def product(slot, count):
        cols = slice(slot * QKV, (slot + count) * QKV)
        acc = jnp.dot(x_own, w_own[:, cols], preferred_element_type=f32)
        acc = acc + jnp.dot(x_sis, w_sis[:, cols], preferred_element_type=f32)
        return acc.astype(bf16)

    def full(slot, out):
        out[:ROWS, :] = product(slot, X_HI)
        out[ROWS:, :QKV] = tail
        out[ROWS:, QKV:] = tail

    if ks == FIRST:
        for xr, out in enumerate(outs):
            out[:ROWS, :] = product(xr, 1)
            out[ROWS:, :] = tail
    else:
        outs, buffer, sems = outs[:-2], outs[-2], outs[-1]
        copies = []
        last = len(ks) - 1
        for i in range(last):
            full(i * X_HI, buffer.at[i])
            copies.append(pltpu.make_async_copy(buffer.at[i], outs[i], sems.at[i]))
            copies[i].start()
        full(last * X_HI, buffer.at[last])
        for xr in range(X_HI):
            half = buffer.at[last, :, xr * QKV : (xr + 1) * QKV]
            copies.append(pltpu.make_async_copy(half, outs[last + xr], sems.at[last + xr]))
            copies[last + xr].start()
        for copy in copies:
            copy.wait()


def partials(ks, own, sis, gains, w_own, w_sis):
    half = jax.ShapeDtypeStruct((SUM_ROWS, QKV), bf16)
    full = jax.ShapeDtypeStruct((SUM_ROWS, X_HI * QKV), bf16)
    if ks == FIRST:
        shapes, specs, scratch = (half, half), (vmem(), vmem()), []
    else:
        shapes = (pltpu.HBM(full.shape, bf16),) * (len(ks) - 1) + (pltpu.HBM(half.shape, bf16),) * 2
        specs = (hbm(),) * (len(ks) + 1)
        scratch = [
            pltpu.VMEM((len(ks), *full.shape), bf16),
            pltpu.SemaphoreType.DMA((len(ks) + 1,)),
        ]
    return pl.pallas_call(
        functools.partial(partial_kernel, ks),
        out_shape=shapes,
        in_specs=[vmem()] * 5,
        out_specs=specs,
        scratch_shapes=scratch,
        compiler_params=limit(20),
        cost_estimate=pl.CostEstimate(
            flops=4 * ROWS * w_own.size, bytes_accessed=8 * w_own.size, transcendentals=0
        ),
    )(own, sis, gains, w_own, w_sis)


def store_sum(out, cols, terms):
    body = sum(term[:ROWS].astype(f32) for term in terms)
    row = sum(one_row(term[ROWS:]) for term in terms)
    out[:ROWS, cols] = body.astype(bf16)
    out[ROWS:, cols] = two_rows(row, row.shape[1])


def first_kernel(up, down, near_up, near_down, out_up, out_down):
    left, right = slice(0, QKV), slice(QKV, 2 * QKV)
    store_sum(out_up, left, [up[...], near_up[:, left]])
    out_up[:, right] = near_up[:, right]
    out_down[:, left] = near_down[:, left]
    store_sum(out_down, right, [down[...], near_down[:, right]])


def next_kernel(up, down, near_up, near_down, out_up, out_down):
    every = slice(0, 2 * QKV)
    store_sum(out_up, every, [up[...], near_up[...]])
    store_sum(out_down, every, [down[...], near_down[...]])


def ring_add(kernel, up, down, near_up, near_down):
    out = jax.ShapeDtypeStruct((SUM_ROWS, X_HI * QKV), bf16)
    return pl.pallas_call(
        kernel,
        out_shape=(out, out),
        in_specs=[vmem()] * 4,
        out_specs=(vmem(), vmem()),
        compiler_params=limit(8),
    )(up, down, near_up, near_down)


def split_kernel(up, down, near_up, near_down, up_own, up_far, down_own, down_far):
    own, far = slice(0, QKV), slice(QKV, 2 * QKV)
    every = slice(0, QKV)
    store_sum(up_own, every, [up[:, own], near_up[:, own]])
    store_sum(up_far, every, [up[:, far], near_up[:, far]])
    store_sum(down_own, every, [down[:, own], near_down[:, own]])
    store_sum(down_far, every, [down[:, far], near_down[:, far]])


def ring_split(up, down, near_up, near_down):
    return pl.pallas_call(
        split_kernel,
        out_shape=(jax.ShapeDtypeStruct((SUM_ROWS, QKV), bf16),) * 4,
        in_specs=[vmem()] * 4,
        out_specs=(vmem(),) * 4,
        compiler_params=limit(8),
    )(up, down, near_up, near_down)


def rotated(x, cosine, sine):
    return x * cosine + pltpu.roll(x, HD // 2, 1) * sine


def finish_kernel(full_width, *refs):
    terms, (cosine, sine, onehot, payload, queries) = refs[:6], refs[6:]
    row = sum(one_row(t[ROWS:]) for t in terms)
    line = lax.broadcasted_iota(jnp.int32, (ROWS, QKV), 0)
    lane = lax.broadcasted_iota(jnp.int32, (ROWS, QKV), 1)
    squares = jnp.sum(jnp.where(line == lane, row, 0.0), axis=1, keepdims=True)
    inv_rms = lax.rsqrt(squares / full_width + epsilon)
    proj = sum(t[:ROWS].astype(f32) for t in terms) * inv_rms
    query = rotated(proj[:, :HD], cosine[...], sine[...]).astype(bf16)
    key = rotated(proj[:, HD : 2 * HD], cosine[...], sine[...]).astype(bf16)
    value = proj[:, 2 * HD :].astype(bf16)
    spots = onehot[...]

    def step(b, carry):
        payload[b, :ROWS, :HD] = key
        payload[b, :ROWS, HD:] = value
        payload[b, ROWS:, :] = spots
        return carry

    lax.fori_loop(0, BLOCKS, step, 0)
    contract = (((0,), (0,)), ((), ()))
    ones = jnp.ones((VAR, HD), bf16)
    changed = lax.dot_general(spots, ones, contract, preferred_element_type=f32)
    placed = lax.dot_general(spots, query[TOK:], contract, preferred_element_type=f32)
    base = query[:TOK]
    queries[:TOK] = base
    queries[TOK:] = jnp.where(changed > 0.5, placed, base.astype(f32)).astype(bf16)


def finish(full_width, terms, cosine, sine, onehot):
    return pl.pallas_call(
        functools.partial(finish_kernel, full_width),
        out_shape=(
            jax.ShapeDtypeStruct((BLOCKS, PAY, 2 * HD), bf16),
            jax.ShapeDtypeStruct((2 * TOK, HD), bf16),
        ),
        in_specs=[vmem()] * 9,
        out_specs=(vmem(), vmem()),
        compiler_params=limit(12),
    )(*terms, cosine, sine, pltpu.with_memory_space_constraint(onehot, pltpu.HBM))


def attend_kernel(queries, blocks, out, scores, peak, denom, total, var_kv, spots):
    my_block = lax.axis_index("x_lo") * Y + lax.axis_index("y")
    scale = 1.0 / HD**0.5
    by_cols = (((1,), (1,)), ((), ()))
    lowest = -jnp.inf
    query = queries[...]

    def score_block(j, own):
        score = lax.dot_general(
            query, blocks[j, :TOK, :HD], by_cols, preferred_element_type=f32
        ) * scale
        gone = jnp.sum(blocks[j, ROWS:, :].astype(f32), axis=0, keepdims=True) > 0.5
        line = lax.broadcasted_iota(jnp.int32, (2 * TOK, TOK), 0)
        hidden = (line >= TOK) & gone
        if own:
            lane = lax.broadcasted_iota(jnp.int32, (2 * TOK, TOK), 1)
            hidden = hidden | (lax.rem(line, TOK) < lane)
        return jnp.where(hidden, lowest, score)

    score = score_block(my_block, True)
    scores[my_block] = score
    peak[...] = jnp.maximum(score[:, :HD], score[:, HD:])

    def first(j, carry):
        score = score_block(j, False)
        scores[j] = score
        peak[...] = jnp.maximum(peak[...], jnp.maximum(score[:, :HD], score[:, HD:]))
        return carry

    lax.fori_loop(0, my_block, first, 0)

    for j in range(BLOCKS):
        var_kv[j * VAR : (j + 1) * VAR, :] = blocks[j, TOK:ROWS, :]
        spots[j * VAR : (j + 1) * VAR, :] = blocks[j, ROWS:, :]
    row = lax.broadcasted_iota(jnp.int32, (TOK, TOK), 0)
    col = lax.broadcasted_iota(jnp.int32, (TOK, TOK), 1)
    reached = lax.dot_general(
        jnp.where(row >= col, 1.0, 0.0).astype(bf16), spots[...], by_cols, preferred_element_type=f32
    )
    source = lax.broadcasted_iota(jnp.int32, (TOK, BLOCKS * VAR), 1) // VAR
    seen = (source < my_block) | ((source == my_block) & (reached > 0.5))
    more = lax.dot_general(
        query[TOK:], var_kv[:, :HD], by_cols, preferred_element_type=f32
    ) * scale
    more = jnp.where(seen, more, lowest)
    peak[TOK:, :] = jnp.maximum(peak[TOK:, :], more)
    top = jnp.max(peak[...], axis=1, keepdims=True)
    peak[...] = jnp.broadcast_to(top, (2 * TOK, HD))

    more = jnp.exp(more - top[TOK:])
    denom[:TOK, :] = jnp.zeros((TOK, HD), f32)
    denom[TOK:, :] = more
    total[:TOK, :] = jnp.zeros((TOK, HD), f32)
    total[TOK:, :] = jnp.dot(more.astype(bf16), var_kv[:, HD:], preferred_element_type=f32)

    def second(j, carry):
        best = peak[...]
        left = jnp.exp(scores[j, :, :HD] - best)
        right = jnp.exp(scores[j, :, HD:] - best)
        denom[...] = denom[...] + left + right
        probs = jnp.concatenate([left.astype(bf16), right.astype(bf16)], axis=1)
        total[...] = total[...] + jnp.dot(
            probs, blocks[j, :TOK, HD:], preferred_element_type=f32
        )
        return carry

    lax.fori_loop(0, my_block + 1, second, 0)
    out[...] = (total[...] / jnp.sum(denom[...], axis=1, keepdims=True)).astype(bf16)


def attend(queries, blocks):
    return pl.pallas_call(
        attend_kernel,
        out_shape=jax.ShapeDtypeStruct((2 * TOK, HD), bf16),
        in_specs=[vmem(), vmem()],
        out_specs=vmem(),
        scratch_shapes=[
            pltpu.VMEM((BLOCKS, 2 * TOK, TOK), f32),
            pltpu.VMEM((2 * TOK, HD), f32),
            pltpu.VMEM((2 * TOK, HD), f32),
            pltpu.VMEM((2 * TOK, HD), f32),
            pltpu.VMEM((BLOCKS * VAR, 2 * HD), bf16),
            pltpu.VMEM((BLOCKS * VAR, TOK), bf16),
        ],
        compiler_params=limit(16),
    )(queries, blocks)


def arrange_kernel(w, out, sems):
    z = lax.axis_index("z")
    copies = []
    for d in range(Z):
        source = lax.rem(z + Z - d, Z)
        copies.append(
            pltpu.make_async_copy(w.at[source], out.at[d * HD : (d + 1) * HD, :], sems.at[d])
        )
    for copy in copies:
        copy.start()
    for copy in copies:
        copy.wait()


def arrange(w):
    return pl.pallas_call(
        arrange_kernel,
        out_shape=jax.ShapeDtypeStruct((Z * HD, w.shape[2]), bf16),
        in_specs=[hbm()],
        out_specs=vmem(),
        scratch_shapes=[pltpu.SemaphoreType.DMA((Z,))],
        compiler_params=limit(4),
    )(pltpu.with_memory_space_constraint(w, pltpu.HBM))


def project_kernel(turned, *refs):
    shards, (keep, near, far), joined = refs[:Z], refs[Z : Z + 3], refs[-1]
    core, x_hi = lax.axis_index("core"), lax.axis_index("x_hi")
    for d in range(Z):
        joined[:, d * HD : (d + 1) * HD] = shards[d][...]

    def product(xr, cr, rows):
        column = (lax.rem(x_hi + xr, X_HI) * CORE + lax.rem(core + cr, CORE)) * TOK
        column = pl.ds(pl.multiple_of(column, TOK), TOK)
        return jnp.dot(joined[rows, :], turned[:, column], preferred_element_type=f32)

    size = 128

    def step(i, carry):
        rows = pl.ds(pl.multiple_of(i * size, size), size)
        for xr in range(X_HI):
            near[rows, xr * TOK : (xr + 1) * TOK] = product(xr, 1, rows).astype(bf16)
        keep[rows, :] = product(0, 0, rows)
        far[rows, :] = product(1, 0, rows)
        return carry

    lax.fori_loop(0, 2 * TOK // size, step, 0)


def project(w, shards):
    rows = shards[0].shape[0]
    return pl.pallas_call(
        project_kernel,
        out_shape=(
            jax.ShapeDtypeStruct((rows, TOK), f32),
            jax.ShapeDtypeStruct((rows, 2 * TOK), bf16),
            jax.ShapeDtypeStruct((rows, TOK), f32),
        ),
        in_specs=[vmem()] * (1 + Z),
        out_specs=(vmem(),) * 3,
        scratch_shapes=[pltpu.VMEM((rows, Z * HD), bf16)],
        compiler_params=limit(16),
    )(w, *shards)


def shards(hidden, gain, embed, qkv_weight, out_weight, ref_ids, var_pos, var_base):
    tok_rows, width_part = hidden.shape
    full_width = out_weight.shape[1]
    x_hi, z, core = lax.axis_index("x_hi"), lax.axis_index("z"), lax.axis_index("core")
    my_block = lax.axis_index("x_lo") * Y + lax.axis_index("y")
    chip_slice = x_hi * Z + z

    with jax.named_scope("inputs"):
        rows, onehot, variant, share = make_variant(
            var_pos, var_base, ref_ids, hidden, embed, out_weight
        )
        rows, qkv_weight = lax.optimization_barrier((rows, qkv_weight))
        rows_sis = shift(rows, "core", CORE, 1)
        send_first, own_first = pick_columns(FIRST, qkv_weight)
        sis_first = shift(send_first, "core", CORE, 1)
        rows_sis, sis_first, qkv_weight, share = lax.optimization_barrier(
            (rows_sis, sis_first, qkv_weight, share)
        )
        send_second, own_second = pick_columns(SECOND, qkv_weight)
        sis_second = shift(send_second, "core", CORE, 1)
        shared = lax.all_to_all(share, "z", 0, 0, tiled=True)
        start = chip_slice * 2 * width_part
        gains = lax.dynamic_slice(gain.reshape(1, full_width), (0, start), (1, 2 * width_part))

    with jax.named_scope("projection"):
        sis_first = pltpu.with_memory_space_constraint(sis_first, pltpu.HBM)
        up, down = partials(FIRST, rows, rows_sis, gains, own_first, sis_first)
        up, down = shift(up, "z", Z, 1), shift(down, "z", Z, -1)
        parts = partials(SECOND, rows, rows_sis, gains, own_second, sis_second)
        near_up = pltpu.with_memory_space_constraint(parts[0], pltpu.HBM)
        near_down = pltpu.with_memory_space_constraint(parts[1], pltpu.HBM)
        up, down, shared, near_up = lax.optimization_barrier((up, down, shared, near_up))
        out_w = lax.all_gather(shared, CTX, axis=1, tiled=True)
        own_term, far_term = parts[-2:]
        far_term = shift(far_term, "x_hi", X_HI, 1)
        parts = dict(zip(SECOND, parts))
        up, down = ring_add(first_kernel, up, down, near_up, near_down)
        up, down = shift(up, "z", Z, 1), shift(down, "z", Z, -1)
        near_up = pltpu.with_memory_space_constraint(parts[2], pltpu.HBM)
        near_down = pltpu.with_memory_space_constraint(parts[6], pltpu.HBM)
        up, down = ring_add(next_kernel, up, down, near_up, near_down)
        up, down = shift(up, "z", Z, 1), shift(down, "z", Z, -1)
        up, down, far_term = lax.optimization_barrier((up, down, far_term))
        up, up_far, down, down_far = ring_split(up, down, parts[1], parts[7])
        up, down = shift(up, "z", Z, 1), shift(down, "z", Z, -1)
        up_far, down_far = shift_diagonal(up_far, 1), shift_diagonal(down_far, -1)
        terms = (up, down, up_far, down_far, own_term, far_term)

    with jax.named_scope("tables"):
        positions = jnp.concatenate([my_block * tok_rows + jnp.arange(tok_rows), var_pos])
        exponent = jnp.arange(HD // 2).astype(f32) * (-2.0 / HD)
        inv_freq = jnp.power(f32(rope_base), exponent)
        angle = positions.astype(f32)[:, None] * inv_freq[None, :]
        cosine, sine = jnp.cos(angle), jnp.sin(angle)
        cosine = jnp.concatenate([cosine, cosine], axis=1)
        sine = jnp.concatenate([-sine, sine], axis=1)

    with jax.named_scope("attention"):
        payload, queries = finish(full_width, terms, cosine, sine, onehot)
        blocks = lax.all_to_all(payload, CTX, 0, 0, tiled=True)
        attn = attend(queries, blocks)
        attn, out_w = lax.optimization_barrier((attn, out_w))

    with jax.named_scope("output"):
        pieces = [attn] + [None] * (Z - 1)
        for d in (1, 2, 3):
            pieces[d] = shift(pieces[d - 1], "z", Z, 1)
            pieces[Z - d] = shift(pieces[(Z - d + 1) % Z], "z", Z, -1)
            if d == 1:
                pieces[Z // 2] = shift(attn, "z", Z, Z // 2)
                out_w, pieces[1], pieces[7] = lax.optimization_barrier(
                    (arrange(out_w), pieces[1], pieces[7])
                )
        keep, near, far = project(out_w, pieces)
        near = shift(near, "core", CORE, 1).astype(f32)
        far = (far + near[:, width_part:]).astype(bf16)
        far = shift(far, "x_hi", X_HI, 1).astype(f32)
        branch = (keep + near[:, :width_part] + far).reshape(2, tok_rows, width_part)
        seqs = jnp.stack([hidden, variant]).astype(f32)
        return (seqs + branch).astype(bf16)


def solution(mesh):
    fine = Mesh(mesh.devices.reshape(X_HI, Z, CORE, X_LO, Y), (*FSDP, *CTX))
    in_specs = (
        P(CTX, FSDP),
        P(),
        P(None, FSDP),
        P(FSDP, None),
        P(FSDP, None),
        P(CTX),
        P(CTX),
        P(CTX),
    )
    out_specs = P(None, CTX, FSDP)
    return jax.shard_map(shards, mesh=fine, in_specs=in_specs, out_specs=out_specs, check_vma=False)
```

```python
import functools

import jax
import jax.numpy as jnp
from jax import lax
from jax.experimental import pallas as pl
from jax.experimental.pallas import tpu as pltpu
from jax.sharding import Mesh, PartitionSpec as P

epsilon = 1e-05
rope_base = 10000.0

X_HI, Z, CORE, X_LO, Y = 2, 8, 2, 2, 4
FSDP = ("x_hi", "z", "core")
CTX = ("x_lo", "y")
BLOCKS = X_LO * Y
HD = 128
QKV = 3 * HD
TOK = 256
VAR = 16
ROWS = TOK + VAR
SUM_ROWS = ROWS + 16
PAY = ROWS + VAR
bf16 = jnp.bfloat16
f32 = jnp.float32
MIB = 1024 * 1024


def shift(value, axis, size, distance):
    return lax.ppermute(value, axis, [(i, (i + distance) % size) for i in range(size)])


def vmem():
    return pl.BlockSpec(memory_space=pltpu.VMEM)


def anywhere():
    return pl.BlockSpec(memory_space=pl.ANY)


def hbm():
    return pl.BlockSpec(memory_space=pltpu.HBM)


def limit(mib):
    return pltpu.CompilerParams(vmem_limit_bytes=mib * MIB)


FIRST = (4,)
SECOND = (3, 5, 2, 6, 1, 7, 0)


def variant_kernel(
    pos, base, ids, hidden, embed, w, rows, onehot, variant, share, spots, block, buffer, sems, share_sems
):
    my_block = lax.axis_index("x_lo") * Y + lax.axis_index("y")
    size, half = buffer.shape[1], buffer.shape[2] // X_HI
    share_rows = pl.ds(pl.multiple_of(my_block * size, size), size)
    copies = []
    for k in range(Z):
        for x in range(X_HI):
            start = (x * Z + k) * half
            copies.append(
                pltpu.make_async_copy(
                    w.at[share_rows, start : start + half],
                    buffer.at[k, :, x * half : (x + 1) * half],
                    share_sems.at[k, x],
                )
            )
    for copy in copies:
        copy.start()
    first = (lax.axis_index("x_lo") * Y + lax.axis_index("y")) * TOK
    vocab = embed.shape[0]
    spot = lax.broadcasted_iota(jnp.int32, (VAR, TOK), 0)
    lane = lax.broadcasted_iota(jnp.int32, (VAR, TOK), 1)
    word_spot = lax.broadcasted_iota(jnp.int32, (VAR, vocab), 0)
    word = lax.broadcasted_iota(jnp.int32, (VAR, vocab), 1)
    places = jnp.zeros((VAR, TOK), f32)
    words = jnp.zeros((VAR, vocab), f32)
    for j in range(VAR):
        place = pos[j] - first
        places = jnp.where((spot == j) & (lane == place), 1.0, places)
        new = jnp.where(word == base[j], 1.0, 0.0)
        old = jnp.where(word == ids[place], 1.0, 0.0)
        words = jnp.where(word_spot == j, new - old, words)
    places = places.astype(bf16)
    change = jnp.dot(words.astype(bf16), embed[...], preferred_element_type=f32)
    picked = jnp.dot(places, hidden[...], preferred_element_type=f32)
    changed_rows = (picked + change).astype(bf16)
    rows[:TOK] = hidden[...]
    rows[TOK:] = changed_rows
    spots[...] = places
    for copy in copies:
        copy.wait()
    share_copy = pltpu.make_async_copy(buffer, share, sems.at[2])
    share_copy.start()
    first_copy = pltpu.make_async_copy(spots, onehot, sems.at[0])
    first_copy.start()
    contract = (((0,), (0,)), ((), ()))
    placed = lax.dot_general(places, changed_rows, contract, preferred_element_type=f32)
    ones = jnp.ones((VAR, hidden.shape[1]), bf16)
    changed = lax.dot_general(places, ones, contract, preferred_element_type=f32)
    block[...] = jnp.where(changed > 0.5, placed, hidden[...].astype(f32)).astype(bf16)
    second_copy = pltpu.make_async_copy(block, variant, sems.at[1])
    second_copy.start()
    first_copy.wait()
    second_copy.wait()
    share_copy.wait()


def make_variant(pos, base, ids, hidden, embed, w):
    width = hidden.shape[1]
    shape = (Z, w.shape[0] // BLOCKS, w.shape[1] // Z)
    args = (pos, base, ids, hidden, embed, w)
    smem = pl.BlockSpec(memory_space=pltpu.SMEM)
    return pl.pallas_call(
        variant_kernel,
        out_shape=(
            jax.ShapeDtypeStruct((ROWS, width), bf16),
            pltpu.HBM((VAR, TOK), bf16),
            pltpu.HBM((TOK, width), bf16),
            pltpu.HBM(shape, bf16),
        ),
        in_specs=[smem, smem, smem, vmem(), vmem(), hbm()],
        out_specs=(vmem(), hbm(), hbm(), hbm()),
        scratch_shapes=[
            pltpu.VMEM((VAR, TOK), bf16),
            pltpu.VMEM((TOK, width), bf16),
            pltpu.VMEM(shape, bf16),
            pltpu.SemaphoreType.DMA((3,)),
            pltpu.SemaphoreType.DMA((Z, X_HI)),
        ],
        compiler_params=limit(4),
    )(*(pltpu.with_memory_space_constraint(v, pltpu.HBM) for v in args))


def column_copies(ks, w, send, own, sems):
    z, core, x_hi = lax.axis_index("z"), lax.axis_index("core"), lax.axis_index("x_hi")
    copies = []
    for index, (whose, out) in enumerate(((1 - core, send), (core, own))):
        for i, k in enumerate(ks):
            for xr in range(X_HI):
                head_pair = lax.rem(x_hi + xr, X_HI) * Z + lax.rem(z + k, Z)
                slot = i * X_HI + xr
                start = pl.multiple_of((head_pair * 2 + whose) * QKV, HD)
                copies.append(
                    pltpu.make_async_copy(
                        w.at[:, pl.ds(start, QKV)],
                        out.at[:, slot * QKV : (slot + 1) * QKV],
                        sems.at[index, slot],
                    )
                )
    return copies


def columns_kernel(ks, w, send, own, sems):
    copies = column_copies(ks, w, send, own, sems)
    for copy in copies:
        copy.start()
    for copy in copies:
        copy.wait()


def pick_columns(ks, w):
    columns = jax.ShapeDtypeStruct((w.shape[0], len(ks) * X_HI * QKV), bf16)
    return pl.pallas_call(
        functools.partial(columns_kernel, ks),
        out_shape=(columns, columns),
        in_specs=[hbm()],
        out_specs=(vmem(), vmem()),
        scratch_shapes=[pltpu.SemaphoreType.DMA((2, len(ks) * X_HI))],
        compiler_params=limit(12),
    )(pltpu.with_memory_space_constraint(w, pltpu.HBM))


def two_rows(row, width):
    high = row.astype(bf16)
    low = (row - high.astype(f32)).astype(bf16)
    line = lax.broadcasted_iota(jnp.int32, (16, width), 0)
    both = jnp.where(line == 0, high.astype(f32), jnp.where(line == 1, low.astype(f32), 0.0))
    return both.astype(bf16)


def one_row(rows):
    return jnp.sum(rows.astype(f32), axis=0, keepdims=True)


def partial_kernel(ks, own, sis, gains, w_own, w_sis, *outs):
    width = X_HI * QKV
    core = lax.axis_index("core")
    own_rows, sis_rows = own[...].astype(f32), sis[...].astype(f32)
    left, right = gains[:, :TOK].astype(f32), gains[:, TOK:].astype(f32)
    x_own = (own_rows * jnp.where(core == 0, left, right)).astype(bf16)
    x_sis = (sis_rows * jnp.where(core == 0, right, left)).astype(bf16)
    squares = jnp.sum(own_rows * own_rows + sis_rows * sis_rows, axis=1, keepdims=True)
    line = lax.broadcasted_iota(jnp.int32, (ROWS, QKV), 0)
    lane = lax.broadcasted_iota(jnp.int32, (ROWS, QKV), 1)
    row = jnp.sum(jnp.where(line == lane, squares, 0.0), axis=0, keepdims=True)
    tail = two_rows(row, QKV)

    def product(slot, count):
        cols = slice(slot * QKV, (slot + count) * QKV)
        acc = jnp.dot(x_own, w_own[:, cols], preferred_element_type=f32)
        acc = acc + jnp.dot(x_sis, w_sis[:, cols], preferred_element_type=f32)
        return acc.astype(bf16)

    def full(slot, out):
        out[:ROWS, :] = product(slot, X_HI)
        out[ROWS:, :QKV] = tail
        out[ROWS:, QKV:] = tail

    if ks == FIRST:
        for xr, out in enumerate(outs):
            out[:ROWS, :] = product(xr, 1)
            out[ROWS:, :] = tail
    else:
        outs, buffer, sems = outs[:-2], outs[-2], outs[-1]
        copies = []
        for i, out in enumerate(outs):
            full(i * X_HI, buffer.at[i])
            copies.append(pltpu.make_async_copy(buffer.at[i], out, sems.at[i]))
            copies[i].start()
        for copy in copies:
            copy.wait()


def partials(ks, own, sis, gains, w_own, w_sis):
    half = jax.ShapeDtypeStruct((SUM_ROWS, QKV), bf16)
    full = jax.ShapeDtypeStruct((SUM_ROWS, X_HI * QKV), bf16)
    if ks == FIRST:
        shapes, specs, scratch = (half, half), (vmem(), vmem()), []
    else:
        shapes, specs = (pltpu.HBM(full.shape, bf16),) * len(ks), (hbm(),) * len(ks)
        scratch = [pltpu.VMEM((len(ks), *full.shape), bf16), pltpu.SemaphoreType.DMA((len(ks),))]
    return pl.pallas_call(
        functools.partial(partial_kernel, ks),
        out_shape=shapes,
        in_specs=[vmem()] * 5,
        out_specs=specs,
        scratch_shapes=scratch,
        compiler_params=limit(20),
        cost_estimate=pl.CostEstimate(
            flops=4 * ROWS * w_own.size, bytes_accessed=8 * w_own.size, transcendentals=0
        ),
    )(own, sis, gains, w_own, w_sis)


def store_sum(out, cols, terms):
    body = sum(term[:ROWS].astype(f32) for term in terms)
    row = sum(one_row(term[ROWS:]) for term in terms)
    out[:ROWS, cols] = body.astype(bf16)
    out[ROWS:, cols] = two_rows(row, row.shape[1])


def first_kernel(up, down, near_up, near_down, out_up, out_down):
    left, right = slice(0, QKV), slice(QKV, 2 * QKV)
    store_sum(out_up, left, [up[...], near_up[:, left]])
    out_up[:, right] = near_up[:, right]
    out_down[:, left] = near_down[:, left]
    store_sum(out_down, right, [down[...], near_down[:, right]])


def next_kernel(up, down, near_up, near_down, out_up, out_down):
    every = slice(0, 2 * QKV)
    store_sum(out_up, every, [up[...], near_up[...]])
    store_sum(out_down, every, [down[...], near_down[...]])


def ring_add(kernel, up, down, near_up, near_down):
    out = jax.ShapeDtypeStruct((SUM_ROWS, X_HI * QKV), bf16)
    return pl.pallas_call(
        kernel,
        out_shape=(out, out),
        in_specs=[vmem()] * 4,
        out_specs=(vmem(), vmem()),
        compiler_params=limit(8),
    )(up, down, near_up, near_down)


def last_kernel(up, down, near, mine, other):
    own, far = slice(0, QKV), slice(QKV, 2 * QKV)
    terms = [up, down, near]
    mine[:ROWS] = sum(term[:ROWS, own].astype(f32) for term in terms)
    row = sum(one_row(term[ROWS:, own]) for term in terms)
    mine[ROWS:] = jnp.broadcast_to(row, (8, QKV))
    store_sum(other, slice(0, QKV), [term[:, far] for term in terms])


def ring_last(up, down, near):
    return pl.pallas_call(
        last_kernel,
        out_shape=(
            jax.ShapeDtypeStruct((ROWS + 8, QKV), f32),
            jax.ShapeDtypeStruct((SUM_ROWS, QKV), bf16),
        ),
        in_specs=[vmem()] * 3,
        out_specs=(vmem(), vmem()),
        compiler_params=limit(8),
    )(up, down, near)


def rotated(x, cosine, sine):
    return x * cosine + pltpu.roll(x, HD // 2, 1) * sine


def finish_kernel(full_width, mine, other, cosine, sine, onehot, payload, queries):
    row = mine[ROWS : ROWS + 1, :] + one_row(other[ROWS:, :])
    line = lax.broadcasted_iota(jnp.int32, (ROWS, QKV), 0)
    lane = lax.broadcasted_iota(jnp.int32, (ROWS, QKV), 1)
    squares = jnp.sum(jnp.where(line == lane, row, 0.0), axis=1, keepdims=True)
    inv_rms = lax.rsqrt(squares / full_width + epsilon)
    proj = (mine[:ROWS, :] + other[:ROWS, :].astype(f32)) * inv_rms
    query = rotated(proj[:, :HD], cosine[...], sine[...]).astype(bf16)
    key = rotated(proj[:, HD : 2 * HD], cosine[...], sine[...]).astype(bf16)
    value = proj[:, 2 * HD :].astype(bf16)
    spots = onehot[...]

    def step(b, carry):
        payload[b, :ROWS, :HD] = key
        payload[b, :ROWS, HD:] = value
        payload[b, ROWS:, :] = spots
        return carry

    lax.fori_loop(0, BLOCKS, step, 0)
    contract = (((0,), (0,)), ((), ()))
    ones = jnp.ones((VAR, HD), bf16)
    changed = lax.dot_general(spots, ones, contract, preferred_element_type=f32)
    placed = lax.dot_general(spots, query[TOK:], contract, preferred_element_type=f32)
    base = query[:TOK]
    queries[:TOK] = base
    queries[TOK:] = jnp.where(changed > 0.5, placed, base.astype(f32)).astype(bf16)


def finish(full_width, mine, other, cosine, sine, onehot):
    return pl.pallas_call(
        functools.partial(finish_kernel, full_width),
        out_shape=(
            jax.ShapeDtypeStruct((BLOCKS, PAY, 2 * HD), bf16),
            jax.ShapeDtypeStruct((2 * TOK, HD), bf16),
        ),
        in_specs=[vmem()] * 5,
        out_specs=(vmem(), vmem()),
        compiler_params=limit(12),
    )(mine, other, cosine, sine, pltpu.with_memory_space_constraint(onehot, pltpu.HBM))


def attend_kernel(queries, blocks, out, scores, peak, denom, total, var_kv, spots):
    my_block = lax.axis_index("x_lo") * Y + lax.axis_index("y")
    scale = 1.0 / HD**0.5
    by_cols = (((1,), (1,)), ((), ()))
    lowest = -jnp.inf
    query = queries[...]

    def score_block(j, own):
        score = lax.dot_general(
            query, blocks[j, :TOK, :HD], by_cols, preferred_element_type=f32
        ) * scale
        gone = jnp.sum(blocks[j, ROWS:, :].astype(f32), axis=0, keepdims=True) > 0.5
        line = lax.broadcasted_iota(jnp.int32, (2 * TOK, TOK), 0)
        hidden = (line >= TOK) & gone
        if own:
            lane = lax.broadcasted_iota(jnp.int32, (2 * TOK, TOK), 1)
            hidden = hidden | (lax.rem(line, TOK) < lane)
        return jnp.where(hidden, lowest, score)

    score = score_block(my_block, True)
    scores[my_block] = score
    peak[...] = jnp.maximum(score[:, :HD], score[:, HD:])

    def first(j, carry):
        score = score_block(j, False)
        scores[j] = score
        peak[...] = jnp.maximum(peak[...], jnp.maximum(score[:, :HD], score[:, HD:]))
        return carry

    lax.fori_loop(0, my_block, first, 0)

    for j in range(BLOCKS):
        var_kv[j * VAR : (j + 1) * VAR, :] = blocks[j, TOK:ROWS, :]
        spots[j * VAR : (j + 1) * VAR, :] = blocks[j, ROWS:, :]
    row = lax.broadcasted_iota(jnp.int32, (TOK, TOK), 0)
    col = lax.broadcasted_iota(jnp.int32, (TOK, TOK), 1)
    reached = lax.dot_general(
        jnp.where(row >= col, 1.0, 0.0).astype(bf16), spots[...], by_cols, preferred_element_type=f32
    )
    source = lax.broadcasted_iota(jnp.int32, (TOK, BLOCKS * VAR), 1) // VAR
    seen = (source < my_block) | ((source == my_block) & (reached > 0.5))
    more = lax.dot_general(
        query[TOK:], var_kv[:, :HD], by_cols, preferred_element_type=f32
    ) * scale
    more = jnp.where(seen, more, lowest)
    peak[TOK:, :] = jnp.maximum(peak[TOK:, :], more)
    top = jnp.max(peak[...], axis=1, keepdims=True)
    peak[...] = jnp.broadcast_to(top, (2 * TOK, HD))

    more = jnp.exp(more - top[TOK:])
    denom[:TOK, :] = jnp.zeros((TOK, HD), f32)
    denom[TOK:, :] = more
    total[:TOK, :] = jnp.zeros((TOK, HD), f32)
    total[TOK:, :] = jnp.dot(more.astype(bf16), var_kv[:, HD:], preferred_element_type=f32)

    def second(j, carry):
        best = peak[...]
        left = jnp.exp(scores[j, :, :HD] - best)
        right = jnp.exp(scores[j, :, HD:] - best)
        denom[...] = denom[...] + left + right
        probs = jnp.concatenate([left.astype(bf16), right.astype(bf16)], axis=1)
        total[...] = total[...] + jnp.dot(
            probs, blocks[j, :TOK, HD:], preferred_element_type=f32
        )
        return carry

    lax.fori_loop(0, my_block + 1, second, 0)
    out[...] = (total[...] / jnp.sum(denom[...], axis=1, keepdims=True)).astype(bf16)


def attend(queries, blocks):
    return pl.pallas_call(
        attend_kernel,
        out_shape=jax.ShapeDtypeStruct((2 * TOK, HD), bf16),
        in_specs=[vmem(), vmem()],
        out_specs=vmem(),
        scratch_shapes=[
            pltpu.VMEM((BLOCKS, 2 * TOK, TOK), f32),
            pltpu.VMEM((2 * TOK, HD), f32),
            pltpu.VMEM((2 * TOK, HD), f32),
            pltpu.VMEM((2 * TOK, HD), f32),
            pltpu.VMEM((BLOCKS * VAR, 2 * HD), bf16),
            pltpu.VMEM((BLOCKS * VAR, TOK), bf16),
        ],
        compiler_params=limit(16),
    )(queries, blocks)


def arrange_kernel(w, out, sems):
    z = lax.axis_index("z")
    copies = []
    for d in range(Z):
        source = lax.rem(z + Z - d, Z)
        copies.append(
            pltpu.make_async_copy(w.at[source], out.at[d * HD : (d + 1) * HD, :], sems.at[d])
        )
    for copy in copies:
        copy.start()
    for copy in copies:
        copy.wait()


def arrange(w):
    return pl.pallas_call(
        arrange_kernel,
        out_shape=jax.ShapeDtypeStruct((Z * HD, w.shape[2]), bf16),
        in_specs=[hbm()],
        out_specs=vmem(),
        scratch_shapes=[pltpu.SemaphoreType.DMA((Z,))],
        compiler_params=limit(4),
    )(pltpu.with_memory_space_constraint(w, pltpu.HBM))


def project_kernel(turned, *refs):
    shards, (rest, keep, near, far, joined) = refs[:Z], refs[Z:]
    core, x_hi = lax.axis_index("core"), lax.axis_index("x_hi")
    for d in range(Z):
        joined[: shards[d].shape[0], d * HD : (d + 1) * HD] = shards[d][...]
    middle = slice(Z // 2 * HD, (Z // 2 + 1) * HD)
    joined[rest.shape[0] :, middle] = rest[...]

    def product(xr, cr, rows):
        column = (lax.rem(x_hi + xr, X_HI) * CORE + lax.rem(core + cr, CORE)) * TOK
        column = pl.ds(pl.multiple_of(column, TOK), TOK)
        return jnp.dot(joined[rows, :], turned[:, column], preferred_element_type=f32)

    size = 128

    def step(i, carry):
        rows = pl.ds(pl.multiple_of(i * size, size), size)
        for xr in range(X_HI):
            near[rows, xr * TOK : (xr + 1) * TOK] = product(xr, 1, rows).astype(bf16)
        keep[rows, :] = product(0, 0, rows)
        far[rows, :] = product(1, 0, rows)
        return carry

    lax.fori_loop(0, 2 * TOK // size, step, 0)


def project(w, shards):
    rows = shards[0].shape[0]
    return pl.pallas_call(
        project_kernel,
        out_shape=(
            jax.ShapeDtypeStruct((rows, TOK), f32),
            jax.ShapeDtypeStruct((rows, 2 * TOK), bf16),
            jax.ShapeDtypeStruct((rows, TOK), f32),
        ),
        in_specs=[vmem()] * (2 + Z),
        out_specs=(vmem(),) * 3,
        scratch_shapes=[pltpu.VMEM((rows, Z * HD), bf16)],
        compiler_params=limit(16),
    )(w, *shards)


def shards(hidden, gain, embed, qkv_weight, out_weight, ref_ids, var_pos, var_base):
    tok_rows, width_part = hidden.shape
    full_width = out_weight.shape[1]
    x_hi, z, core = lax.axis_index("x_hi"), lax.axis_index("z"), lax.axis_index("core")
    my_block = lax.axis_index("x_lo") * Y + lax.axis_index("y")
    chip_slice = x_hi * Z + z

    with jax.named_scope("inputs"):
        rows, onehot, variant, share = make_variant(
            var_pos, var_base, ref_ids, hidden, embed, out_weight
        )
        rows, qkv_weight = lax.optimization_barrier((rows, qkv_weight))
        rows_sis = shift(rows, "core", CORE, 1)
        send_first, own_first = pick_columns(FIRST, qkv_weight)
        sis_first = shift(send_first, "core", CORE, 1)
        rows_sis, sis_first, qkv_weight, share = lax.optimization_barrier(
            (rows_sis, sis_first, qkv_weight, share)
        )
        send_second, own_second = pick_columns(SECOND, qkv_weight)
        sis_second = shift(send_second, "core", CORE, 1)
        shared = lax.all_to_all(share, "z", 0, 0, tiled=True)
        start = chip_slice * 2 * width_part
        gains = lax.dynamic_slice(gain.reshape(1, full_width), (0, start), (1, 2 * width_part))

    with jax.named_scope("projection"):
        sis_first = pltpu.with_memory_space_constraint(sis_first, pltpu.HBM)
        up, down = partials(FIRST, rows, rows_sis, gains, own_first, sis_first)
        up, down = shift(up, "z", Z, 1), shift(down, "z", Z, -1)
        parts = partials(SECOND, rows, rows_sis, gains, own_second, sis_second)
        near_up = pltpu.with_memory_space_constraint(parts[0], pltpu.HBM)
        near_down = pltpu.with_memory_space_constraint(parts[1], pltpu.HBM)
        up, down, shared, near_up = lax.optimization_barrier((up, down, shared, near_up))
        out_w = lax.all_gather(shared, CTX, axis=1, tiled=True)
        parts = dict(zip(SECOND, parts))
        up, down = ring_add(first_kernel, up, down, near_up, near_down)
        up, down = shift(up, "z", Z, 1), shift(down, "z", Z, -1)
        near_up = pltpu.with_memory_space_constraint(parts[2], pltpu.HBM)
        near_down = pltpu.with_memory_space_constraint(parts[6], pltpu.HBM)
        up, down = ring_add(next_kernel, up, down, near_up, near_down)
        up, down = shift(up, "z", Z, 1), shift(down, "z", Z, -1)
        up, down = ring_add(next_kernel, up, down, parts[1], parts[7])
        up, down = shift(up, "z", Z, 1), shift(down, "z", Z, -1)
        mine, other = ring_last(up, down, parts[0])
        other = shift(other, "x_hi", X_HI, 1)

    with jax.named_scope("tables"):
        positions = jnp.concatenate([my_block * tok_rows + jnp.arange(tok_rows), var_pos])
        exponent = jnp.arange(HD // 2).astype(f32) * (-2.0 / HD)
        inv_freq = jnp.power(f32(rope_base), exponent)
        angle = positions.astype(f32)[:, None] * inv_freq[None, :]
        cosine, sine = jnp.cos(angle), jnp.sin(angle)
        cosine = jnp.concatenate([cosine, cosine], axis=1)
        sine = jnp.concatenate([-sine, sine], axis=1)

    with jax.named_scope("attention"):
        payload, queries = finish(full_width, mine, other, cosine, sine, onehot)
        blocks = lax.all_to_all(payload, CTX, 0, 0, tiled=True)
        attn = attend(queries, blocks)
        attn, out_w = lax.optimization_barrier((attn, out_w))

    with jax.named_scope("output"):
        pieces = [attn] + [None] * (Z - 1)
        for d in (1, 2, 3):
            pieces[d] = shift(pieces[d - 1], "z", Z, 1)
            pieces[Z - d] = shift(pieces[(Z - d + 1) % Z], "z", Z, -1)
            if d == 1:
                out_w, pieces[1], pieces[7] = lax.optimization_barrier(
                    (arrange(out_w), pieces[1], pieces[7])
                )
        first_half = shift(pieces[2][:tok_rows], "z", Z, 2)
        pieces.append(shift(pieces[6][tok_rows:], "z", Z, -2))
        pieces[Z // 2] = first_half
        keep, near, far = project(out_w, pieces)
        near = shift(near, "core", CORE, 1).astype(f32)
        far = (far + near[:, width_part:]).astype(bf16)
        far = shift(far, "x_hi", X_HI, 1).astype(f32)
        branch = (keep + near[:, :width_part] + far).reshape(2, tok_rows, width_part)
        seqs = jnp.stack([hidden, variant]).astype(f32)
        return (seqs + branch).astype(bf16)


def solution(mesh):
    fine = Mesh(mesh.devices.reshape(X_HI, Z, CORE, X_LO, Y), (*FSDP, *CTX))
    in_specs = (
        P(CTX, FSDP),
        P(),
        P(None, FSDP),
        P(FSDP, None),
        P(FSDP, None),
        P(CTX),
        P(CTX),
        P(CTX),
    )
    out_specs = P(None, CTX, FSDP)
    return jax.shard_map(shards, mesh=fine, in_specs=in_specs, out_specs=out_specs, check_vma=False)
```

```python
import functools

import jax
import jax.numpy as jnp
from jax import lax
from jax.experimental import pallas as pl
from jax.experimental.pallas import tpu as pltpu
from jax.sharding import Mesh, PartitionSpec as P

epsilon = 1e-05
rope_base = 10000.0

X_HI, Z, CORE, X_LO, Y = 2, 8, 2, 2, 4
FSDP = ("x_hi", "z", "core")
CTX = ("x_lo", "y")
BLOCKS = X_LO * Y
HD = 128
QKV = 3 * HD
TOK = 256
VAR = 16
ROWS = TOK + VAR
SUM_ROWS = ROWS + 16
PAY = ROWS + VAR
bf16 = jnp.bfloat16
f32 = jnp.float32
MIB = 1024 * 1024


def shift(value, axis, size, distance):
    return lax.ppermute(value, axis, [(i, (i + distance) % size) for i in range(size)])


def vmem():
    return pl.BlockSpec(memory_space=pltpu.VMEM)


def anywhere():
    return pl.BlockSpec(memory_space=pl.ANY)


def hbm():
    return pl.BlockSpec(memory_space=pltpu.HBM)


def limit(mib):
    return pltpu.CompilerParams(vmem_limit_bytes=mib * MIB)


FIRST = (4,)
SECOND = (3, 5, 2, 6, 1, 7, 0)


def variant_kernel(
    pos, base, ids, hidden, embed, w, rows, onehot, variant, share, spots, block, buffer, sems, share_sems
):
    my_block = lax.axis_index("x_lo") * Y + lax.axis_index("y")
    size, half = buffer.shape[1], buffer.shape[2] // X_HI
    share_rows = pl.ds(pl.multiple_of(my_block * size, size), size)
    copies = []
    for k in range(Z):
        for x in range(X_HI):
            start = (x * Z + k) * half
            copies.append(
                pltpu.make_async_copy(
                    w.at[share_rows, start : start + half],
                    buffer.at[k, :, x * half : (x + 1) * half],
                    share_sems.at[k, x],
                )
            )
    for copy in copies:
        copy.start()
    first = (lax.axis_index("x_lo") * Y + lax.axis_index("y")) * TOK
    vocab = embed.shape[0]
    spot = lax.broadcasted_iota(jnp.int32, (VAR, TOK), 0)
    lane = lax.broadcasted_iota(jnp.int32, (VAR, TOK), 1)
    word_spot = lax.broadcasted_iota(jnp.int32, (VAR, vocab), 0)
    word = lax.broadcasted_iota(jnp.int32, (VAR, vocab), 1)
    places = jnp.zeros((VAR, TOK), f32)
    words = jnp.zeros((VAR, vocab), f32)
    for j in range(VAR):
        place = pos[j] - first
        places = jnp.where((spot == j) & (lane == place), 1.0, places)
        new = jnp.where(word == base[j], 1.0, 0.0)
        old = jnp.where(word == ids[place], 1.0, 0.0)
        words = jnp.where(word_spot == j, new - old, words)
    places = places.astype(bf16)
    change = jnp.dot(words.astype(bf16), embed[...], preferred_element_type=f32)
    picked = jnp.dot(places, hidden[...], preferred_element_type=f32)
    changed_rows = (picked + change).astype(bf16)
    rows[:TOK] = hidden[...]
    rows[TOK:] = changed_rows
    spots[...] = places
    for copy in copies:
        copy.wait()
    share_copy = pltpu.make_async_copy(buffer, share, sems.at[2])
    share_copy.start()
    first_copy = pltpu.make_async_copy(spots, onehot, sems.at[0])
    first_copy.start()
    contract = (((0,), (0,)), ((), ()))
    placed = lax.dot_general(places, changed_rows, contract, preferred_element_type=f32)
    ones = jnp.ones((VAR, hidden.shape[1]), bf16)
    changed = lax.dot_general(places, ones, contract, preferred_element_type=f32)
    block[...] = jnp.where(changed > 0.5, placed, hidden[...].astype(f32)).astype(bf16)
    second_copy = pltpu.make_async_copy(block, variant, sems.at[1])
    second_copy.start()
    first_copy.wait()
    second_copy.wait()
    share_copy.wait()


def make_variant(pos, base, ids, hidden, embed, w):
    width = hidden.shape[1]
    shape = (Z, w.shape[0] // BLOCKS, w.shape[1] // Z)
    args = (pos, base, ids, hidden, embed, w)
    smem = pl.BlockSpec(memory_space=pltpu.SMEM)
    return pl.pallas_call(
        variant_kernel,
        out_shape=(
            jax.ShapeDtypeStruct((ROWS, width), bf16),
            pltpu.HBM((VAR, TOK), bf16),
            pltpu.HBM((TOK, width), bf16),
            pltpu.HBM(shape, bf16),
        ),
        in_specs=[smem, smem, smem, vmem(), vmem(), hbm()],
        out_specs=(vmem(), hbm(), hbm(), hbm()),
        scratch_shapes=[
            pltpu.VMEM((VAR, TOK), bf16),
            pltpu.VMEM((TOK, width), bf16),
            pltpu.VMEM(shape, bf16),
            pltpu.SemaphoreType.DMA((3,)),
            pltpu.SemaphoreType.DMA((Z, X_HI)),
        ],
        compiler_params=limit(4),
    )(*(pltpu.with_memory_space_constraint(v, pltpu.HBM) for v in args))


def column_copies(ks, w, send, own, sems):
    z, core, x_hi = lax.axis_index("z"), lax.axis_index("core"), lax.axis_index("x_hi")
    copies = []
    for index, (whose, out) in enumerate(((1 - core, send), (core, own))):
        for i, k in enumerate(ks):
            for xr in range(X_HI):
                head_pair = lax.rem(x_hi + xr, X_HI) * Z + lax.rem(z + k, Z)
                slot = i * X_HI + xr
                start = pl.multiple_of((head_pair * 2 + whose) * QKV, HD)
                copies.append(
                    pltpu.make_async_copy(
                        w.at[:, pl.ds(start, QKV)],
                        out.at[:, slot * QKV : (slot + 1) * QKV],
                        sems.at[index, slot],
                    )
                )
    return copies


def columns_kernel(ks, w, send, own, sems):
    copies = column_copies(ks, w, send, own, sems)
    for copy in copies:
        copy.start()
    for copy in copies:
        copy.wait()


def pick_columns(ks, w):
    columns = jax.ShapeDtypeStruct((w.shape[0], len(ks) * X_HI * QKV), bf16)
    return pl.pallas_call(
        functools.partial(columns_kernel, ks),
        out_shape=(columns, columns),
        in_specs=[hbm()],
        out_specs=(vmem(), vmem()),
        scratch_shapes=[pltpu.SemaphoreType.DMA((2, len(ks) * X_HI))],
        compiler_params=limit(12),
    )(pltpu.with_memory_space_constraint(w, pltpu.HBM))


def two_rows(row, width):
    high = row.astype(bf16)
    low = (row - high.astype(f32)).astype(bf16)
    line = lax.broadcasted_iota(jnp.int32, (16, width), 0)
    both = jnp.where(line == 0, high.astype(f32), jnp.where(line == 1, low.astype(f32), 0.0))
    return both.astype(bf16)


def one_row(rows):
    return jnp.sum(rows.astype(f32), axis=0, keepdims=True)


def partial_kernel(ks, own, sis, gains, w_own, w_sis, *outs):
    width = X_HI * QKV
    core = lax.axis_index("core")
    own_rows, sis_rows = own[...].astype(f32), sis[...].astype(f32)
    left, right = gains[:, :TOK].astype(f32), gains[:, TOK:].astype(f32)
    x_own = (own_rows * jnp.where(core == 0, left, right)).astype(bf16)
    x_sis = (sis_rows * jnp.where(core == 0, right, left)).astype(bf16)
    squares = jnp.sum(own_rows * own_rows + sis_rows * sis_rows, axis=1, keepdims=True)
    line = lax.broadcasted_iota(jnp.int32, (ROWS, QKV), 0)
    lane = lax.broadcasted_iota(jnp.int32, (ROWS, QKV), 1)
    row = jnp.sum(jnp.where(line == lane, squares, 0.0), axis=0, keepdims=True)
    tail = two_rows(row, QKV)

    def product(slot, count):
        cols = slice(slot * QKV, (slot + count) * QKV)
        acc = jnp.dot(x_own, w_own[:, cols], preferred_element_type=f32)
        acc = acc + jnp.dot(x_sis, w_sis[:, cols], preferred_element_type=f32)
        return acc.astype(bf16)

    def full(slot, out):
        out[:ROWS, :] = product(slot, X_HI)
        out[ROWS:, :QKV] = tail
        out[ROWS:, QKV:] = tail

    if ks == FIRST:
        for xr, out in enumerate(outs):
            out[:ROWS, :] = product(xr, 1)
            out[ROWS:, :] = tail
    else:
        outs, buffer, sems = outs[:-2], outs[-2], outs[-1]
        copies = []
        for i, out in enumerate(outs):
            full(i * X_HI, buffer.at[i])
            copies.append(pltpu.make_async_copy(buffer.at[i], out, sems.at[i]))
            copies[i].start()
        for copy in copies:
            copy.wait()


def partials(ks, own, sis, gains, w_own, w_sis):
    half = jax.ShapeDtypeStruct((SUM_ROWS, QKV), bf16)
    full = jax.ShapeDtypeStruct((SUM_ROWS, X_HI * QKV), bf16)
    if ks == FIRST:
        shapes, specs, scratch = (half, half), (vmem(), vmem()), []
    else:
        shapes, specs = (pltpu.HBM(full.shape, bf16),) * len(ks), (hbm(),) * len(ks)
        scratch = [pltpu.VMEM((len(ks), *full.shape), bf16), pltpu.SemaphoreType.DMA((len(ks),))]
    return pl.pallas_call(
        functools.partial(partial_kernel, ks),
        out_shape=shapes,
        in_specs=[vmem()] * 5,
        out_specs=specs,
        scratch_shapes=scratch,
        compiler_params=limit(20),
        cost_estimate=pl.CostEstimate(
            flops=4 * ROWS * w_own.size, bytes_accessed=8 * w_own.size, transcendentals=0
        ),
    )(own, sis, gains, w_own, w_sis)


def store_sum(out, cols, terms):
    body = sum(term[:ROWS].astype(f32) for term in terms)
    row = sum(one_row(term[ROWS:]) for term in terms)
    out[:ROWS, cols] = body.astype(bf16)
    out[ROWS:, cols] = two_rows(row, row.shape[1])


def first_kernel(up, down, near_up, near_down, out_up, out_down):
    left, right = slice(0, QKV), slice(QKV, 2 * QKV)
    store_sum(out_up, left, [up[...], near_up[:, left]])
    out_up[:, right] = near_up[:, right]
    out_down[:, left] = near_down[:, left]
    store_sum(out_down, right, [down[...], near_down[:, right]])


def next_kernel(up, down, near_up, near_down, out_up, out_down):
    every = slice(0, 2 * QKV)
    store_sum(out_up, every, [up[...], near_up[...]])
    store_sum(out_down, every, [down[...], near_down[...]])


def ring_add(kernel, up, down, near_up, near_down):
    out = jax.ShapeDtypeStruct((SUM_ROWS, X_HI * QKV), bf16)
    return pl.pallas_call(
        kernel,
        out_shape=(out, out),
        in_specs=[vmem()] * 4,
        out_specs=(vmem(), vmem()),
        compiler_params=limit(8),
    )(up, down, near_up, near_down)


def last_kernel(up, down, near, mine, other):
    own, far = slice(0, QKV), slice(QKV, 2 * QKV)
    terms = [up, down, near]
    mine[:ROWS] = sum(term[:ROWS, own].astype(f32) for term in terms)
    row = sum(one_row(term[ROWS:, own]) for term in terms)
    mine[ROWS:] = jnp.broadcast_to(row, (8, QKV))
    store_sum(other, slice(0, QKV), [term[:, far] for term in terms])


def ring_last(up, down, near):
    return pl.pallas_call(
        last_kernel,
        out_shape=(
            jax.ShapeDtypeStruct((ROWS + 8, QKV), f32),
            jax.ShapeDtypeStruct((SUM_ROWS, QKV), bf16),
        ),
        in_specs=[vmem()] * 3,
        out_specs=(vmem(), vmem()),
        compiler_params=limit(8),
    )(up, down, near)


def rotated(x, cosine, sine):
    return x * cosine + pltpu.roll(x, HD // 2, 1) * sine


def finish_kernel(full_width, mine, other, cosine, sine, onehot, payload, queries):
    row = mine[ROWS : ROWS + 1, :] + one_row(other[ROWS:, :])
    line = lax.broadcasted_iota(jnp.int32, (ROWS, QKV), 0)
    lane = lax.broadcasted_iota(jnp.int32, (ROWS, QKV), 1)
    squares = jnp.sum(jnp.where(line == lane, row, 0.0), axis=1, keepdims=True)
    inv_rms = lax.rsqrt(squares / full_width + epsilon)
    proj = (mine[:ROWS, :] + other[:ROWS, :].astype(f32)) * inv_rms
    query = rotated(proj[:, :HD], cosine[...], sine[...]).astype(bf16)
    key = rotated(proj[:, HD : 2 * HD], cosine[...], sine[...]).astype(bf16)
    value = proj[:, 2 * HD :].astype(bf16)
    spots = onehot[...]

    def step(b, carry):
        payload[b, :ROWS, :HD] = key
        payload[b, :ROWS, HD:] = value
        payload[b, ROWS:, :] = spots
        return carry

    lax.fori_loop(0, BLOCKS, step, 0)
    contract = (((0,), (0,)), ((), ()))
    ones = jnp.ones((VAR, HD), bf16)
    changed = lax.dot_general(spots, ones, contract, preferred_element_type=f32)
    placed = lax.dot_general(spots, query[TOK:], contract, preferred_element_type=f32)
    base = query[:TOK]
    queries[:TOK] = base
    queries[TOK:] = jnp.where(changed > 0.5, placed, base.astype(f32)).astype(bf16)


def finish(full_width, mine, other, cosine, sine, onehot):
    return pl.pallas_call(
        functools.partial(finish_kernel, full_width),
        out_shape=(
            jax.ShapeDtypeStruct((BLOCKS, PAY, 2 * HD), bf16),
            jax.ShapeDtypeStruct((2 * TOK, HD), bf16),
        ),
        in_specs=[vmem()] * 5,
        out_specs=(vmem(), vmem()),
        compiler_params=limit(12),
    )(mine, other, cosine, sine, pltpu.with_memory_space_constraint(onehot, pltpu.HBM))


def attend_kernel(queries, blocks, out, scores, peak, denom, total, var_kv, spots):
    my_block = lax.axis_index("x_lo") * Y + lax.axis_index("y")
    scale = 1.0 / HD**0.5
    by_cols = (((1,), (1,)), ((), ()))
    lowest = -jnp.inf
    query = queries[...]

    def score_block(j, own):
        score = lax.dot_general(
            query, blocks[j, :TOK, :HD], by_cols, preferred_element_type=f32
        ) * scale
        gone = jnp.sum(blocks[j, ROWS:, :].astype(f32), axis=0, keepdims=True) > 0.5
        line = lax.broadcasted_iota(jnp.int32, (2 * TOK, TOK), 0)
        hidden = (line >= TOK) & gone
        if own:
            lane = lax.broadcasted_iota(jnp.int32, (2 * TOK, TOK), 1)
            hidden = hidden | (lax.rem(line, TOK) < lane)
        return jnp.where(hidden, lowest, score)

    score = score_block(my_block, True)
    scores[my_block] = score
    peak[...] = jnp.maximum(score[:, :HD], score[:, HD:])

    def first(j, carry):
        score = score_block(j, False)
        scores[j] = score
        peak[...] = jnp.maximum(peak[...], jnp.maximum(score[:, :HD], score[:, HD:]))
        return carry

    lax.fori_loop(0, my_block, first, 0)

    for j in range(BLOCKS):
        var_kv[j * VAR : (j + 1) * VAR, :] = blocks[j, TOK:ROWS, :]
        spots[j * VAR : (j + 1) * VAR, :] = blocks[j, ROWS:, :]
    row = lax.broadcasted_iota(jnp.int32, (TOK, TOK), 0)
    col = lax.broadcasted_iota(jnp.int32, (TOK, TOK), 1)
    reached = lax.dot_general(
        jnp.where(row >= col, 1.0, 0.0).astype(bf16), spots[...], by_cols, preferred_element_type=f32
    )
    source = lax.broadcasted_iota(jnp.int32, (TOK, BLOCKS * VAR), 1) // VAR
    seen = (source < my_block) | ((source == my_block) & (reached > 0.5))
    more = lax.dot_general(
        query[TOK:], var_kv[:, :HD], by_cols, preferred_element_type=f32
    ) * scale
    more = jnp.where(seen, more, lowest)
    peak[TOK:, :] = jnp.maximum(peak[TOK:, :], more)
    top = jnp.max(peak[...], axis=1, keepdims=True)
    peak[...] = jnp.broadcast_to(top, (2 * TOK, HD))

    more = jnp.exp(more - top[TOK:])
    denom[:TOK, :] = jnp.zeros((TOK, HD), f32)
    denom[TOK:, :] = more
    total[:TOK, :] = jnp.zeros((TOK, HD), f32)
    total[TOK:, :] = jnp.dot(more.astype(bf16), var_kv[:, HD:], preferred_element_type=f32)

    def second(j, carry):
        best = peak[...]
        left = jnp.exp(scores[j, :, :HD] - best)
        right = jnp.exp(scores[j, :, HD:] - best)
        denom[...] = denom[...] + left + right
        probs = jnp.concatenate([left.astype(bf16), right.astype(bf16)], axis=1)
        total[...] = total[...] + jnp.dot(
            probs, blocks[j, :TOK, HD:], preferred_element_type=f32
        )
        return carry

    lax.fori_loop(0, my_block + 1, second, 0)
    out[...] = (total[...] / jnp.sum(denom[...], axis=1, keepdims=True)).astype(bf16)


def attend(queries, blocks):
    return pl.pallas_call(
        attend_kernel,
        out_shape=jax.ShapeDtypeStruct((2 * TOK, HD), bf16),
        in_specs=[vmem(), vmem()],
        out_specs=vmem(),
        scratch_shapes=[
            pltpu.VMEM((BLOCKS, 2 * TOK, TOK), f32),
            pltpu.VMEM((2 * TOK, HD), f32),
            pltpu.VMEM((2 * TOK, HD), f32),
            pltpu.VMEM((2 * TOK, HD), f32),
            pltpu.VMEM((BLOCKS * VAR, 2 * HD), bf16),
            pltpu.VMEM((BLOCKS * VAR, TOK), bf16),
        ],
        compiler_params=limit(16),
    )(queries, blocks)


def arrange_kernel(w, out, sems):
    z = lax.axis_index("z")
    copies = []
    for d in range(Z):
        source = lax.rem(z + Z - d, Z)
        copies.append(
            pltpu.make_async_copy(w.at[source], out.at[d * HD : (d + 1) * HD, :], sems.at[d])
        )
    for copy in copies:
        copy.start()
    for copy in copies:
        copy.wait()


def arrange(w):
    return pl.pallas_call(
        arrange_kernel,
        out_shape=jax.ShapeDtypeStruct((Z * HD, w.shape[2]), bf16),
        in_specs=[hbm()],
        out_specs=vmem(),
        scratch_shapes=[pltpu.SemaphoreType.DMA((Z,))],
        compiler_params=limit(4),
    )(pltpu.with_memory_space_constraint(w, pltpu.HBM))


def project_kernel(first, turned, *refs):
    shards, (keep, near, far), joined = refs[:Z], refs[Z : Z + 3], refs[-1]
    core, x_hi = lax.axis_index("core"), lax.axis_index("x_hi")
    for d in range(Z):
        joined[:, d * HD : (d + 1) * HD] = shards[d][first : first + TOK, :]

    def product(xr, cr, rows):
        column = (lax.rem(x_hi + xr, X_HI) * CORE + lax.rem(core + cr, CORE)) * TOK
        column = pl.ds(pl.multiple_of(column, TOK), TOK)
        return jnp.dot(joined[rows, :], turned[:, column], preferred_element_type=f32)

    size = 128

    def step(i, carry):
        rows = pl.ds(pl.multiple_of(i * size, size), size)
        for xr in range(X_HI):
            near[rows, xr * TOK : (xr + 1) * TOK] = product(xr, 1, rows).astype(bf16)
        keep[rows, :] = product(0, 0, rows)
        far[rows, :] = product(1, 0, rows)
        return carry

    lax.fori_loop(0, TOK // size, step, 0)


def project(first, w, shards):
    rows = TOK
    return pl.pallas_call(
        functools.partial(project_kernel, first),
        out_shape=(
            jax.ShapeDtypeStruct((rows, TOK), f32),
            jax.ShapeDtypeStruct((rows, 2 * TOK), bf16),
            jax.ShapeDtypeStruct((rows, TOK), f32),
        ),
        in_specs=[vmem()] * (1 + Z),
        out_specs=(vmem(),) * 3,
        scratch_shapes=[pltpu.VMEM((rows, Z * HD), bf16)],
        compiler_params=limit(16),
    )(w, *shards)


def shards(hidden, gain, embed, qkv_weight, out_weight, ref_ids, var_pos, var_base):
    tok_rows, width_part = hidden.shape
    full_width = out_weight.shape[1]
    x_hi, z, core = lax.axis_index("x_hi"), lax.axis_index("z"), lax.axis_index("core")
    my_block = lax.axis_index("x_lo") * Y + lax.axis_index("y")
    chip_slice = x_hi * Z + z

    with jax.named_scope("inputs"):
        rows, onehot, variant, share = make_variant(
            var_pos, var_base, ref_ids, hidden, embed, out_weight
        )
        rows, qkv_weight = lax.optimization_barrier((rows, qkv_weight))
        rows_sis = shift(rows, "core", CORE, 1)
        send_first, own_first = pick_columns(FIRST, qkv_weight)
        sis_first = shift(send_first, "core", CORE, 1)
        rows_sis, sis_first, qkv_weight, share = lax.optimization_barrier(
            (rows_sis, sis_first, qkv_weight, share)
        )
        send_second, own_second = pick_columns(SECOND, qkv_weight)
        sis_second = shift(send_second, "core", CORE, 1)
        shared = lax.all_to_all(share, "z", 0, 0, tiled=True)
        start = chip_slice * 2 * width_part
        gains = lax.dynamic_slice(gain.reshape(1, full_width), (0, start), (1, 2 * width_part))

    with jax.named_scope("projection"):
        sis_first = pltpu.with_memory_space_constraint(sis_first, pltpu.HBM)
        up, down = partials(FIRST, rows, rows_sis, gains, own_first, sis_first)
        up, down = shift(up, "z", Z, 1), shift(down, "z", Z, -1)
        parts = partials(SECOND, rows, rows_sis, gains, own_second, sis_second)
        near_up = pltpu.with_memory_space_constraint(parts[0], pltpu.HBM)
        near_down = pltpu.with_memory_space_constraint(parts[1], pltpu.HBM)
        up, down, shared, near_up = lax.optimization_barrier((up, down, shared, near_up))
        out_w = lax.all_gather(shared, CTX, axis=1, tiled=True)
        parts = dict(zip(SECOND, parts))
        up, down = ring_add(first_kernel, up, down, near_up, near_down)
        up, down = shift(up, "z", Z, 1), shift(down, "z", Z, -1)
        near_up = pltpu.with_memory_space_constraint(parts[2], pltpu.HBM)
        near_down = pltpu.with_memory_space_constraint(parts[6], pltpu.HBM)
        up, down = ring_add(next_kernel, up, down, near_up, near_down)
        up, down = shift(up, "z", Z, 1), shift(down, "z", Z, -1)
        up, down = ring_add(next_kernel, up, down, parts[1], parts[7])
        up, down = shift(up, "z", Z, 1), shift(down, "z", Z, -1)
        mine, other = ring_last(up, down, parts[0])
        other = shift(other, "x_hi", X_HI, 1)

    with jax.named_scope("tables"):
        positions = jnp.concatenate([my_block * tok_rows + jnp.arange(tok_rows), var_pos])
        exponent = jnp.arange(HD // 2).astype(f32) * (-2.0 / HD)
        inv_freq = jnp.power(f32(rope_base), exponent)
        angle = positions.astype(f32)[:, None] * inv_freq[None, :]
        cosine, sine = jnp.cos(angle), jnp.sin(angle)
        cosine = jnp.concatenate([cosine, cosine], axis=1)
        sine = jnp.concatenate([-sine, sine], axis=1)

    with jax.named_scope("attention"):
        payload, queries = finish(full_width, mine, other, cosine, sine, onehot)
        blocks = lax.all_to_all(payload, CTX, 0, 0, tiled=True)
        attn = attend(queries, blocks)
        attn, out_w = lax.optimization_barrier((attn, out_w))

    with jax.named_scope("output"):
        pieces = [attn] + [None] * (Z - 1)
        for d in (1, 2, 3):
            pieces[d] = shift(pieces[d - 1], "z", Z, 1)
            pieces[Z - d] = shift(pieces[(Z - d + 1) % Z], "z", Z, -1)
            if d == 1:
                pieces[Z // 2] = shift(attn, "z", Z, Z // 2)
                out_w, pieces[1], pieces[7] = lax.optimization_barrier(
                    (arrange(out_w), pieces[1], pieces[7])
                )
        mixed = []
        for first, seq in ((0, hidden), (tok_rows, variant)):
            keep, near, far = project(first, out_w, pieces)
            near = shift(near, "core", CORE, 1).astype(f32)
            far = (far + near[:, width_part:]).astype(bf16)
            far = shift(far, "x_hi", X_HI, 1).astype(f32)
            branch = keep + near[:, :width_part] + far
            mixed.append((seq.astype(f32) + branch).astype(bf16))
        return jnp.stack(mixed)


def solution(mesh):
    fine = Mesh(mesh.devices.reshape(X_HI, Z, CORE, X_LO, Y), (*FSDP, *CTX))
    in_specs = (
        P(CTX, FSDP),
        P(),
        P(None, FSDP),
        P(FSDP, None),
        P(FSDP, None),
        P(CTX),
        P(CTX),
        P(CTX),
    )
    out_specs = P(None, CTX, FSDP)
    return jax.shard_map(shards, mesh=fine, in_specs=in_specs, out_specs=out_specs, check_vma=False)
```

```python
import functools

import jax
import jax.numpy as jnp
from jax import lax
from jax.experimental import pallas as pl
from jax.experimental.pallas import tpu as pltpu
from jax.sharding import Mesh, PartitionSpec as P

epsilon = 1e-05
rope_base = 10000.0

X_HI, Z, CORE, X_LO, Y = 2, 8, 2, 2, 4
FSDP = ("x_hi", "z", "core")
CTX = ("x_lo", "y")
BLOCKS = X_LO * Y
HD = 128
QKV = 3 * HD
TOK = 256
VAR = 16
ROWS = TOK + VAR
SUM_ROWS = ROWS + 16
PAY = ROWS + VAR
bf16 = jnp.bfloat16
f32 = jnp.float32
MIB = 1024 * 1024


def shift(value, axis, size, distance):
    return lax.ppermute(value, axis, [(i, (i + distance) % size) for i in range(size)])


def vmem():
    return pl.BlockSpec(memory_space=pltpu.VMEM)


def anywhere():
    return pl.BlockSpec(memory_space=pl.ANY)


def hbm():
    return pl.BlockSpec(memory_space=pltpu.HBM)


def limit(mib):
    return pltpu.CompilerParams(vmem_limit_bytes=mib * MIB)


FIRST = (4,)
SECOND = (3, 5, 2, 6, 1, 7, 0)


def variant_kernel(
    pos, base, ids, hidden, embed, w, rows, onehot, variant, share, spots, block, buffer, sems, share_sems
):
    my_block = lax.axis_index("x_lo") * Y + lax.axis_index("y")
    size, half = buffer.shape[1], buffer.shape[2] // X_HI
    share_rows = pl.ds(pl.multiple_of(my_block * size, size), size)
    copies = []
    for k in range(Z):
        for x in range(X_HI):
            start = (x * Z + k) * half
            copies.append(
                pltpu.make_async_copy(
                    w.at[share_rows, start : start + half],
                    buffer.at[k, :, x * half : (x + 1) * half],
                    share_sems.at[k, x],
                )
            )
    for copy in copies:
        copy.start()
    first = (lax.axis_index("x_lo") * Y + lax.axis_index("y")) * TOK
    vocab = embed.shape[0]
    spot = lax.broadcasted_iota(jnp.int32, (VAR, TOK), 0)
    lane = lax.broadcasted_iota(jnp.int32, (VAR, TOK), 1)
    word_spot = lax.broadcasted_iota(jnp.int32, (VAR, vocab), 0)
    word = lax.broadcasted_iota(jnp.int32, (VAR, vocab), 1)
    places = jnp.zeros((VAR, TOK), f32)
    words = jnp.zeros((VAR, vocab), f32)
    for j in range(VAR):
        place = pos[j] - first
        places = jnp.where((spot == j) & (lane == place), 1.0, places)
        new = jnp.where(word == base[j], 1.0, 0.0)
        old = jnp.where(word == ids[place], 1.0, 0.0)
        words = jnp.where(word_spot == j, new - old, words)
    places = places.astype(bf16)
    change = jnp.dot(words.astype(bf16), embed[...], preferred_element_type=f32)
    picked = jnp.dot(places, hidden[...], preferred_element_type=f32)
    changed_rows = (picked + change).astype(bf16)
    rows[:TOK] = hidden[...]
    rows[TOK:] = changed_rows
    spots[...] = places
    for copy in copies:
        copy.wait()
    share_copy = pltpu.make_async_copy(buffer, share, sems.at[2])
    share_copy.start()
    first_copy = pltpu.make_async_copy(spots, onehot, sems.at[0])
    first_copy.start()
    contract = (((0,), (0,)), ((), ()))
    placed = lax.dot_general(places, changed_rows, contract, preferred_element_type=f32)
    ones = jnp.ones((VAR, hidden.shape[1]), bf16)
    changed = lax.dot_general(places, ones, contract, preferred_element_type=f32)
    block[...] = jnp.where(changed > 0.5, placed, hidden[...].astype(f32)).astype(bf16)
    second_copy = pltpu.make_async_copy(block, variant, sems.at[1])
    second_copy.start()
    first_copy.wait()
    second_copy.wait()
    share_copy.wait()


def make_variant(pos, base, ids, hidden, embed, w):
    width = hidden.shape[1]
    shape = (Z, w.shape[0] // BLOCKS, w.shape[1] // Z)
    args = (pos, base, ids, hidden, embed, w)
    smem = pl.BlockSpec(memory_space=pltpu.SMEM)
    return pl.pallas_call(
        variant_kernel,
        out_shape=(
            jax.ShapeDtypeStruct((ROWS, width), bf16),
            pltpu.HBM((VAR, TOK), bf16),
            pltpu.HBM((TOK, width), bf16),
            pltpu.HBM(shape, bf16),
        ),
        in_specs=[smem, smem, smem, vmem(), vmem(), hbm()],
        out_specs=(vmem(), hbm(), hbm(), hbm()),
        scratch_shapes=[
            pltpu.VMEM((VAR, TOK), bf16),
            pltpu.VMEM((TOK, width), bf16),
            pltpu.VMEM(shape, bf16),
            pltpu.SemaphoreType.DMA((3,)),
            pltpu.SemaphoreType.DMA((Z, X_HI)),
        ],
        compiler_params=limit(4),
    )(*(pltpu.with_memory_space_constraint(v, pltpu.HBM) for v in args))


def column_copies(ks, sister, w, out, sems):
    z, core, x_hi = lax.axis_index("z"), lax.axis_index("core"), lax.axis_index("x_hi")
    whose = 1 - core if sister else core
    copies = []
    for i, k in enumerate(ks):
        for xr in range(X_HI):
            head_pair = lax.rem(x_hi + xr, X_HI) * Z + lax.rem(z + k, Z)
            slot = i * X_HI + xr
            start = pl.multiple_of((head_pair * 2 + whose) * QKV, HD)
            copies.append(
                pltpu.make_async_copy(
                    w.at[:, pl.ds(start, QKV)],
                    out.at[:, slot * QKV : (slot + 1) * QKV],
                    sems.at[slot],
                )
            )
    return copies


def columns_kernel(wanted, w, *refs):
    outs, sems = refs[: len(wanted)], refs[len(wanted) :]
    copies = []
    for (ks, sister), out, sem in zip(wanted, outs, sems):
        copies += column_copies(ks, sister, w, out, sem)
    for copy in copies:
        copy.start()
    for copy in copies:
        copy.wait()


def pick_columns(wanted, w):
    return pl.pallas_call(
        functools.partial(columns_kernel, wanted),
        out_shape=tuple(
            jax.ShapeDtypeStruct((w.shape[0], len(ks) * X_HI * QKV), bf16) for ks, _ in wanted
        ),
        in_specs=[hbm()],
        out_specs=(vmem(),) * len(wanted),
        scratch_shapes=[pltpu.SemaphoreType.DMA((len(ks) * X_HI,)) for ks, _ in wanted],
        compiler_params=limit(12),
    )(pltpu.with_memory_space_constraint(w, pltpu.HBM))


def two_rows(row, width):
    high = row.astype(bf16)
    low = (row - high.astype(f32)).astype(bf16)
    line = lax.broadcasted_iota(jnp.int32, (16, width), 0)
    both = jnp.where(line == 0, high.astype(f32), jnp.where(line == 1, low.astype(f32), 0.0))
    return both.astype(bf16)


def one_row(rows):
    return jnp.sum(rows.astype(f32), axis=0, keepdims=True)


def partial_kernel(ks, own, sis, gains, w_own, w_sis, *outs):
    width = X_HI * QKV
    core = lax.axis_index("core")
    own_rows, sis_rows = own[...].astype(f32), sis[...].astype(f32)
    left, right = gains[:, :TOK].astype(f32), gains[:, TOK:].astype(f32)
    x_own = (own_rows * jnp.where(core == 0, left, right)).astype(bf16)
    x_sis = (sis_rows * jnp.where(core == 0, right, left)).astype(bf16)
    squares = jnp.sum(own_rows * own_rows + sis_rows * sis_rows, axis=1, keepdims=True)
    line = lax.broadcasted_iota(jnp.int32, (ROWS, QKV), 0)
    lane = lax.broadcasted_iota(jnp.int32, (ROWS, QKV), 1)
    row = jnp.sum(jnp.where(line == lane, squares, 0.0), axis=0, keepdims=True)
    tail = two_rows(row, QKV)

    def product(slot, count):
        cols = slice(slot * QKV, (slot + count) * QKV)
        acc = jnp.dot(x_own, w_own[:, cols], preferred_element_type=f32)
        acc = acc + jnp.dot(x_sis, w_sis[:, cols], preferred_element_type=f32)
        return acc.astype(bf16)

    def full(slot, out):
        out[:ROWS, :] = product(slot, X_HI)
        out[ROWS:, :QKV] = tail
        out[ROWS:, QKV:] = tail

    if ks == FIRST:
        for xr, out in enumerate(outs):
            out[:ROWS, :] = product(xr, 1)
            out[ROWS:, :] = tail
    else:
        outs, buffer, sems = outs[:-2], outs[-2], outs[-1]
        copies = []
        for i, out in enumerate(outs):
            full(i * X_HI, buffer.at[i])
            copies.append(pltpu.make_async_copy(buffer.at[i], out, sems.at[i]))
            copies[i].start()
        for copy in copies:
            copy.wait()


def partials(ks, own, sis, gains, w_own, w_sis):
    half = jax.ShapeDtypeStruct((SUM_ROWS, QKV), bf16)
    full = jax.ShapeDtypeStruct((SUM_ROWS, X_HI * QKV), bf16)
    if ks == FIRST:
        shapes, specs, scratch = (half, half), (vmem(), vmem()), []
    else:
        shapes, specs = (pltpu.HBM(full.shape, bf16),) * len(ks), (hbm(),) * len(ks)
        scratch = [pltpu.VMEM((len(ks), *full.shape), bf16), pltpu.SemaphoreType.DMA((len(ks),))]
    return pl.pallas_call(
        functools.partial(partial_kernel, ks),
        out_shape=shapes,
        in_specs=[vmem()] * 5,
        out_specs=specs,
        scratch_shapes=scratch,
        compiler_params=limit(20),
        cost_estimate=pl.CostEstimate(
            flops=4 * ROWS * w_own.size, bytes_accessed=8 * w_own.size, transcendentals=0
        ),
    )(own, sis, gains, w_own, w_sis)


def store_sum(out, cols, terms):
    body = sum(term[:ROWS].astype(f32) for term in terms)
    row = sum(one_row(term[ROWS:]) for term in terms)
    out[:ROWS, cols] = body.astype(bf16)
    out[ROWS:, cols] = two_rows(row, row.shape[1])


def first_kernel(up, down, near_up, near_down, out_up, out_down):
    left, right = slice(0, QKV), slice(QKV, 2 * QKV)
    store_sum(out_up, left, [up[...], near_up[:, left]])
    out_up[:, right] = near_up[:, right]
    out_down[:, left] = near_down[:, left]
    store_sum(out_down, right, [down[...], near_down[:, right]])


def next_kernel(up, down, near_up, near_down, out_up, out_down):
    every = slice(0, 2 * QKV)
    store_sum(out_up, every, [up[...], near_up[...]])
    store_sum(out_down, every, [down[...], near_down[...]])


def ring_add(kernel, up, down, near_up, near_down):
    out = jax.ShapeDtypeStruct((SUM_ROWS, X_HI * QKV), bf16)
    return pl.pallas_call(
        kernel,
        out_shape=(out, out),
        in_specs=[vmem()] * 4,
        out_specs=(vmem(), vmem()),
        compiler_params=limit(8),
    )(up, down, near_up, near_down)


def last_kernel(up, down, near, mine, other):
    own, far = slice(0, QKV), slice(QKV, 2 * QKV)
    terms = [up, down, near]
    mine[:ROWS] = sum(term[:ROWS, own].astype(f32) for term in terms)
    row = sum(one_row(term[ROWS:, own]) for term in terms)
    mine[ROWS:] = jnp.broadcast_to(row, (8, QKV))
    store_sum(other, slice(0, QKV), [term[:, far] for term in terms])


def ring_last(up, down, near):
    return pl.pallas_call(
        last_kernel,
        out_shape=(
            jax.ShapeDtypeStruct((ROWS + 8, QKV), f32),
            jax.ShapeDtypeStruct((SUM_ROWS, QKV), bf16),
        ),
        in_specs=[vmem()] * 3,
        out_specs=(vmem(), vmem()),
        compiler_params=limit(8),
    )(up, down, near)


def rotated(x, cosine, sine):
    return x * cosine + pltpu.roll(x, HD // 2, 1) * sine


def finish_kernel(full_width, mine, other, cosine, sine, onehot, payload, queries):
    row = mine[ROWS : ROWS + 1, :] + one_row(other[ROWS:, :])
    line = lax.broadcasted_iota(jnp.int32, (ROWS, QKV), 0)
    lane = lax.broadcasted_iota(jnp.int32, (ROWS, QKV), 1)
    squares = jnp.sum(jnp.where(line == lane, row, 0.0), axis=1, keepdims=True)
    inv_rms = lax.rsqrt(squares / full_width + epsilon)
    proj = (mine[:ROWS, :] + other[:ROWS, :].astype(f32)) * inv_rms
    query = rotated(proj[:, :HD], cosine[...], sine[...]).astype(bf16)
    key = rotated(proj[:, HD : 2 * HD], cosine[...], sine[...]).astype(bf16)
    value = proj[:, 2 * HD :].astype(bf16)
    spots = onehot[...]

    def step(b, carry):
        payload[b, :ROWS, :HD] = key
        payload[b, :ROWS, HD:] = value
        payload[b, ROWS:, :] = spots
        return carry

    lax.fori_loop(0, BLOCKS, step, 0)
    contract = (((0,), (0,)), ((), ()))
    ones = jnp.ones((VAR, HD), bf16)
    changed = lax.dot_general(spots, ones, contract, preferred_element_type=f32)
    placed = lax.dot_general(spots, query[TOK:], contract, preferred_element_type=f32)
    base = query[:TOK]
    queries[:TOK] = base
    queries[TOK:] = jnp.where(changed > 0.5, placed, base.astype(f32)).astype(bf16)


def finish(full_width, mine, other, cosine, sine, onehot):
    return pl.pallas_call(
        functools.partial(finish_kernel, full_width),
        out_shape=(
            jax.ShapeDtypeStruct((BLOCKS, PAY, 2 * HD), bf16),
            jax.ShapeDtypeStruct((2 * TOK, HD), bf16),
        ),
        in_specs=[vmem()] * 5,
        out_specs=(vmem(), vmem()),
        compiler_params=limit(12),
    )(mine, other, cosine, sine, pltpu.with_memory_space_constraint(onehot, pltpu.HBM))


def attend_kernel(queries, blocks, out, scores, peak, denom, total, var_kv, spots):
    my_block = lax.axis_index("x_lo") * Y + lax.axis_index("y")
    scale = 1.0 / HD**0.5
    by_cols = (((1,), (1,)), ((), ()))
    lowest = -jnp.inf
    query = queries[...]

    def score_block(j, own):
        score = lax.dot_general(
            query, blocks[j, :TOK, :HD], by_cols, preferred_element_type=f32
        ) * scale
        gone = jnp.sum(blocks[j, ROWS:, :].astype(f32), axis=0, keepdims=True) > 0.5
        line = lax.broadcasted_iota(jnp.int32, (2 * TOK, TOK), 0)
        hidden = (line >= TOK) & gone
        if own:
            lane = lax.broadcasted_iota(jnp.int32, (2 * TOK, TOK), 1)
            hidden = hidden | (lax.rem(line, TOK) < lane)
        return jnp.where(hidden, lowest, score)

    score = score_block(my_block, True)
    scores[my_block] = score
    peak[...] = jnp.maximum(score[:, :HD], score[:, HD:])

    def first(j, carry):
        score = score_block(j, False)
        scores[j] = score
        peak[...] = jnp.maximum(peak[...], jnp.maximum(score[:, :HD], score[:, HD:]))
        return carry

    lax.fori_loop(0, my_block, first, 0)

    for j in range(BLOCKS):
        var_kv[j * VAR : (j + 1) * VAR, :] = blocks[j, TOK:ROWS, :]
        spots[j * VAR : (j + 1) * VAR, :] = blocks[j, ROWS:, :]
    row = lax.broadcasted_iota(jnp.int32, (TOK, TOK), 0)
    col = lax.broadcasted_iota(jnp.int32, (TOK, TOK), 1)
    reached = lax.dot_general(
        jnp.where(row >= col, 1.0, 0.0).astype(bf16), spots[...], by_cols, preferred_element_type=f32
    )
    source = lax.broadcasted_iota(jnp.int32, (TOK, BLOCKS * VAR), 1) // VAR
    seen = (source < my_block) | ((source == my_block) & (reached > 0.5))
    more = lax.dot_general(
        query[TOK:], var_kv[:, :HD], by_cols, preferred_element_type=f32
    ) * scale
    more = jnp.where(seen, more, lowest)
    peak[TOK:, :] = jnp.maximum(peak[TOK:, :], more)
    top = jnp.max(peak[...], axis=1, keepdims=True)
    peak[...] = jnp.broadcast_to(top, (2 * TOK, HD))

    more = jnp.exp(more - top[TOK:])
    denom[:TOK, :] = jnp.zeros((TOK, HD), f32)
    denom[TOK:, :] = more
    total[:TOK, :] = jnp.zeros((TOK, HD), f32)
    total[TOK:, :] = jnp.dot(more.astype(bf16), var_kv[:, HD:], preferred_element_type=f32)

    def second(j, carry):
        best = peak[...]
        left = jnp.exp(scores[j, :, :HD] - best)
        right = jnp.exp(scores[j, :, HD:] - best)
        denom[...] = denom[...] + left + right
        probs = jnp.concatenate([left.astype(bf16), right.astype(bf16)], axis=1)
        total[...] = total[...] + jnp.dot(
            probs, blocks[j, :TOK, HD:], preferred_element_type=f32
        )
        return carry

    lax.fori_loop(0, my_block + 1, second, 0)
    out[...] = (total[...] / jnp.sum(denom[...], axis=1, keepdims=True)).astype(bf16)


def attend(queries, blocks):
    return pl.pallas_call(
        attend_kernel,
        out_shape=jax.ShapeDtypeStruct((2 * TOK, HD), bf16),
        in_specs=[vmem(), vmem()],
        out_specs=vmem(),
        scratch_shapes=[
            pltpu.VMEM((BLOCKS, 2 * TOK, TOK), f32),
            pltpu.VMEM((2 * TOK, HD), f32),
            pltpu.VMEM((2 * TOK, HD), f32),
            pltpu.VMEM((2 * TOK, HD), f32),
            pltpu.VMEM((BLOCKS * VAR, 2 * HD), bf16),
            pltpu.VMEM((BLOCKS * VAR, TOK), bf16),
        ],
        compiler_params=limit(16),
    )(queries, blocks)


def arrange_kernel(w, out, sems):
    z = lax.axis_index("z")
    copies = []
    for d in range(Z):
        source = lax.rem(z + Z - d, Z)
        copies.append(
            pltpu.make_async_copy(w.at[source], out.at[d * HD : (d + 1) * HD, :], sems.at[d])
        )
    for copy in copies:
        copy.start()
    for copy in copies:
        copy.wait()


def arrange(w):
    return pl.pallas_call(
        arrange_kernel,
        out_shape=jax.ShapeDtypeStruct((Z * HD, w.shape[2]), bf16),
        in_specs=[hbm()],
        out_specs=vmem(),
        scratch_shapes=[pltpu.SemaphoreType.DMA((Z,))],
        compiler_params=limit(4),
    )(pltpu.with_memory_space_constraint(w, pltpu.HBM))


def project_kernel(first, turned, *refs):
    shards, (keep, near, far), joined = refs[:Z], refs[Z : Z + 3], refs[-1]
    core, x_hi = lax.axis_index("core"), lax.axis_index("x_hi")
    for d in range(Z):
        joined[:, d * HD : (d + 1) * HD] = shards[d][first : first + TOK, :]

    def product(xr, cr, rows):
        column = (lax.rem(x_hi + xr, X_HI) * CORE + lax.rem(core + cr, CORE)) * TOK
        column = pl.ds(pl.multiple_of(column, TOK), TOK)
        return jnp.dot(joined[rows, :], turned[:, column], preferred_element_type=f32)

    size = 128

    def step(i, carry):
        rows = pl.ds(pl.multiple_of(i * size, size), size)
        for xr in range(X_HI):
            near[rows, xr * TOK : (xr + 1) * TOK] = product(xr, 1, rows).astype(bf16)
        keep[rows, :] = product(0, 0, rows)
        far[rows, :] = product(1, 0, rows)
        return carry

    lax.fori_loop(0, TOK // size, step, 0)


def project(first, w, shards):
    rows = TOK
    return pl.pallas_call(
        functools.partial(project_kernel, first),
        out_shape=(
            jax.ShapeDtypeStruct((rows, TOK), f32),
            jax.ShapeDtypeStruct((rows, 2 * TOK), bf16),
            jax.ShapeDtypeStruct((rows, TOK), f32),
        ),
        in_specs=[vmem()] * (1 + Z),
        out_specs=(vmem(),) * 3,
        scratch_shapes=[pltpu.VMEM((rows, Z * HD), bf16)],
        compiler_params=limit(16),
    )(w, *shards)


def shards(hidden, gain, embed, qkv_weight, out_weight, ref_ids, var_pos, var_base):
    tok_rows, width_part = hidden.shape
    full_width = out_weight.shape[1]
    x_hi, z, core = lax.axis_index("x_hi"), lax.axis_index("z"), lax.axis_index("core")
    my_block = lax.axis_index("x_lo") * Y + lax.axis_index("y")
    chip_slice = x_hi * Z + z

    with jax.named_scope("inputs"):
        rows, onehot, variant, share = make_variant(
            var_pos, var_base, ref_ids, hidden, embed, out_weight
        )
        rows, qkv_weight = lax.optimization_barrier((rows, qkv_weight))
        rows_sis = shift(rows, "core", CORE, 1)
        (send_first,) = pick_columns(((FIRST, True),), qkv_weight)
        sis_first = shift(send_first, "core", CORE, 1)
        start = chip_slice * 2 * width_part
        gains = lax.dynamic_slice(gain.reshape(1, full_width), (0, start), (1, 2 * width_part))
        rows_sis, sis_first, qkv_weight, share, gains = lax.optimization_barrier(
            (rows_sis, sis_first, qkv_weight, share, gains)
        )
        send_second, own_first, own_second = pick_columns(
            ((SECOND, True), (FIRST, False), (SECOND, False)), qkv_weight
        )
        sis_second = shift(send_second, "core", CORE, 1)
        shared = lax.all_to_all(share, "z", 0, 0, tiled=True)

    with jax.named_scope("projection"):
        sis_first = pltpu.with_memory_space_constraint(sis_first, pltpu.HBM)
        up, down = partials(FIRST, rows, rows_sis, gains, own_first, sis_first)
        up, down = shift(up, "z", Z, 1), shift(down, "z", Z, -1)
        parts = partials(SECOND, rows, rows_sis, gains, own_second, sis_second)
        near_up = pltpu.with_memory_space_constraint(parts[0], pltpu.HBM)
        near_down = pltpu.with_memory_space_constraint(parts[1], pltpu.HBM)
        up, down, shared, near_up = lax.optimization_barrier((up, down, shared, near_up))
        out_w = lax.all_gather(shared, CTX, axis=1, tiled=True)
        parts = dict(zip(SECOND, parts))
        up, down = ring_add(first_kernel, up, down, near_up, near_down)
        up, down = shift(up, "z", Z, 1), shift(down, "z", Z, -1)
        near_up = pltpu.with_memory_space_constraint(parts[2], pltpu.HBM)
        near_down = pltpu.with_memory_space_constraint(parts[6], pltpu.HBM)
        up, down = ring_add(next_kernel, up, down, near_up, near_down)
        up, down = shift(up, "z", Z, 1), shift(down, "z", Z, -1)
        up, down = ring_add(next_kernel, up, down, parts[1], parts[7])
        up, down = shift(up, "z", Z, 1), shift(down, "z", Z, -1)
        mine, other = ring_last(up, down, parts[0])
        other = shift(other, "x_hi", X_HI, 1)

    with jax.named_scope("tables"):
        positions = jnp.concatenate([my_block * tok_rows + jnp.arange(tok_rows), var_pos])
        exponent = jnp.arange(HD // 2).astype(f32) * (-2.0 / HD)
        inv_freq = jnp.power(f32(rope_base), exponent)
        angle = positions.astype(f32)[:, None] * inv_freq[None, :]
        cosine, sine = jnp.cos(angle), jnp.sin(angle)
        cosine = jnp.concatenate([cosine, cosine], axis=1)
        sine = jnp.concatenate([-sine, sine], axis=1)

    with jax.named_scope("attention"):
        payload, queries = finish(full_width, mine, other, cosine, sine, onehot)
        blocks = lax.all_to_all(payload, CTX, 0, 0, tiled=True)
        attn = attend(queries, blocks)
        attn, out_w = lax.optimization_barrier((attn, out_w))

    with jax.named_scope("output"):
        pieces = [attn] + [None] * (Z - 1)
        for d in (1, 2, 3):
            pieces[d] = shift(pieces[d - 1], "z", Z, 1)
            pieces[Z - d] = shift(pieces[(Z - d + 1) % Z], "z", Z, -1)
            if d == 1:
                pieces[Z // 2] = shift(attn, "z", Z, Z // 2)
                out_w, pieces[1], pieces[7] = lax.optimization_barrier(
                    (arrange(out_w), pieces[1], pieces[7])
                )
        mixed = []
        for first, seq in ((0, hidden), (tok_rows, variant)):
            keep, near, far = project(first, out_w, pieces)
            near = shift(near, "core", CORE, 1).astype(f32)
            far = (far + near[:, width_part:]).astype(bf16)
            far = shift(far, "x_hi", X_HI, 1).astype(f32)
            branch = keep + near[:, :width_part] + far
            mixed.append((seq.astype(f32) + branch).astype(bf16))
        return jnp.stack(mixed)


def solution(mesh):
    fine = Mesh(mesh.devices.reshape(X_HI, Z, CORE, X_LO, Y), (*FSDP, *CTX))
    in_specs = (
        P(CTX, FSDP),
        P(),
        P(None, FSDP),
        P(FSDP, None),
        P(FSDP, None),
        P(CTX),
        P(CTX),
        P(CTX),
    )
    out_specs = P(None, CTX, FSDP)
    return jax.shard_map(shards, mesh=fine, in_specs=in_specs, out_specs=out_specs, check_vma=False)
```

```python
import functools

import jax
import jax.numpy as jnp
from jax import lax
from jax.experimental import pallas as pl
from jax.experimental.pallas import tpu as pltpu
from jax.sharding import Mesh, PartitionSpec as P

epsilon = 1e-05
rope_base = 10000.0

X_HI, Z, CORE, X_LO, Y = 2, 8, 2, 2, 4
FSDP = ("x_hi", "z", "core")
CTX = ("x_lo", "y")
BLOCKS = X_LO * Y
HD = 128
QKV = 3 * HD
TOK = 256
VAR = 16
ROWS = TOK + VAR
SUM_ROWS = ROWS + 16
PAY = ROWS + VAR
bf16 = jnp.bfloat16
f32 = jnp.float32
MIB = 1024 * 1024


def shift(value, axis, size, distance):
    return lax.ppermute(value, axis, [(i, (i + distance) % size) for i in range(size)])


def vmem():
    return pl.BlockSpec(memory_space=pltpu.VMEM)


def anywhere():
    return pl.BlockSpec(memory_space=pl.ANY)


def hbm():
    return pl.BlockSpec(memory_space=pltpu.HBM)


def limit(mib):
    return pltpu.CompilerParams(vmem_limit_bytes=mib * MIB)


FIRST = (4,)
SECOND = (3, 5, 2, 6, 1, 7, 0)


def variant_kernel(
    pos, base, ids, hidden, embed, w, rows, onehot, variant, share, spots, block, buffer, sems, share_sems
):
    my_block = lax.axis_index("x_lo") * Y + lax.axis_index("y")
    size, half = buffer.shape[1], buffer.shape[2] // X_HI
    share_rows = pl.ds(pl.multiple_of(my_block * size, size), size)
    copies = []
    for k in range(Z):
        for x in range(X_HI):
            start = (x * Z + k) * half
            copies.append(
                pltpu.make_async_copy(
                    w.at[share_rows, start : start + half],
                    buffer.at[k, :, x * half : (x + 1) * half],
                    share_sems.at[k, x],
                )
            )
    for copy in copies:
        copy.start()
    first = (lax.axis_index("x_lo") * Y + lax.axis_index("y")) * TOK
    vocab = embed.shape[0]
    spot = lax.broadcasted_iota(jnp.int32, (VAR, TOK), 0)
    lane = lax.broadcasted_iota(jnp.int32, (VAR, TOK), 1)
    word_spot = lax.broadcasted_iota(jnp.int32, (VAR, vocab), 0)
    word = lax.broadcasted_iota(jnp.int32, (VAR, vocab), 1)
    places = jnp.zeros((VAR, TOK), f32)
    words = jnp.zeros((VAR, vocab), f32)
    for j in range(VAR):
        place = pos[j] - first
        places = jnp.where((spot == j) & (lane == place), 1.0, places)
        new = jnp.where(word == base[j], 1.0, 0.0)
        old = jnp.where(word == ids[place], 1.0, 0.0)
        words = jnp.where(word_spot == j, new - old, words)
    places = places.astype(bf16)
    change = jnp.dot(words.astype(bf16), embed[...], preferred_element_type=f32)
    picked = jnp.dot(places, hidden[...], preferred_element_type=f32)
    changed_rows = (picked + change).astype(bf16)
    rows[:TOK] = hidden[...]
    rows[TOK:] = changed_rows
    spots[...] = places
    for copy in copies:
        copy.wait()
    share_copy = pltpu.make_async_copy(buffer, share, sems.at[2])
    share_copy.start()
    first_copy = pltpu.make_async_copy(spots, onehot, sems.at[0])
    first_copy.start()
    contract = (((0,), (0,)), ((), ()))
    placed = lax.dot_general(places, changed_rows, contract, preferred_element_type=f32)
    ones = jnp.ones((VAR, hidden.shape[1]), bf16)
    changed = lax.dot_general(places, ones, contract, preferred_element_type=f32)
    block[...] = jnp.where(changed > 0.5, placed, hidden[...].astype(f32)).astype(bf16)
    second_copy = pltpu.make_async_copy(block, variant, sems.at[1])
    second_copy.start()
    first_copy.wait()
    second_copy.wait()
    share_copy.wait()


def make_variant(pos, base, ids, hidden, embed, w):
    width = hidden.shape[1]
    shape = (Z, w.shape[0] // BLOCKS, w.shape[1] // Z)
    args = (pos, base, ids, hidden, embed, w)
    smem = pl.BlockSpec(memory_space=pltpu.SMEM)
    return pl.pallas_call(
        variant_kernel,
        out_shape=(
            jax.ShapeDtypeStruct((ROWS, width), bf16),
            pltpu.HBM((VAR, TOK), bf16),
            pltpu.HBM((TOK, width), bf16),
            pltpu.HBM(shape, bf16),
        ),
        in_specs=[smem, smem, smem, vmem(), vmem(), hbm()],
        out_specs=(vmem(), hbm(), hbm(), hbm()),
        scratch_shapes=[
            pltpu.VMEM((VAR, TOK), bf16),
            pltpu.VMEM((TOK, width), bf16),
            pltpu.VMEM(shape, bf16),
            pltpu.SemaphoreType.DMA((3,)),
            pltpu.SemaphoreType.DMA((Z, X_HI)),
        ],
        compiler_params=limit(4),
    )(*(pltpu.with_memory_space_constraint(v, pltpu.HBM) for v in args))


def column_copies(ks, w, send, own, sems):
    z, core, x_hi = lax.axis_index("z"), lax.axis_index("core"), lax.axis_index("x_hi")
    copies = []
    for index, (whose, out) in enumerate(((1 - core, send), (core, own))):
        for i, k in enumerate(ks):
            for xr in range(X_HI):
                head_pair = lax.rem(x_hi + xr, X_HI) * Z + lax.rem(z + k, Z)
                slot = i * X_HI + xr
                start = pl.multiple_of((head_pair * 2 + whose) * QKV, HD)
                copies.append(
                    pltpu.make_async_copy(
                        w.at[:, pl.ds(start, QKV)],
                        out.at[:, slot * QKV : (slot + 1) * QKV],
                        sems.at[index, slot],
                    )
                )
    return copies


def columns_kernel(ks, w, send, own, sems):
    copies = column_copies(ks, w, send, own, sems)
    for copy in copies:
        copy.start()
    for copy in copies:
        copy.wait()


def pick_columns(ks, w):
    columns = jax.ShapeDtypeStruct((w.shape[0], len(ks) * X_HI * QKV), bf16)
    return pl.pallas_call(
        functools.partial(columns_kernel, ks),
        out_shape=(columns, columns),
        in_specs=[hbm()],
        out_specs=(vmem(), vmem()),
        scratch_shapes=[pltpu.SemaphoreType.DMA((2, len(ks) * X_HI))],
        compiler_params=limit(12),
    )(pltpu.with_memory_space_constraint(w, pltpu.HBM))


def two_rows(row, width):
    high = row.astype(bf16)
    low = (row - high.astype(f32)).astype(bf16)
    line = lax.broadcasted_iota(jnp.int32, (16, width), 0)
    both = jnp.where(line == 0, high.astype(f32), jnp.where(line == 1, low.astype(f32), 0.0))
    return both.astype(bf16)


def one_row(rows):
    return jnp.sum(rows.astype(f32), axis=0, keepdims=True)


def partial_kernel(ks, own, sis, gains, w_own, w_sis, *outs):
    width = X_HI * QKV
    core = lax.axis_index("core")
    own_rows, sis_rows = own[...].astype(f32), sis[...].astype(f32)
    left, right = gains[:, :TOK].astype(f32), gains[:, TOK:].astype(f32)
    x_own = (own_rows * jnp.where(core == 0, left, right)).astype(bf16)
    x_sis = (sis_rows * jnp.where(core == 0, right, left)).astype(bf16)
    squares = jnp.sum(own_rows * own_rows + sis_rows * sis_rows, axis=1, keepdims=True)
    line = lax.broadcasted_iota(jnp.int32, (ROWS, QKV), 0)
    lane = lax.broadcasted_iota(jnp.int32, (ROWS, QKV), 1)
    row = jnp.sum(jnp.where(line == lane, squares, 0.0), axis=0, keepdims=True)
    tail = two_rows(row, QKV)

    def product(slot, count):
        cols = slice(slot * QKV, (slot + count) * QKV)
        acc = jnp.dot(x_own, w_own[:, cols], preferred_element_type=f32)
        acc = acc + jnp.dot(x_sis, w_sis[:, cols], preferred_element_type=f32)
        return acc.astype(bf16)

    def full(slot, out):
        out[:ROWS, :] = product(slot, X_HI)
        out[ROWS:, :QKV] = tail
        out[ROWS:, QKV:] = tail

    if ks == FIRST:
        for xr, out in enumerate(outs):
            out[:ROWS, :] = product(xr, 1)
            out[ROWS:, :] = tail
    else:
        outs, buffer, sems = outs[:-2], outs[-2], outs[-1]
        copies = []
        for i, out in enumerate(outs):
            full(i * X_HI, buffer.at[i])
            copies.append(pltpu.make_async_copy(buffer.at[i], out, sems.at[i]))
            copies[i].start()
        for copy in copies:
            copy.wait()


def partials(ks, own, sis, gains, w_own, w_sis):
    half = jax.ShapeDtypeStruct((SUM_ROWS, QKV), bf16)
    full = jax.ShapeDtypeStruct((SUM_ROWS, X_HI * QKV), bf16)
    if ks == FIRST:
        shapes, specs, scratch = (half, half), (vmem(), vmem()), []
    else:
        shapes, specs = (pltpu.HBM(full.shape, bf16),) * len(ks), (hbm(),) * len(ks)
        scratch = [pltpu.VMEM((len(ks), *full.shape), bf16), pltpu.SemaphoreType.DMA((len(ks),))]
    return pl.pallas_call(
        functools.partial(partial_kernel, ks),
        out_shape=shapes,
        in_specs=[vmem()] * 5,
        out_specs=specs,
        scratch_shapes=scratch,
        compiler_params=limit(20),
        cost_estimate=pl.CostEstimate(
            flops=4 * ROWS * w_own.size, bytes_accessed=8 * w_own.size, transcendentals=0
        ),
    )(own, sis, gains, w_own, w_sis)


def store_sum(out, cols, terms):
    body = sum(term[:ROWS].astype(f32) for term in terms)
    row = sum(one_row(term[ROWS:]) for term in terms)
    out[:ROWS, cols] = body.astype(bf16)
    out[ROWS:, cols] = two_rows(row, row.shape[1])


def first_kernel(up, down, near_up, near_down, out_up, out_down):
    left, right = slice(0, QKV), slice(QKV, 2 * QKV)
    store_sum(out_up, left, [up[...], near_up[:, left]])
    out_up[:, right] = near_up[:, right]
    out_down[:, left] = near_down[:, left]
    store_sum(out_down, right, [down[...], near_down[:, right]])


def next_kernel(up, down, near_up, near_down, out_up, out_down):
    every = slice(0, 2 * QKV)
    store_sum(out_up, every, [up[...], near_up[...]])
    store_sum(out_down, every, [down[...], near_down[...]])


def ring_add(kernel, up, down, near_up, near_down):
    out = jax.ShapeDtypeStruct((SUM_ROWS, X_HI * QKV), bf16)
    return pl.pallas_call(
        kernel,
        out_shape=(out, out),
        in_specs=[vmem()] * 4,
        out_specs=(vmem(), vmem()),
        compiler_params=limit(8),
    )(up, down, near_up, near_down)


def last_kernel(up, down, near, mine, other):
    own, far = slice(0, QKV), slice(QKV, 2 * QKV)
    terms = [up, down, near]
    mine[:ROWS] = sum(term[:ROWS, own].astype(f32) for term in terms)
    row = sum(one_row(term[ROWS:, own]) for term in terms)
    mine[ROWS:] = jnp.broadcast_to(row, (8, QKV))
    store_sum(other, slice(0, QKV), [term[:, far] for term in terms])


def ring_last(up, down, near):
    return pl.pallas_call(
        last_kernel,
        out_shape=(
            jax.ShapeDtypeStruct((ROWS + 8, QKV), f32),
            jax.ShapeDtypeStruct((SUM_ROWS, QKV), bf16),
        ),
        in_specs=[vmem()] * 3,
        out_specs=(vmem(), vmem()),
        compiler_params=limit(8),
    )(up, down, near)


def rotated(x, cosine, sine):
    return x * cosine + pltpu.roll(x, HD // 2, 1) * sine


def finish_kernel(full_width, mine, other, cosine, sine, onehot, payload, queries):
    row = mine[ROWS : ROWS + 1, :] + one_row(other[ROWS:, :])
    line = lax.broadcasted_iota(jnp.int32, (ROWS, QKV), 0)
    lane = lax.broadcasted_iota(jnp.int32, (ROWS, QKV), 1)
    squares = jnp.sum(jnp.where(line == lane, row, 0.0), axis=1, keepdims=True)
    inv_rms = lax.rsqrt(squares / full_width + epsilon)
    proj = (mine[:ROWS, :] + other[:ROWS, :].astype(f32)) * inv_rms
    query = rotated(proj[:, :HD], cosine[...], sine[...]).astype(bf16)
    key = rotated(proj[:, HD : 2 * HD], cosine[...], sine[...]).astype(bf16)
    value = proj[:, 2 * HD :].astype(bf16)
    spots = onehot[...]

    def step(b, carry):
        payload[b, :ROWS, :HD] = key
        payload[b, :ROWS, HD:] = value
        payload[b, ROWS:, :] = spots
        return carry

    lax.fori_loop(0, BLOCKS, step, 0)
    contract = (((0,), (0,)), ((), ()))
    ones = jnp.ones((VAR, HD), bf16)
    changed = lax.dot_general(spots, ones, contract, preferred_element_type=f32)
    placed = lax.dot_general(spots, query[TOK:], contract, preferred_element_type=f32)
    base = query[:TOK]
    queries[:TOK] = base
    queries[TOK:] = jnp.where(changed > 0.5, placed, base.astype(f32)).astype(bf16)


def finish(full_width, mine, other, cosine, sine, onehot):
    return pl.pallas_call(
        functools.partial(finish_kernel, full_width),
        out_shape=(
            jax.ShapeDtypeStruct((BLOCKS, PAY, 2 * HD), bf16),
            jax.ShapeDtypeStruct((2 * TOK, HD), bf16),
        ),
        in_specs=[vmem()] * 5,
        out_specs=(vmem(), vmem()),
        compiler_params=limit(12),
    )(mine, other, cosine, sine, pltpu.with_memory_space_constraint(onehot, pltpu.HBM))


def attend_kernel(queries, blocks, out, scores, peak, denom, total, var_kv, spots):
    my_block = lax.axis_index("x_lo") * Y + lax.axis_index("y")
    scale = 1.0 / HD**0.5
    by_cols = (((1,), (1,)), ((), ()))
    lowest = -jnp.inf
    query = queries[...]

    def score_block(j, own):
        score = lax.dot_general(
            query, blocks[j, :TOK, :HD], by_cols, preferred_element_type=f32
        ) * scale
        gone = jnp.sum(blocks[j, ROWS:, :].astype(f32), axis=0, keepdims=True) > 0.5
        line = lax.broadcasted_iota(jnp.int32, (2 * TOK, TOK), 0)
        hidden = (line >= TOK) & gone
        if own:
            lane = lax.broadcasted_iota(jnp.int32, (2 * TOK, TOK), 1)
            hidden = hidden | (lax.rem(line, TOK) < lane)
        return jnp.where(hidden, lowest, score)

    score = score_block(my_block, True)
    scores[my_block] = score
    peak[...] = jnp.maximum(score[:, :HD], score[:, HD:])

    def first(j, carry):
        score = score_block(j, False)
        scores[j] = score
        peak[...] = jnp.maximum(peak[...], jnp.maximum(score[:, :HD], score[:, HD:]))
        return carry

    lax.fori_loop(0, my_block, first, 0)

    for j in range(BLOCKS):
        var_kv[j * VAR : (j + 1) * VAR, :] = blocks[j, TOK:ROWS, :]
        spots[j * VAR : (j + 1) * VAR, :] = blocks[j, ROWS:, :]
    row = lax.broadcasted_iota(jnp.int32, (TOK, TOK), 0)
    col = lax.broadcasted_iota(jnp.int32, (TOK, TOK), 1)
    reached = lax.dot_general(
        jnp.where(row >= col, 1.0, 0.0).astype(bf16), spots[...], by_cols, preferred_element_type=f32
    )
    source = lax.broadcasted_iota(jnp.int32, (TOK, BLOCKS * VAR), 1) // VAR
    seen = (source < my_block) | ((source == my_block) & (reached > 0.5))
    more = lax.dot_general(
        query[TOK:], var_kv[:, :HD], by_cols, preferred_element_type=f32
    ) * scale
    more = jnp.where(seen, more, lowest)
    peak[TOK:, :] = jnp.maximum(peak[TOK:, :], more)
    top = jnp.max(peak[...], axis=1, keepdims=True)
    peak[...] = jnp.broadcast_to(top, (2 * TOK, HD))

    more = jnp.exp(more - top[TOK:])
    denom[:TOK, :] = jnp.zeros((TOK, HD), f32)
    denom[TOK:, :] = more
    total[:TOK, :] = jnp.zeros((TOK, HD), f32)
    total[TOK:, :] = jnp.dot(more.astype(bf16), var_kv[:, HD:], preferred_element_type=f32)

    def second(j, carry):
        best = peak[...]
        left = jnp.exp(scores[j, :, :HD] - best)
        right = jnp.exp(scores[j, :, HD:] - best)
        denom[...] = denom[...] + left + right
        probs = jnp.concatenate([left.astype(bf16), right.astype(bf16)], axis=1)
        total[...] = total[...] + jnp.dot(
            probs, blocks[j, :TOK, HD:], preferred_element_type=f32
        )
        return carry

    lax.fori_loop(0, my_block + 1, second, 0)
    out[...] = (total[...] / jnp.sum(denom[...], axis=1, keepdims=True)).astype(bf16)


def attend(queries, blocks):
    return pl.pallas_call(
        attend_kernel,
        out_shape=jax.ShapeDtypeStruct((2 * TOK, HD), bf16),
        in_specs=[vmem(), vmem()],
        out_specs=vmem(),
        scratch_shapes=[
            pltpu.VMEM((BLOCKS, 2 * TOK, TOK), f32),
            pltpu.VMEM((2 * TOK, HD), f32),
            pltpu.VMEM((2 * TOK, HD), f32),
            pltpu.VMEM((2 * TOK, HD), f32),
            pltpu.VMEM((BLOCKS * VAR, 2 * HD), bf16),
            pltpu.VMEM((BLOCKS * VAR, TOK), bf16),
        ],
        compiler_params=limit(16),
    )(queries, blocks)


def arrange_kernel(w, out, sems):
    z = lax.axis_index("z")
    copies = []
    for d in range(Z):
        source = lax.rem(z + Z - d, Z)
        copies.append(
            pltpu.make_async_copy(w.at[source], out.at[d * HD : (d + 1) * HD, :], sems.at[d])
        )
    for copy in copies:
        copy.start()
    for copy in copies:
        copy.wait()


def arrange(w):
    return pl.pallas_call(
        arrange_kernel,
        out_shape=jax.ShapeDtypeStruct((Z * HD, w.shape[2]), bf16),
        in_specs=[hbm()],
        out_specs=vmem(),
        scratch_shapes=[pltpu.SemaphoreType.DMA((Z,))],
        compiler_params=limit(4),
    )(pltpu.with_memory_space_constraint(w, pltpu.HBM))


def project_kernel(first, turned, *refs):
    shards, (keep, near, far), joined = refs[:Z], refs[Z : Z + 3], refs[-1]
    core, x_hi = lax.axis_index("core"), lax.axis_index("x_hi")
    for d in range(Z):
        joined[:, d * HD : (d + 1) * HD] = shards[d][first : first + TOK, :]

    def product(xr, cr, rows):
        column = (lax.rem(x_hi + xr, X_HI) * CORE + lax.rem(core + cr, CORE)) * TOK
        column = pl.ds(pl.multiple_of(column, TOK), TOK)
        return jnp.dot(joined[rows, :], turned[:, column], preferred_element_type=f32)

    size = TOK

    def step(i, carry):
        rows = pl.ds(pl.multiple_of(i * size, size), size)
        for xr in range(X_HI):
            near[rows, xr * TOK : (xr + 1) * TOK] = product(xr, 1, rows).astype(bf16)
        keep[rows, :] = product(0, 0, rows)
        far[rows, :] = product(1, 0, rows)
        return carry

    lax.fori_loop(0, TOK // size, step, 0)


def project(first, w, shards):
    rows = TOK
    return pl.pallas_call(
        functools.partial(project_kernel, first),
        out_shape=(
            jax.ShapeDtypeStruct((rows, TOK), f32),
            jax.ShapeDtypeStruct((rows, 2 * TOK), bf16),
            jax.ShapeDtypeStruct((rows, TOK), f32),
        ),
        in_specs=[vmem()] * (1 + Z),
        out_specs=(vmem(),) * 3,
        scratch_shapes=[pltpu.VMEM((rows, Z * HD), bf16)],
        compiler_params=limit(16),
    )(w, *shards)


def shards(hidden, gain, embed, qkv_weight, out_weight, ref_ids, var_pos, var_base):
    tok_rows, width_part = hidden.shape
    full_width = out_weight.shape[1]
    x_hi, z, core = lax.axis_index("x_hi"), lax.axis_index("z"), lax.axis_index("core")
    my_block = lax.axis_index("x_lo") * Y + lax.axis_index("y")
    chip_slice = x_hi * Z + z

    with jax.named_scope("inputs"):
        rows, onehot, variant, share = make_variant(
            var_pos, var_base, ref_ids, hidden, embed, out_weight
        )
        rows, qkv_weight = lax.optimization_barrier((rows, qkv_weight))
        rows_sis = shift(rows, "core", CORE, 1)
        send_first, own_first = pick_columns(FIRST, qkv_weight)
        sis_first = shift(send_first, "core", CORE, 1)
        rows_sis, sis_first, qkv_weight, share = lax.optimization_barrier(
            (rows_sis, sis_first, qkv_weight, share)
        )
        send_second, own_second = pick_columns(SECOND, qkv_weight)
        sis_second = shift(send_second, "core", CORE, 1)
        shared = lax.all_to_all(share, "z", 0, 0, tiled=True)
        start = chip_slice * 2 * width_part
        gains = lax.dynamic_slice(gain.reshape(1, full_width), (0, start), (1, 2 * width_part))

    with jax.named_scope("projection"):
        sis_first = pltpu.with_memory_space_constraint(sis_first, pltpu.HBM)
        up, down = partials(FIRST, rows, rows_sis, gains, own_first, sis_first)
        up, down = shift(up, "z", Z, 1), shift(down, "z", Z, -1)
        parts = partials(SECOND, rows, rows_sis, gains, own_second, sis_second)
        near_up = pltpu.with_memory_space_constraint(parts[0], pltpu.HBM)
        near_down = pltpu.with_memory_space_constraint(parts[1], pltpu.HBM)
        up, down, shared, near_up = lax.optimization_barrier((up, down, shared, near_up))
        out_w = lax.all_gather(shared, CTX, axis=1, tiled=True)
        parts = dict(zip(SECOND, parts))
        up, down = ring_add(first_kernel, up, down, near_up, near_down)
        up, down = shift(up, "z", Z, 1), shift(down, "z", Z, -1)
        near_up = pltpu.with_memory_space_constraint(parts[2], pltpu.HBM)
        near_down = pltpu.with_memory_space_constraint(parts[6], pltpu.HBM)
        up, down = ring_add(next_kernel, up, down, near_up, near_down)
        up, down = shift(up, "z", Z, 1), shift(down, "z", Z, -1)
        up, down = ring_add(next_kernel, up, down, parts[1], parts[7])
        up, down = shift(up, "z", Z, 1), shift(down, "z", Z, -1)
        mine, other = ring_last(up, down, parts[0])
        other = shift(other, "x_hi", X_HI, 1)

    with jax.named_scope("tables"):
        positions = jnp.concatenate([my_block * tok_rows + jnp.arange(tok_rows), var_pos])
        exponent = jnp.arange(HD // 2).astype(f32) * (-2.0 / HD)
        inv_freq = jnp.power(f32(rope_base), exponent)
        angle = positions.astype(f32)[:, None] * inv_freq[None, :]
        cosine, sine = jnp.cos(angle), jnp.sin(angle)
        cosine = jnp.concatenate([cosine, cosine], axis=1)
        sine = jnp.concatenate([-sine, sine], axis=1)

    with jax.named_scope("attention"):
        payload, queries = finish(full_width, mine, other, cosine, sine, onehot)
        blocks = lax.all_to_all(payload, CTX, 0, 0, tiled=True)
        attn = attend(queries, blocks)
        attn, out_w = lax.optimization_barrier((attn, out_w))

    with jax.named_scope("output"):
        pieces = [attn] + [None] * (Z - 1)
        for d in (1, 2, 3):
            pieces[d] = shift(pieces[d - 1], "z", Z, 1)
            pieces[Z - d] = shift(pieces[(Z - d + 1) % Z], "z", Z, -1)
            if d == 1:
                pieces[Z // 2] = shift(attn, "z", Z, Z // 2)
                out_w, pieces[1], pieces[7] = lax.optimization_barrier(
                    (arrange(out_w), pieces[1], pieces[7])
                )
        mixed = []
        for first, seq in ((0, hidden), (tok_rows, variant)):
            keep, near, far = project(first, out_w, pieces)
            near = shift(near, "core", CORE, 1).astype(f32)
            far = (far + near[:, width_part:]).astype(bf16)
            far = shift(far, "x_hi", X_HI, 1).astype(f32)
            branch = keep + near[:, :width_part] + far
            mixed.append((seq.astype(f32) + branch).astype(bf16))
        return jnp.stack(mixed)


def solution(mesh):
    fine = Mesh(mesh.devices.reshape(X_HI, Z, CORE, X_LO, Y), (*FSDP, *CTX))
    in_specs = (
        P(CTX, FSDP),
        P(),
        P(None, FSDP),
        P(FSDP, None),
        P(FSDP, None),
        P(CTX),
        P(CTX),
        P(CTX),
    )
    out_specs = P(None, CTX, FSDP)
    return jax.shard_map(shards, mesh=fine, in_specs=in_specs, out_specs=out_specs, check_vma=False)
```
